32 devices in a mesh: dp: 16 (over z, x, core), tensor: 2 (over y).
Axes of the slice: x: 2, y: 2, z: 4, core: 2. Of those that a mesh axis runs over, the one named last changes fastest.
Arguments:
- tokens: bfloat16 [8192, 1024], P(('dp', 'tensor')), may hold values from -6 to 6
- cotangent: bfloat16 [8192, 1024], P(('dp', 'tensor')), may hold values from -6 to 6
- norm1_gain: bfloat16 [1024], P('dp'), may hold values from 0.5 to 1.5
- norm1_shift: bfloat16 [1024], P('dp'), may hold values from -1.75 to 1.75
- w_query: bfloat16 [1024, 1024], P('dp', 'tensor'), may hold values from -0.25 to 0.25
- b_query: bfloat16 [1024], P('dp'), may hold values from -3 to 3
- w_key: bfloat16 [1024, 1024], P('dp', 'tensor'), may hold values from -0.25 to 0.25
- w_value: bfloat16 [1024, 1024], P('dp', 'tensor'), may hold values from -0.1875 to 0.1875
- b_value: bfloat16 [1024], P('dp'), may hold values from -3 to 3
- w_out: bfloat16 [1024, 1024], P('tensor', 'dp'), may hold values from -0.75 to 0.75
- b_out: bfloat16 [1024], P('dp'), may hold values from -1.75 to 1.75
- norm2_gain: bfloat16 [1024], P('dp'), may hold values from 0.5 to 1.5
- norm2_shift: bfloat16 [1024], P('dp'), may hold values from -1.75 to 1.75
- w_up: bfloat16 [1024, 4096], P('dp', 'tensor'), may hold values from -0.1875 to 0.1875
- b_up: bfloat16 [4096], P('dp'), may hold values from -3 to 3
- w_down: bfloat16 [4096, 1024], P('tensor', 'dp'), may hold values from -0.09375 to 0.09375
- b_down: bfloat16 [1024], P('dp'), may hold values from -1.75 to 1.75
- lengths: int32 [16, 3], P('dp'), may hold values from 128 to 192, as said below
- deal_rank: int32 [16, 2, 256], P('dp', 'tensor'), may hold values from 0 to 255, each once within a row
- arrival: int32 [16, 2, 256], P('dp', 'tensor'), may hold values from 0 to 255, each once within a row
Outputs:
- output: bfloat16 [8192, 1024], P(('dp', 'tensor'))
- tokens_grad: bfloat16 [8192, 1024], P(('dp', 'tensor'))
- grad_norm1_gain: float32 [1024], P('dp')
- grad_norm1_shift: float32 [1024], P('dp')
- grad_w_query: float32 [1024, 1024], P('dp', 'tensor')
- grad_b_query: float32 [1024], P('dp')
- grad_w_key: float32 [1024, 1024], P('dp', 'tensor')
- grad_w_value: float32 [1024, 1024], P('dp', 'tensor')
- grad_b_value: float32 [1024], P('dp')
- grad_w_out: float32 [1024, 1024], P('tensor', 'dp')
- grad_b_out: float32 [1024], P('dp')
- grad_norm2_gain: float32 [1024], P('dp')
- grad_norm2_shift: float32 [1024], P('dp')
- grad_w_up: float32 [1024, 4096], P('dp', 'tensor')
- grad_b_up: float32 [4096], P('dp')
- grad_w_down: float32 [4096, 1024], P('tensor', 'dp')
- grad_b_down: float32 [1024], P('dp')
The draws below stay inside these ranges and needn't reach their ends.
Inputs may be any that keep to these rules, and one draw needn't show every extreme that they name: `lengths`: each row sums to 512 and holds 192 at least once; 128 occurs in some row. `deal_rank`: a permutation of 0 to 255 along the last dimension. `arrival`: a permutation of 0 to 255 along the last dimension.
All inputs are finite; a program needn't handle non-finite values.
Results may differ from the reference program's by a relative error of at most 0.024.
Values may be sent and summed in bfloat16 or wider, within the bound.
A program may use at most 128 MiB of HBM per device.

```python
import jax
import jax.numpy as jnp
from jax import lax

D = 1024
HEADS = 16
HEAD_DIM = 64
FF = 4096
TOK_DEV = 256
NSEQ = 3
GROUP = 512
SHORTEST = 128
LONGEST = 192
TOKENS = 8192
PIECE = 16
QBLOCK = 512
N_DP = 16
N_TENSOR = 2


def draw_lengths(key, part):
    key_first = jax.random.fold_in(key, 11)
    key_middle = jax.random.fold_in(key, 23)
    key_forced = jax.random.fold_in(key, 37)
    longest_at = jax.random.randint(key_first, (N_DP,), 0, NSEQ).astype(jnp.int32)
    middle = jax.random.randint(key_middle, (N_DP,), SHORTEST, LONGEST + 1).astype(jnp.int32)
    forced = jax.random.randint(key_forced, (), 0, N_DP).astype(jnp.int32)
    group_ids = lax.iota(jnp.int32, N_DP)
    middle = jnp.where(group_ids == forced, SHORTEST, middle).astype(jnp.int32)
    other = (LONGEST + SHORTEST - middle).astype(jnp.int32)
    slots = lax.broadcasted_iota(jnp.int32, (N_DP, NSEQ), 1)
    offset = (slots - longest_at[:, None]) % NSEQ
    picked = jnp.where(offset == 0, LONGEST, jnp.where(offset == 1, middle[:, None], other[:, None]))
    return picked.astype(jnp.int32)


def levels(stream_key, shape, pieces, low, top_value):
    gain = 1.0
    for position, parts in pieces:
        heights = jax.random.uniform(jax.random.fold_in(jax.random.fold_in(stream_key, 6), position), (parts,), jnp.float32, low / len(pieces), top_value / len(pieces))
        gain = gain * jnp.repeat(jnp.exp(heights), shape[position] // parts).reshape((-1,) + (1,) * (len(shape) - 1 - position))
    return gain


def noise(key, shape, scale, reach, split=(), kind=jnp.bfloat16):
    entries = jax.random.normal(key, shape, jnp.float32) * scale
    if len(split) > 0:
        entries = levels(key, shape, split, -0.22, 0.18) * entries
    return jnp.clip(entries, min=-reach, max=reach).astype(kind)


def setup_inputs(seed: int = 0) -> dict:
    keys = jax.random.split(jax.random.key(seed), 21)
    tokens = noise(keys[0], (TOKENS, D), 1.0, 6.0, ((0, 32),))
    cotangent = noise(keys[1], (TOKENS, D), 1.0, 6.0, ((0, 32),))
    norm1_gain = jnp.clip(1.0 + 0.1 * jax.random.normal(keys[2], (D,), jnp.float32), 0.5, 1.5).astype(jnp.bfloat16)
    norm1_shift = noise(keys[3], (D,), 0.3, 1.75, ((0, 16),))
    w_query = noise(keys[4], (D, D), (D // 2) ** -0.5, 0.25, ((0, 16), (1, 2)))
    b_query = noise(keys[5], (D,), 0.5, 3.0, ((0, 16),))
    w_key = noise(keys[6], (D, D), (D // 2) ** -0.5, 0.25, ((0, 16), (1, 2)))
    w_value = noise(keys[7], (D, D), D ** -0.5, 0.1875, ((0, 16), (1, 2)))
    b_value = noise(keys[8], (D,), 0.5, 3.0, ((0, 16),))
    w_out = noise(keys[9], (D, D), HEAD_DIM ** -0.5, 0.75, ((0, 2), (1, 16)))
    b_out = noise(keys[10], (D,), 0.3, 1.75, ((0, 16),))
    norm2_gain = jnp.clip(1.0 + 0.1 * jax.random.normal(keys[11], (D,), jnp.float32), 0.5, 1.5).astype(jnp.bfloat16)
    norm2_shift = noise(keys[12], (D,), 0.3, 1.75, ((0, 16),))
    w_up = noise(keys[13], (D, FF), D ** -0.5, 0.1875, ((0, 16), (1, 2)))
    b_up = noise(keys[14], (FF,), 0.5, 3.0, ((0, 16),))
    w_down = noise(keys[15], (FF, D), FF ** -0.5, 0.09375, ((0, 2), (1, 16)))
    b_down = noise(keys[16], (D,), 0.3, 1.75, ((0, 16),))
    lengths = draw_lengths(jax.random.fold_in(keys[20], 71), 0)
    deal_rank = jax.vmap(lambda own: jax.random.permutation(own, TOK_DEV))(jax.random.split(keys[18], N_DP * N_TENSOR)).reshape((N_DP, N_TENSOR, TOK_DEV)).astype(jnp.int32)
    arrival = jax.vmap(lambda own: jax.random.permutation(own, TOK_DEV))(jax.random.split(keys[19], N_DP * N_TENSOR)).reshape((N_DP, N_TENSOR, TOK_DEV)).astype(jnp.int32)
    return {"tokens": tokens, "cotangent": cotangent, "norm1_gain": norm1_gain, "norm1_shift": norm1_shift, "w_query": w_query, "b_query": b_query, "w_key": w_key, "w_value": w_value, "b_value": b_value, "w_out": w_out, "b_out": b_out, "norm2_gain": norm2_gain, "norm2_shift": norm2_shift, "w_up": w_up, "b_up": b_up, "w_down": w_down, "b_down": b_down, "lengths": lengths, "deal_rank": deal_rank, "arrival": arrival}


@jax.custom_vjp
def low(v):
    return lax.optimization_barrier(v.astype(jnp.bfloat16)).astype(jnp.float32)

@jax.custom_vjp
def low_back(v):
    return v

def low_keep(v):
    return (low(v), None)

def low_pass(kept, grad):
    return (grad,)

def back_keep(v):
    return (v, None)

def back_low(kept, grad):
    return (low(grad),)
low.defvjp(low_keep, low_pass)
low_back.defvjp(back_keep, back_low)
EPSILON = 1e-05

def matmul(first_op, second_op):
    return jnp.dot(first_op, second_op, precision=lax.Precision.HIGHEST, preferred_element_type=jnp.float32)

def layer_norm(values, norm_gain, norm_shift):
    center = values - lax.optimization_barrier(jnp.mean(values, axis=-1, keepdims=True))
    spread = lax.optimization_barrier(jnp.mean(center * center, axis=-1, keepdims=True))
    return center * lax.rsqrt(spread + EPSILON) * norm_gain + norm_shift

def source_rows(deal_rank, arrival):
    inverse = jnp.argsort(deal_rank, axis=-1).astype(jnp.int32)
    flat_inverse = inverse.reshape(N_DP * N_TENSOR * TOK_DEV)
    sender = (arrival // PIECE).astype(jnp.int32)
    rank_in = (arrival % PIECE).astype(jnp.int32)
    group_ids = lax.broadcasted_iota(jnp.int32, arrival.shape, 0)
    tensor_ids = lax.broadcasted_iota(jnp.int32, arrival.shape, 1)
    block_ids = sender * N_TENSOR + tensor_ids
    slot_ids = group_ids * PIECE + rank_in
    local_row = flat_inverse[block_ids * TOK_DEV + slot_ids]
    return (block_ids * TOK_DEV + local_row).reshape(TOKENS).astype(jnp.int32)

def sequence_marks(lengths):
    seq_ends = jnp.cumsum(lengths, axis=1).astype(jnp.int32)
    seq_starts = (seq_ends - lengths).astype(jnp.int32)
    row_ids = lax.broadcasted_iota(jnp.int32, (N_DP, GROUP), 1)
    inside = (row_ids[:, :, None] >= seq_starts[:, None, :]) & (row_ids[:, :, None] < seq_ends[:, None, :])
    seq_index = lax.broadcasted_iota(jnp.int32, (1, 1, NSEQ), 2)
    seq_ids = lax.optimization_barrier(jnp.sum(jnp.where(inside, seq_index, 0), axis=2)).astype(jnp.int32)
    seq_start = lax.optimization_barrier(jnp.sum(jnp.where(inside, seq_starts[:, None, :], 0), axis=2)).astype(jnp.int32)
    return (seq_ids, (row_ids - seq_start).astype(jnp.int32))

def group_layer(params, grouped, seq_ids, positions):
    norm1_gain, norm1_shift, w_query, b_query, w_key, w_value, b_value, w_out, b_out, norm2_gain, norm2_shift, w_up, b_up, w_down, b_down = params
    first_in = low(layer_norm(grouped, norm1_gain, norm1_shift))
    queries = low(low_back(matmul(first_in, w_query) + b_query)).reshape(GROUP, HEADS, HEAD_DIM)
    keyset = low(low_back(matmul(first_in, w_key))).reshape(GROUP, HEADS, HEAD_DIM)
    valset = low(low_back(matmul(first_in, w_value) + b_value)).reshape(GROUP, HEADS, HEAD_DIM)
    slopes = jnp.exp2(-8.0 * (lax.iota(jnp.float32, HEADS) + 1.0) / HEADS)
    row_all = lax.iota(jnp.int32, GROUP)
    blocks = GROUP // QBLOCK

    def attend(block_item):
        query_rows, seq_rows, pos_rows, row_rows = block_item
        raw_scores = jnp.einsum('qhd,khd->hqk', query_rows, keyset, precision=lax.Precision.HIGHEST) * HEAD_DIM ** (-0.5)
        distance = (pos_rows[:, None] - positions[None, :]).astype(jnp.float32)
        scores = low_back(raw_scores - slopes[:, None, None] * distance[None])
        allowed = (seq_rows[:, None] == seq_ids[None, :]) & (row_rows[:, None] >= row_all[None, :])
        scores = jnp.where(allowed[None], scores, -1e+30)
        attn_probs = low(jax.nn.softmax(scores, axis=-1))
        return jnp.einsum('hqk,khd->qhd', attn_probs, valset, precision=lax.Precision.HIGHEST)
    mixed = lax.map(jax.checkpoint(attend), (queries.reshape(blocks, QBLOCK, HEADS, HEAD_DIM), seq_ids.reshape(blocks, QBLOCK), positions.reshape(blocks, QBLOCK), row_all.reshape(blocks, QBLOCK)))
    heads_out = low(low_back(mixed.reshape(GROUP, D)))
    attn_out = low_back(matmul(heads_out, w_out) + b_out)
    residual = grouped + attn_out
    second_in = low(layer_norm(residual, norm2_gain, norm2_shift))
    pre_act = low_back(matmul(second_in, w_up) + b_up)
    activated = low(jax.nn.gelu(pre_act, approximate=True))
    mlp_out = low_back(matmul(activated, w_down) + b_down)
    return residual + mlp_out

def reference(tokens, cotangent, norm1_gain, norm1_shift, w_query, b_query, w_key, w_value, b_value, w_out, b_out, norm2_gain, norm2_shift, w_up, b_up, w_down, b_down, lengths, deal_rank, arrival):
    weights = tuple([member.astype(jnp.float32) for member in (norm1_gain, norm1_shift, w_query, b_query, w_key, w_value, b_value, w_out, b_out, norm2_gain, norm2_shift, w_up, b_up, w_down, b_down)])
    source = source_rows(deal_rank, arrival)
    seq_ids, positions = sequence_marks(lengths)

    def forward(values, params):
        grouped = values[source].reshape(N_DP, GROUP, D)

        def one_group(group_item):
            return group_layer(params, group_item[0], group_item[1], group_item[2])
        result = lax.map(jax.checkpoint(one_group), (grouped, seq_ids, positions))
        return jnp.zeros_like(values).at[source].set(result.reshape(TOKENS, D))
    output, pullback = jax.vjp(forward, tokens.astype(jnp.float32), weights)
    token_grad, grads = pullback(cotangent.astype(jnp.float32))
    return (output.astype(jnp.bfloat16), token_grad.astype(jnp.bfloat16), grads[0], grads[1], grads[2], grads[3], grads[4], grads[5], grads[6], grads[7], grads[8], grads[9], grads[10], grads[11], grads[12], grads[13], grads[14])
```

```python
import jax
import jax.numpy as jnp
from jax import lax
from jax.sharding import PartitionSpec as P

D = 1024
HEADS = 16
HEAD_DIM = 64
FF = 4096


EPSILON = 1e-05


def layer_norm(values, norm_gain, norm_shift):
    center = values - jnp.mean(values, axis=-1, keepdims=True)
    spread = jnp.mean(center * center, axis=-1, keepdims=True)
    return center * lax.rsqrt(spread + EPSILON) * norm_gain + norm_shift


def gelu_tanh(values):
    return jax.nn.gelu(values, approximate=True)


def contract_rows(first_op, second_op):
    return lax.dot_general(
        first_op, second_op, (((0,), (0,)), ((), ())), preferred_element_type=jnp.float32
    )


def contract_cols(first_op, second_op):
    return lax.dot_general(
        first_op, second_op, (((1,), (1,)), ((), ())), preferred_element_type=jnp.float32
    )


def take_block(vector, block_index, block_size):
    return lax.dynamic_slice_in_dim(vector, block_index * block_size, block_size, 0).astype(
        jnp.float32
    )


def place_block(total_size, block_vec, block_index):
    holder = jnp.zeros((total_size,), jnp.float32)
    return lax.dynamic_update_slice_in_dim(holder, block_vec, block_index * block_vec.shape[0], 0)


def sequence_marks(seq_lengths, group_rows):
    seq_ends = jnp.cumsum(seq_lengths)
    seq_starts = seq_ends - seq_lengths
    row_ids = lax.iota(jnp.int32, group_rows)
    inside = (row_ids[:, None] >= seq_starts[None, :]) & (row_ids[:, None] < seq_ends[None, :])
    seq_index = lax.iota(jnp.int32, seq_lengths.shape[0])
    seq_ids = jnp.sum(jnp.where(inside, seq_index[None, :], 0), axis=1)
    seq_start = jnp.sum(jnp.where(inside, seq_starts[None, :], 0), axis=1)
    return (seq_ids, row_ids - seq_start, row_ids)


def body(
    tokens,
    cotangent,
    norm1_gain,
    norm1_shift,
    w_query,
    b_query,
    w_key,
    w_value,
    b_value,
    w_out,
    b_out,
    norm2_gain,
    norm2_shift,
    w_up,
    b_up,
    w_down,
    b_down,
    lengths,
    deal_rank,
    arrival,
):
    dp_count = lax.axis_size("dp")
    tensor_count = lax.axis_size("tensor")
    tensor_rank = lax.axis_index("tensor")
    tok_rows = tokens.shape[0]
    features = tokens.shape[1]
    piece_rows = tok_rows // dp_count
    group_rows = tok_rows * tensor_count
    sending_rank = deal_rank.reshape(tok_rows)
    deal_order = jnp.argsort(sending_rank)
    arrive_order = arrival.reshape(tok_rows)
    return_order = jnp.argsort(arrive_order)

    def relocate(first_part, second_part):
        return (
            lax.all_to_all(first_part, "dp", split_axis=0, concat_axis=0, tiled=True),
            lax.all_to_all(second_part, "dp", split_axis=0, concat_axis=0, tiled=True),
        )

    def to_pieces(row_data, row_order):
        return row_data[row_order].reshape(dp_count, piece_rows, features)

    moved_x, moved_dy = relocate(to_pieces(tokens, deal_order), to_pieces(cotangent, deal_order))
    local_x = moved_x.reshape(tok_rows, features)[arrive_order]
    local_dy = moved_dy.reshape(tok_rows, features)[arrive_order]
    part_rows = w_query.shape[0]
    head_cols = w_query.shape[1]
    hidden_cols = w_up.shape[1]
    vectors = (
        norm1_gain,
        norm1_shift,
        b_query,
        b_value,
        b_out,
        norm2_gain,
        norm2_shift,
        b_down,
    )
    up_wide = b_up.shape[0] // part_rows
    vec_cols = jnp.concatenate(
        [jnp.stack(vectors, axis=1), b_up.reshape(part_rows, up_wide)], axis=1
    )
    vec_cols = jnp.pad(vec_cols, ((0, 0), (0, 128 - vec_cols.shape[1])))
    packed = jnp.concatenate(
        [w_query, w_key, w_value, w_out.T, w_up, w_down.T, vec_cols], axis=1
    )
    packed_all = lax.all_gather(packed, "dp", axis=0, tiled=True)
    edges = [0, head_cols, 2 * head_cols, 3 * head_cols, 4 * head_cols]
    edges += [4 * head_cols + hidden_cols, 4 * head_cols + 2 * hidden_cols]
    query_cols, key_cols, value_cols, out_cols, up_cols, down_cols = (
        packed_all[:, edges[i] : edges[i + 1]] for i in range(6)
    )
    out_rows = out_cols.T
    down_rows = down_cols.T
    vec_all = packed_all[:, edges[6] :]
    (
        gain_one,
        shift_one,
        bias_query,
        bias_value,
        bias_out,
        gain_two,
        shift_two,
        bias_down,
    ) = (vec_all[:, i] for i in range(8))
    bias_up = vec_all[:, 8 : 8 + up_wide].reshape(-1)
    gain_one = gain_one.astype(jnp.float32)
    shift_one = shift_one.astype(jnp.float32)
    gain_two = gain_two.astype(jnp.float32)
    shift_two = shift_two.astype(jnp.float32)
    local_heads = head_cols // HEAD_DIM
    score_scale = HEAD_DIM ** (-0.5)
    query_bias = take_block(bias_query, tensor_rank, head_cols)
    value_bias = take_block(bias_value, tensor_rank, head_cols)
    up_bias = take_block(bias_up, tensor_rank, hidden_cols)
    x_rows = local_x.astype(jnp.float32)
    first_in = layer_norm(x_rows, gain_one, shift_one).astype(jnp.bfloat16)
    group_one = lax.all_gather(first_in, "tensor", axis=0, tiled=True)
    queries = (
        jnp.dot(group_one, query_cols, preferred_element_type=jnp.float32) + query_bias
    ).astype(jnp.bfloat16)
    queries = queries.reshape(group_rows, local_heads, HEAD_DIM)
    keyset = jnp.dot(group_one, key_cols, preferred_element_type=jnp.float32).astype(jnp.bfloat16)
    keyset = keyset.reshape(group_rows, local_heads, HEAD_DIM)
    valset = (
        jnp.dot(group_one, value_cols, preferred_element_type=jnp.float32) + value_bias
    ).astype(jnp.bfloat16)
    valset = valset.reshape(group_rows, local_heads, HEAD_DIM)
    head_ids = tensor_rank * local_heads + lax.iota(jnp.int32, local_heads)
    slopes = jnp.exp2(-8.0 * (head_ids.astype(jnp.float32) + 1.0) / HEADS)
    seq_ids, positions, row_ids = sequence_marks(lengths[0], group_rows)
    qblock = min(512, group_rows)
    blocks = group_rows // qblock
    block_starts = lax.iota(jnp.int32, blocks) * qblock

    def block_scores(row_start):
        query_rows = lax.dynamic_slice_in_dim(queries, row_start, qblock, 0)
        raw_scores = (
            jnp.einsum("qhd,khd->hqk", query_rows, keyset, preferred_element_type=jnp.float32)
            * score_scale
        )
        seq_rows = lax.dynamic_slice_in_dim(seq_ids, row_start, qblock, 0)
        pos_rows = lax.dynamic_slice_in_dim(positions, row_start, qblock, 0)
        row_rows = lax.dynamic_slice_in_dim(row_ids, row_start, qblock, 0)
        distance = (pos_rows[:, None] - positions[None, :]).astype(jnp.float32)
        allowed = (seq_rows[:, None] == seq_ids[None, :]) & (row_rows[:, None] >= row_ids[None, :])
        scores = jnp.where(
            allowed[None], raw_scores - slopes[:, None, None] * distance[None], -1e30
        )
        return (query_rows, scores)

    def attend(row_start):
        query_rows, scores = block_scores(row_start)
        row_max = jnp.max(scores, axis=-1, keepdims=True)
        exponent = jnp.exp(scores - row_max)
        row_total = jnp.sum(exponent, axis=-1, keepdims=True)
        attn_probs = (exponent / row_total).astype(jnp.bfloat16)
        mixed = jnp.einsum("hqk,khd->qhd", attn_probs, valset, preferred_element_type=jnp.float32)
        return (mixed, row_max[..., 0] + jnp.log(row_total[..., 0]))

    mixed_all, log_totals = lax.map(attend, block_starts)
    heads_out = mixed_all.reshape(group_rows, head_cols).astype(jnp.bfloat16)
    attn_out = lax.psum_scatter(
        jnp.dot(heads_out, out_rows, preferred_element_type=jnp.float32).astype(jnp.bfloat16),
        "tensor",
        scatter_dimension=0,
        tiled=True,
    ).astype(jnp.float32) + bias_out.astype(jnp.float32)
    residual = x_rows + attn_out
    second_in = layer_norm(residual, gain_two, shift_two).astype(jnp.bfloat16)
    grad_in = local_dy.astype(jnp.float32)
    down_bias_term = jnp.sum(grad_in, axis=0)
    group_two = lax.all_gather(second_in, "tensor", axis=0, tiled=True)
    pre_act = jnp.dot(group_two, up_cols, preferred_element_type=jnp.float32) + up_bias
    activated = gelu_tanh(pre_act).astype(jnp.bfloat16)
    mlp_out = lax.psum_scatter(
        jnp.dot(activated, down_rows, preferred_element_type=jnp.float32).astype(jnp.bfloat16),
        "tensor",
        scatter_dimension=0,
        tiled=True,
    ).astype(jnp.float32)
    result = residual + mlp_out + bias_down.astype(jnp.float32)
    group_dy = lax.all_gather(local_dy, "tensor", axis=0, tiled=True)
    grad_down = contract_rows(activated, group_dy)
    grad_act = contract_cols(group_dy, down_rows)
    gelu_pull = jax.vjp(gelu_tanh, pre_act)[1]
    grad_pre = gelu_pull(grad_act)[0].astype(jnp.bfloat16)
    grad_up = contract_rows(group_two, grad_pre)
    up_bias_term = place_block(FF, jnp.sum(grad_pre, axis=0, dtype=jnp.float32), tensor_rank)
    grad_two = lax.psum_scatter(
        contract_cols(grad_pre, up_cols).astype(jnp.bfloat16),
        "tensor",
        scatter_dimension=0,
        tiled=True,
    ).astype(jnp.float32)
    result_low = result.astype(jnp.bfloat16)
    norm_two_pull = jax.vjp(layer_norm, residual, gain_two, shift_two)[1]
    grad_res_norm, gain_two_term, shift_two_term = norm_two_pull(grad_two)
    grad_resid = grad_in + grad_res_norm
    grad_attn = grad_resid.astype(jnp.bfloat16)
    out_bias_term = jnp.sum(grad_attn, axis=0, dtype=jnp.float32)
    group_grad = lax.all_gather(grad_attn, "tensor", axis=0, tiled=True)
    grad_out = contract_rows(heads_out, group_grad)
    grad_heads = (
        contract_cols(group_grad, out_rows)
        .astype(jnp.bfloat16)
        .reshape(group_rows, local_heads, HEAD_DIM)
    )

    def attend_back(running, block_item):
        key_accum, value_accum = running
        row_start, log_total = block_item
        query_rows, scores = block_scores(row_start)
        attn_probs = jnp.exp(scores - log_total[..., None])
        grad_rows = lax.dynamic_slice_in_dim(grad_heads, row_start, qblock, 0)
        grad_probs = jnp.einsum(
            "qhd,khd->hqk", grad_rows, valset, preferred_element_type=jnp.float32
        )
        row_dot = jnp.sum(attn_probs * grad_probs, axis=-1, keepdims=True)
        grad_scores = (attn_probs * (grad_probs - row_dot)).astype(jnp.bfloat16)
        grad_query_rows = jnp.einsum(
            "hqk,khd->qhd", grad_scores, keyset, preferred_element_type=jnp.float32
        )
        grad_query_rows = (grad_query_rows * score_scale).astype(jnp.bfloat16)
        key_accum = (
            key_accum
            + jnp.einsum(
                "hqk,qhd->khd", grad_scores, query_rows, preferred_element_type=jnp.float32
            )
            * score_scale
        )
        value_accum = value_accum + jnp.einsum(
            "hqk,qhd->khd",
            attn_probs.astype(jnp.bfloat16),
            grad_rows,
            preferred_element_type=jnp.float32,
        )
        return ((key_accum, value_accum), grad_query_rows)

    zero_heads = jnp.zeros((group_rows, local_heads, HEAD_DIM), jnp.float32)
    (key_accum, value_accum), grad_query_blocks = lax.scan(
        attend_back, (zero_heads, zero_heads), (block_starts, log_totals)
    )
    grad_query = grad_query_blocks.reshape(group_rows, head_cols)
    grad_key = key_accum.reshape(group_rows, head_cols).astype(jnp.bfloat16)
    grad_value = value_accum.reshape(group_rows, head_cols).astype(jnp.bfloat16)
    query_bias_term = place_block(D, jnp.sum(grad_query, axis=0, dtype=jnp.float32), tensor_rank)
    value_bias_term = place_block(D, jnp.sum(grad_value, axis=0, dtype=jnp.float32), tensor_rank)
    grad_wquery = contract_rows(group_one, grad_query)
    grad_wkey = contract_rows(group_one, grad_key)
    grad_wvalue = contract_rows(group_one, grad_value)
    grad_one = lax.psum_scatter(
        (
            contract_cols(grad_query, query_cols)
            + contract_cols(grad_key, key_cols)
            + contract_cols(grad_value, value_cols)
        ).astype(jnp.bfloat16),
        "tensor",
        scatter_dimension=0,
        tiled=True,
    ).astype(jnp.float32)
    norm_one_pull = jax.vjp(layer_norm, x_rows, gain_one, shift_one)[1]
    grad_x_norm, gain_one_term, shift_one_term = norm_one_pull(grad_one)
    grad_tokens = (grad_resid + grad_x_norm).astype(jnp.bfloat16)
    small_terms = jnp.stack(
        (
            gain_one_term,
            shift_one_term,
            query_bias_term,
            value_bias_term,
            out_bias_term,
            gain_two_term,
            shift_two_term,
            down_bias_term,
        ),
        axis=1,
    )
    small_terms = jnp.concatenate([small_terms, up_bias_term.reshape(-1, up_wide)], axis=1)
    small_terms = jnp.pad(small_terms, ((0, 0), (0, 128 - small_terms.shape[1])))
    terms = (grad_wquery, grad_wkey, grad_wvalue, grad_out.T, grad_up, grad_down.T, small_terms)
    packed_grads = jnp.concatenate([term.astype(jnp.bfloat16) for term in terms], axis=1)
    reduced = lax.psum_scatter(packed_grads, "dp", scatter_dimension=0, tiled=True).astype(
        jnp.float32
    )
    shards = [reduced[:, edges[i] : edges[i + 1]] for i in range(6)]
    shards[3] = shards[3].T
    shards[5] = shards[5].T
    sums = lax.psum(reduced[:, edges[6] : edges[6] + 8 + up_wide], "tensor")
    smalls = [sums[:, i] for i in range(7)] + [sums[:, 8:].reshape(-1), sums[:, 7]]
    back_y, back_dx = relocate(
        to_pieces(result_low, return_order), to_pieces(grad_tokens, return_order)
    )
    given_y = back_y.reshape(tok_rows, features)[sending_rank]
    given_dx = back_dx.reshape(tok_rows, features)[sending_rank]
    return (
        given_y,
        given_dx,
        smalls[0],
        smalls[1],
        shards[0],
        smalls[2],
        shards[1],
        shards[2],
        smalls[3],
        shards[3],
        smalls[4],
        smalls[5],
        smalls[6],
        shards[4],
        smalls[7],
        shards[5],
        smalls[8],
    )


def solution(mesh):
    in_specs = (
        P(("dp", "tensor"), None),
        P(("dp", "tensor"), None),
        P("dp"),
        P("dp"),
        P("dp", "tensor"),
        P("dp"),
        P("dp", "tensor"),
        P("dp", "tensor"),
        P("dp"),
        P("tensor", "dp"),
        P("dp"),
        P("dp"),
        P("dp"),
        P("dp", "tensor"),
        P("dp"),
        P("tensor", "dp"),
        P("dp"),
        P("dp", None),
        P("dp", "tensor", None),
        P("dp", "tensor", None),
    )
    out_specs = (
        P(("dp", "tensor"), None),
        P(("dp", "tensor"), None),
        P("dp"),
        P("dp"),
        P("dp", "tensor"),
        P("dp"),
        P("dp", "tensor"),
        P("dp", "tensor"),
        P("dp"),
        P("tensor", "dp"),
        P("dp"),
        P("dp"),
        P("dp"),
        P("dp", "tensor"),
        P("dp"),
        P("tensor", "dp"),
        P("dp"),
    )
    return jax.shard_map(body, mesh=mesh, in_specs=in_specs, out_specs=out_specs, check_vma=False)
```

```python
import jax
import jax.numpy as jnp
from jax import lax
from jax.experimental import pallas as pl
from jax.experimental.pallas import tpu as pltpu
from jax.sharding import PartitionSpec as P

D = 1024
HEADS = 16
HEAD_DIM = 64
FF = 4096


EPSILON = 1e-05
GELU_SCALE = 0.7978845608028654


def layer_norm(values, norm_gain, norm_shift):
    center = values - jnp.mean(values, axis=-1, keepdims=True)
    spread = jnp.mean(center * center, axis=-1, keepdims=True)
    return center * lax.rsqrt(spread + EPSILON) * norm_gain + norm_shift


def gelu_tanh(values):
    return jax.nn.gelu(values, approximate=True)


def contract_rows(first_op, second_op):
    return lax.dot_general(
        first_op, second_op, (((0,), (0,)), ((), ())), preferred_element_type=jnp.float32
    )


def contract_cols(first_op, second_op):
    return lax.dot_general(
        first_op, second_op, (((1,), (1,)), ((), ())), preferred_element_type=jnp.float32
    )


def take_block(vector, block_index, block_size):
    return lax.dynamic_slice_in_dim(vector, block_index * block_size, block_size, 0).astype(
        jnp.float32
    )


def place_block(total_size, block_vec, block_index):
    holder = jnp.zeros((total_size,), jnp.float32)
    return lax.dynamic_update_slice_in_dim(holder, block_vec, block_index * block_vec.shape[0], 0)


def sequence_marks(seq_lengths, group_rows):
    seq_ends = jnp.cumsum(seq_lengths)
    seq_starts = seq_ends - seq_lengths
    row_ids = lax.iota(jnp.int32, group_rows)
    inside = (row_ids[:, None] >= seq_starts[None, :]) & (row_ids[:, None] < seq_ends[None, :])
    seq_index = lax.iota(jnp.int32, seq_lengths.shape[0])
    seq_ids = jnp.sum(jnp.where(inside, seq_index[None, :], 0), axis=1)
    seq_start = jnp.sum(jnp.where(inside, seq_starts[None, :], 0), axis=1)
    return (seq_ids, row_ids - seq_start, row_ids)


def body(
    tokens,
    cotangent,
    norm1_gain,
    norm1_shift,
    w_query,
    b_query,
    w_key,
    w_value,
    b_value,
    w_out,
    b_out,
    norm2_gain,
    norm2_shift,
    w_up,
    b_up,
    w_down,
    b_down,
    lengths,
    deal_rank,
    arrival,
):
    dp_count = lax.axis_size("dp")
    tensor_count = lax.axis_size("tensor")
    tensor_rank = lax.axis_index("tensor")
    tok_rows = tokens.shape[0]
    features = tokens.shape[1]
    piece_rows = tok_rows // dp_count
    group_rows = tok_rows * tensor_count
    sending_rank = deal_rank.reshape(tok_rows)
    deal_order = jnp.argsort(sending_rank)
    arrive_order = arrival.reshape(tok_rows)
    return_order = jnp.argsort(arrive_order)

    def relocate(first_part, second_part):
        return (
            lax.all_to_all(first_part, "dp", split_axis=0, concat_axis=0, tiled=True),
            lax.all_to_all(second_part, "dp", split_axis=0, concat_axis=0, tiled=True),
        )

    def to_pieces(row_data, row_order):
        return row_data[row_order].reshape(dp_count, piece_rows, features)

    moved_x, moved_dy = relocate(to_pieces(tokens, deal_order), to_pieces(cotangent, deal_order))
    local_x = moved_x.reshape(tok_rows, features)[arrive_order]
    local_dy = moved_dy.reshape(tok_rows, features)[arrive_order]
    part_rows = w_query.shape[0]
    head_cols = w_query.shape[1]
    hidden_cols = w_up.shape[1]
    vectors = (
        norm1_gain,
        norm1_shift,
        b_query,
        b_value,
        b_out,
        norm2_gain,
        norm2_shift,
        b_down,
    )
    up_wide = b_up.shape[0] // part_rows
    vec_cols = jnp.concatenate(
        [jnp.stack(vectors, axis=1), b_up.reshape(part_rows, up_wide)], axis=1
    )
    vec_cols = jnp.pad(vec_cols, ((0, 0), (0, 128 - vec_cols.shape[1])))
    packed = jnp.concatenate(
        [w_query, w_key, w_value, w_out.T, w_up, w_down.T, vec_cols], axis=1
    )
    packed_all = lax.all_gather(packed, "dp", axis=0, tiled=True)
    edges = [0, head_cols, 2 * head_cols, 3 * head_cols, 4 * head_cols]
    edges += [4 * head_cols + hidden_cols, 4 * head_cols + 2 * hidden_cols]
    query_cols, key_cols, value_cols, out_cols, up_cols, down_cols = (
        packed_all[:, edges[i] : edges[i + 1]] for i in range(6)
    )
    out_rows = out_cols.T
    down_rows = down_cols.T
    vec_all = packed_all[:, edges[6] :]
    (
        gain_one,
        shift_one,
        bias_query,
        bias_value,
        bias_out,
        gain_two,
        shift_two,
        bias_down,
    ) = (vec_all[:, i] for i in range(8))
    bias_up = vec_all[:, 8 : 8 + up_wide].reshape(-1)
    gain_one = gain_one.astype(jnp.float32)
    shift_one = shift_one.astype(jnp.float32)
    gain_two = gain_two.astype(jnp.float32)
    shift_two = shift_two.astype(jnp.float32)
    local_heads = head_cols // HEAD_DIM
    score_scale = HEAD_DIM ** (-0.5)
    query_bias = take_block(bias_query, tensor_rank, head_cols)
    value_bias = take_block(bias_value, tensor_rank, head_cols)
    up_bias = take_block(bias_up, tensor_rank, hidden_cols)
    x_rows = local_x.astype(jnp.float32)
    first_in = layer_norm(x_rows, gain_one, shift_one).astype(jnp.bfloat16)
    group_one = lax.all_gather(first_in, "tensor", axis=0, tiled=True)
    queries = (
        jnp.dot(group_one, query_cols, preferred_element_type=jnp.float32) + query_bias
    ).astype(jnp.bfloat16)
    queries = queries.reshape(group_rows, local_heads, HEAD_DIM)
    keyset = jnp.dot(group_one, key_cols, preferred_element_type=jnp.float32).astype(jnp.bfloat16)
    keyset = keyset.reshape(group_rows, local_heads, HEAD_DIM)
    valset = (
        jnp.dot(group_one, value_cols, preferred_element_type=jnp.float32) + value_bias
    ).astype(jnp.bfloat16)
    valset = valset.reshape(group_rows, local_heads, HEAD_DIM)
    head_ids = tensor_rank * local_heads + lax.iota(jnp.int32, local_heads)
    slopes = jnp.exp2(-8.0 * (head_ids.astype(jnp.float32) + 1.0) / HEADS)
    seq_ids, positions, row_ids = sequence_marks(lengths[0], group_rows)
    qblock = min(512, group_rows)
    blocks = group_rows // qblock
    block_starts = lax.iota(jnp.int32, blocks) * qblock

    def block_scores(row_start):
        query_rows = lax.dynamic_slice_in_dim(queries, row_start, qblock, 0)
        raw_scores = (
            jnp.einsum("qhd,khd->hqk", query_rows, keyset, preferred_element_type=jnp.float32)
            * score_scale
        )
        seq_rows = lax.dynamic_slice_in_dim(seq_ids, row_start, qblock, 0)
        pos_rows = lax.dynamic_slice_in_dim(positions, row_start, qblock, 0)
        row_rows = lax.dynamic_slice_in_dim(row_ids, row_start, qblock, 0)
        distance = (pos_rows[:, None] - positions[None, :]).astype(jnp.float32)
        allowed = (seq_rows[:, None] == seq_ids[None, :]) & (row_rows[:, None] >= row_ids[None, :])
        scores = jnp.where(
            allowed[None], raw_scores - slopes[:, None, None] * distance[None], -1e30
        )
        return (query_rows, scores)

    def attend(row_start):
        query_rows, scores = block_scores(row_start)
        row_max = jnp.max(scores, axis=-1, keepdims=True)
        exponent = jnp.exp(scores - row_max)
        row_total = jnp.sum(exponent, axis=-1, keepdims=True)
        attn_probs = (exponent / row_total).astype(jnp.bfloat16)
        mixed = jnp.einsum("hqk,khd->qhd", attn_probs, valset, preferred_element_type=jnp.float32)
        return (mixed, row_max[..., 0] + jnp.log(row_total[..., 0]))

    mixed_all, log_totals = lax.map(attend, block_starts)
    heads_out = mixed_all.reshape(group_rows, head_cols).astype(jnp.bfloat16)
    attn_out = lax.psum_scatter(
        jnp.dot(heads_out, out_rows, preferred_element_type=jnp.float32).astype(jnp.bfloat16),
        "tensor",
        scatter_dimension=0,
        tiled=True,
    ).astype(jnp.float32) + bias_out.astype(jnp.float32)
    residual = x_rows + attn_out
    second_in = layer_norm(residual, gain_two, shift_two).astype(jnp.bfloat16)
    grad_in = local_dy.astype(jnp.float32)
    down_bias_term = jnp.sum(grad_in, axis=0)
    group_two = lax.all_gather(second_in, "tensor", axis=0, tiled=True)
    pre_act = jnp.dot(group_two, up_cols, preferred_element_type=jnp.float32) + up_bias
    activated = gelu_tanh(pre_act).astype(jnp.bfloat16)
    mlp_out = lax.psum_scatter(
        jnp.dot(activated, down_rows, preferred_element_type=jnp.float32).astype(jnp.bfloat16),
        "tensor",
        scatter_dimension=0,
        tiled=True,
    ).astype(jnp.float32)
    result = residual + mlp_out + bias_down.astype(jnp.float32)
    group_dy = lax.all_gather(local_dy, "tensor", axis=0, tiled=True)
    grad_down = contract_rows(activated, group_dy)
    grad_act = contract_cols(group_dy, down_rows)
    gelu_pull = jax.vjp(gelu_tanh, pre_act)[1]
    grad_pre = gelu_pull(grad_act)[0].astype(jnp.bfloat16)
    grad_up = contract_rows(group_two, grad_pre)
    up_bias_term = place_block(FF, jnp.sum(grad_pre, axis=0, dtype=jnp.float32), tensor_rank)
    grad_two = lax.psum_scatter(
        contract_cols(grad_pre, up_cols).astype(jnp.bfloat16),
        "tensor",
        scatter_dimension=0,
        tiled=True,
    ).astype(jnp.float32)
    result_low = result.astype(jnp.bfloat16)
    norm_two_pull = jax.vjp(layer_norm, residual, gain_two, shift_two)[1]
    grad_res_norm, gain_two_term, shift_two_term = norm_two_pull(grad_two)
    grad_resid = grad_in + grad_res_norm
    grad_attn = grad_resid.astype(jnp.bfloat16)
    out_bias_term = jnp.sum(grad_attn, axis=0, dtype=jnp.float32)
    group_grad = lax.all_gather(grad_attn, "tensor", axis=0, tiled=True)
    grad_out = contract_rows(heads_out, group_grad)
    grad_heads = (
        contract_cols(group_grad, out_rows)
        .astype(jnp.bfloat16)
        .reshape(group_rows, local_heads, HEAD_DIM)
    )

    def attend_back(running, block_item):
        key_accum, value_accum = running
        row_start, log_total = block_item
        query_rows, scores = block_scores(row_start)
        attn_probs = jnp.exp(scores - log_total[..., None])
        grad_rows = lax.dynamic_slice_in_dim(grad_heads, row_start, qblock, 0)
        grad_probs = jnp.einsum(
            "qhd,khd->hqk", grad_rows, valset, preferred_element_type=jnp.float32
        )
        row_dot = jnp.sum(attn_probs * grad_probs, axis=-1, keepdims=True)
        grad_scores = (attn_probs * (grad_probs - row_dot)).astype(jnp.bfloat16)
        grad_query_rows = jnp.einsum(
            "hqk,khd->qhd", grad_scores, keyset, preferred_element_type=jnp.float32
        )
        grad_query_rows = (grad_query_rows * score_scale).astype(jnp.bfloat16)
        key_accum = (
            key_accum
            + jnp.einsum(
                "hqk,qhd->khd", grad_scores, query_rows, preferred_element_type=jnp.float32
            )
            * score_scale
        )
        value_accum = value_accum + jnp.einsum(
            "hqk,qhd->khd",
            attn_probs.astype(jnp.bfloat16),
            grad_rows,
            preferred_element_type=jnp.float32,
        )
        return ((key_accum, value_accum), grad_query_rows)

    zero_heads = jnp.zeros((group_rows, local_heads, HEAD_DIM), jnp.float32)
    (key_accum, value_accum), grad_query_blocks = lax.scan(
        attend_back, (zero_heads, zero_heads), (block_starts, log_totals)
    )
    grad_query = grad_query_blocks.reshape(group_rows, head_cols)
    grad_key = key_accum.reshape(group_rows, head_cols).astype(jnp.bfloat16)
    grad_value = value_accum.reshape(group_rows, head_cols).astype(jnp.bfloat16)
    query_bias_term = place_block(D, jnp.sum(grad_query, axis=0, dtype=jnp.float32), tensor_rank)
    value_bias_term = place_block(D, jnp.sum(grad_value, axis=0, dtype=jnp.float32), tensor_rank)
    grad_wquery = contract_rows(group_one, grad_query)
    grad_wkey = contract_rows(group_one, grad_key)
    grad_wvalue = contract_rows(group_one, grad_value)
    grad_one = lax.psum_scatter(
        (
            contract_cols(grad_query, query_cols)
            + contract_cols(grad_key, key_cols)
            + contract_cols(grad_value, value_cols)
        ).astype(jnp.bfloat16),
        "tensor",
        scatter_dimension=0,
        tiled=True,
    ).astype(jnp.float32)
    norm_one_pull = jax.vjp(layer_norm, x_rows, gain_one, shift_one)[1]
    grad_x_norm, gain_one_term, shift_one_term = norm_one_pull(grad_one)
    grad_tokens = (grad_resid + grad_x_norm).astype(jnp.bfloat16)
    small_terms = jnp.stack(
        (
            gain_one_term,
            shift_one_term,
            query_bias_term,
            value_bias_term,
            out_bias_term,
            gain_two_term,
            shift_two_term,
            down_bias_term,
        ),
        axis=1,
    )
    small_terms = jnp.concatenate([small_terms, up_bias_term.reshape(-1, up_wide)], axis=1)
    small_terms = jnp.pad(small_terms, ((0, 0), (0, 128 - small_terms.shape[1])))
    terms = (grad_wquery, grad_wkey, grad_wvalue, grad_out.T, grad_up, grad_down.T, small_terms)
    packed_grads = jnp.concatenate([term.astype(jnp.bfloat16) for term in terms], axis=1)
    reduced = lax.psum_scatter(packed_grads, "dp", scatter_dimension=0, tiled=True).astype(
        jnp.float32
    )
    shards = [reduced[:, edges[i] : edges[i + 1]] for i in range(6)]
    shards[3] = shards[3].T
    shards[5] = shards[5].T
    sums = lax.psum(reduced[:, edges[6] : edges[6] + 8 + up_wide], "tensor")
    smalls = [sums[:, i] for i in range(7)] + [sums[:, 8:].reshape(-1), sums[:, 7]]
    back_y, back_dx = relocate(
        to_pieces(result_low, return_order), to_pieces(grad_tokens, return_order)
    )
    given_y = back_y.reshape(tok_rows, features)[sending_rank]
    given_dx = back_dx.reshape(tok_rows, features)[sending_rank]
    return (
        given_y,
        given_dx,
        smalls[0],
        smalls[1],
        shards[0],
        smalls[2],
        shards[1],
        shards[2],
        smalls[3],
        shards[3],
        smalls[4],
        smalls[5],
        smalls[6],
        shards[4],
        smalls[7],
        shards[5],
        smalls[8],
    )


MESH = pl.DeviceIdType.MESH
F32 = jnp.float32
LOW = jnp.bfloat16
RING = 8
PAIR = 128


def dot_nn(first_op, second_op):
    return lax.dot_general(
        first_op, second_op, (((1,), (0,)), ((), ())), preferred_element_type=F32
    )


def dot_nt(first_op, second_op):
    return lax.dot_general(
        first_op, second_op, (((1,), (1,)), ((), ())), preferred_element_type=F32
    )


def loop(count, step):
    def run(i, carry):
        step(i)
        return carry

    lax.fori_loop(0, count, run, 0)


def at(index, size):
    return pl.ds(pl.multiple_of(index * size, size), size)


def one_hot(first, second):
    return jnp.where(first == second, 1.0, 0.0).astype(LOW)


def fused_kernel(
    tok_ref,
    cot_ref,
    wq_ref,
    wk_ref,
    wv_ref,
    wot_ref,
    wup_ref,
    wdt_ref,
    vec_ref,
    rank_row,
    rank_col,
    arr_row,
    arr_col,
    len_ref,
    y_out,
    dx_out,
    gqkv_out,
    go_out,
    gu_out,
    gd_out,
    small_out,
    wqkv,
    wo,
    wu,
    wd,
    gqkv,
    go,
    gu,
    gd,
    tok_v,
    cot_v,
    pcx,
    pcd,
    arrx,
    arrd,
    backy,
    backd,
    xg,
    dyg,
    a1,
    qkv,
    qkvt,
    ho,
    lse,
    po,
    por,
    res,
    yb,
    a2,
    act,
    dpre,
    pm,
    pmr,
    pd,
    pdr,
    dattn,
    dh,
    dht,
    dqkv,
    dk_acc,
    dv_acc,
    tbuf,
    vgat,
    vrow,
    bqkv,
    bup,
    gvec,
    gbup,
    svec,
    svr,
    sown,
    sown_r,
    start_row,
    ld,
    ag_s,
    ag_r,
    mt_s,
    mt_r,
    aa_s,
    aa_r,
    y_s,
    y_r,
    rm_s,
    rm_r,
    rr_s,
    rr_r,
    ready_one,
    ready_two,
):
    d = lax.axis_index("dp")
    t = lax.axis_index("tensor")
    other = 1 - t
    core = lax.rem(d, 2)
    chip = lax.div(d, 2)
    xc = lax.rem(chip, 2)
    zc = lax.div(chip, 2)
    p = zc + xc * (7 - 2 * zc)

    def chip_at(pos):
        pos = lax.rem(pos + 2 * RING, RING)
        xx = lax.div(pos, 4)
        zz = pos + xx * (7 - 2 * pos)
        return zz * 2 + xx

    def dev(pos):
        return chip_at(pos) * 2 + core

    def mdev(pos):
        return chip_at(pos) * 2 + 1 - core

    mate = d + 1 - 2 * core
    sides = (dev(p + 1), dev(p - 1))
    weights = (wqkv, wo, wu, wd)
    grads = (gqkv, go, gu, gd)

    def remote(src, dst, send, recv, device):
        return pltpu.make_async_remote_copy(
            src_ref=src,
            dst_ref=dst,
            send_sem=send,
            recv_sem=recv,
            device_id=device,
            device_id_type=MESH,
        )

    def signal(sem, device):
        pl.semaphore_signal(sem, inc=1, device_id=device, device_id_type=MESH)

    loads = [
        pltpu.make_async_copy(tok_ref, tok_v, ld.at[0]),
        pltpu.make_async_copy(cot_ref, cot_v, ld.at[1]),
        pltpu.make_async_copy(wq_ref, wqkv.at[d, :, pl.ds(0, 512)], ld.at[2]),
        pltpu.make_async_copy(wk_ref, wqkv.at[d, :, pl.ds(512, 512)], ld.at[3]),
        pltpu.make_async_copy(wv_ref, wqkv.at[d, :, pl.ds(1024, 512)], ld.at[4]),
        pltpu.make_async_copy(wot_ref, wo.at[d], ld.at[5]),
        pltpu.make_async_copy(wup_ref, wu.at[d], ld.at[6]),
        pltpu.make_async_copy(wdt_ref, wd.at[d], ld.at[7]),
        pltpu.make_async_copy(vec_ref, vgat.at[d], ld.at[8]),
    ]
    for load in loads:
        load.start()
    barrier = pltpu.get_barrier_semaphore()

    def greet(k):
        signal(barrier, {"dp": lax.rem(d + k + 1, 16)})

    loop(15, greet)
    signal(barrier, {"tensor": other})

    def rows_copy(kind, src, dst, k, receive):
        if receive:
            spot = lax.rem(d + 16 - k, 16)
            return remote(
                src.at[at(spot, 16)],
                dst.at[at(spot, 16)],
                aa_s.at[kind, k],
                aa_r.at[kind, k],
                {"dp": spot},
            )
        spot = lax.rem(d + k, 16)
        return remote(
            src.at[at(spot, 16)],
            dst.at[at(d, 16)],
            aa_s.at[kind, k],
            aa_r.at[kind, k],
            {"dp": spot},
        )

    def rows_send(kind, src, dst):
        loop(15, lambda k: rows_copy(kind, src, dst, k + 1, False).start())
        dst[at(d, 16), :] = src[at(d, 16), :]

    def rows_wait(kind, src, dst):
        loop(15, lambda k: rows_copy(kind, src, dst, k + 1, True).wait_recv())

    def rows_drain(kind, src, dst):
        loop(15, lambda k: rows_copy(kind, src, dst, k + 1, False).wait_send())

    def tile_copy(kind, src_of, dst, k, receive):
        spot = lax.rem(d + 16 - k, 16) if receive else lax.rem(d + k, 16)
        return remote(
            src_of(spot),
            dst.at[spot if receive else d],
            aa_s.at[kind, k],
            aa_r.at[kind, k],
            {"dp": spot},
        )

    def cross(i, src, dst):
        return remote(src, dst, y_s.at[i], y_r.at[i], {"tensor": other})

    def ring_part(ref, slot, way, step):
        if step == 3:
            return ref.at[slot, pl.ds(32 * way, 32)]
        return ref.at[slot]

    def turn(way, steps):
        return p - steps if way == 0 else p + steps

    def ag_copy(c, way, step):
        part = ring_part(weights[c], dev(turn(way, step)), way, step)
        return remote(
            part, part, ag_s.at[c, way, step], ag_r.at[c, way, step], {"dp": sides[way]}
        )

    def ag_arrival(c, way, step):
        part = ring_part(weights[c], dev(turn(way, step + 1)), way, step)
        return remote(
            part, part, ag_s.at[c, way, step], ag_r.at[c, way, step], {"dp": sides[way]}
        )

    def mate_copy(c, k, place):
        if k == 0:
            part = weights[c].at[place(p)]
        else:
            way, step = (k - 1) // 4, (k - 1) % 4
            part = ring_part(weights[c], place(turn(way, step + 1)), way, step)
        return remote(part, part, mt_s.at[c, k], mt_r.at[c, k], {"dp": mate})

    def ag_start(c):
        for way in range(2):
            ag_copy(c, way, 0).start()
        mate_copy(c, 0, dev).start()

    def ag_event(c, step):
        for way in range(2):
            ag_arrival(c, way, step).wait_recv()
            if step < 3:
                ag_copy(c, way, step + 1).start()
            mate_copy(c, 1 + 4 * way + step, dev).start()

    def ag_finish(c):
        for k in range(9):
            mate_copy(c, k, mdev).wait_recv()

    def ag_drain(c):
        for way in range(2):
            for step in range(4):
                ag_copy(c, way, step).wait_send()
        for k in range(9):
            mate_copy(c, k, dev).wait_send()

    def rm_copy(c, spot):
        return remote(
            grads[c].at[spot * 2 + 1 - core],
            weights[c].at[spot],
            rm_s.at[c, spot],
            rm_r.at[c, spot],
            {"dp": mate},
        )

    def rs_copy(c, way, step):
        dest = dev(p + 4 - step if way == 0 else p - 4 + step)
        slot = 8 + way * 4 + step
        if step == 0:
            half = pl.ds(32 * way, 32)
            src, dst = grads[c].at[dest, half], weights[c].at[slot, half]
        else:
            src, dst = grads[c].at[dest], weights[c].at[slot]
        return remote(src, dst, rr_s.at[c, way, step], rr_r.at[c, way, step], {"dp": sides[way]})

    def rs_start(c):
        far = chip_at(p + 4)
        rm_copy(c, far).wait_recv()
        slot = far * 2 + core

        def add(i):
            rows = at(i, 16)
            total = grads[c][slot, rows, :].astype(F32) + weights[c][far, rows, :].astype(F32)
            grads[c][slot, rows, :] = total.astype(LOW)

        loop(4, add)
        for way in range(2):
            rs_copy(c, way, 0).start()

    def rs_event(c, step):
        for way in range(2):
            pos = p + 3 - step if way == 0 else p - 3 + step
            spot = chip_at(pos)
            slot = spot * 2 + core
            held = 8 + way * 4 + step
            rs_copy(c, way, step).wait_recv()
            rm_copy(c, spot).wait_recv()

            def add(i, with_held):
                rows = at(i, 16)
                total = grads[c][slot, rows, :].astype(F32) + weights[c][spot, rows, :].astype(F32)
                if with_held:
                    total += weights[c][held, rows, :].astype(F32)
                grads[c][slot, rows, :] = total.astype(LOW)

            if step == 0:
                loop(2, lambda i: add(i + 2 * way, True))
                loop(2, lambda i: add(i + 2 - 2 * way, False))
            else:
                loop(4, lambda i: add(i, True))
            rs_copy(c, way, step + 1).start()

    def rs_finish(c, out):
        for way in range(2):
            rs_copy(c, way, 3).wait_recv()
        rm_copy(c, chip).wait_recv()

        def add(i):
            rows = at(i, 16)
            total = grads[c][d, rows, :].astype(F32) + weights[c][chip, rows, :].astype(F32)
            total += weights[c][11, rows, :].astype(F32) + weights[c][15, rows, :].astype(F32)
            out[rows, :] = total

        loop(4, add)

    def rs_drain(c):
        for way in range(2):
            for step in range(4):
                rs_copy(c, way, step).wait_send()
        loop(8, lambda i: rm_copy(c, i).wait_send())

    def free_for_reduction(sem):
        signal(sem, {"dp": mate})
        for side in sides:
            signal(sem, {"dp": side})

    loads[0].wait()
    spread = one_hot(lax.broadcasted_iota(jnp.int32, (256, 256), 0), rank_row[...])
    pcx[...] = dot_nn(spread, tok_v[...]).astype(LOW)
    pl.semaphore_wait(barrier, 16)
    rows_send(0, pcx, arrx)
    loads[8].wait()
    loop(15, lambda k: tile_copy(4, lambda spot: vgat.at[d], vgat, k + 1, False).start())
    for i in range(2, 6):
        loads[i].wait()
    ag_start(0)
    ag_start(1)
    loads[1].wait()
    pcd[...] = dot_nn(spread, cot_v[...]).astype(LOW)
    for i in range(6, 8):
        loads[i].wait()

    own = at(t, 256)
    gather_rows = one_hot(arr_col[...], lax.broadcasted_iota(jnp.int32, (256, 256), 1))
    rows_wait(0, pcx, arrx)
    xg[own, :] = dot_nn(gather_rows, arrx[...]).astype(LOW)
    cross(0, xg.at[own], xg.at[own]).start()
    ag_event(0, 0)
    ag_event(1, 0)

    loop(15, lambda k: tile_copy(4, lambda spot: vgat.at[d], vgat, k + 1, True).wait_recv())
    for m in range(8):
        both = vgat[2 * m, :, :].astype(F32) + vgat[2 * m + 1, :, :].astype(F32)
        vrow[:, 128 * m : 128 * (m + 1)] = both[0:8, :]
    for j in range(8):
        block = vgat[8 * t + j, :, :].astype(F32)
        bup[:, 256 * j : 256 * j + 128] = block[8:9, :]
        bup[:, 256 * j + 128 : 256 * j + 256] = block[9:10, :]
    bqkv[:, 0:512] = vrow[2:3, at(t, 512)]
    bqkv[:, 512:1024] = jnp.zeros((1, 512), F32)
    bqkv[:, 1024:1536] = vrow[3:4, at(t, 512)]
    ends = jnp.int32(0)
    row_ids = lax.broadcasted_iota(jnp.int32, (1, 512), 1)
    starts = jnp.zeros((1, 512), jnp.int32)
    for i in range(3):
        ends = ends + len_ref[0, i]
        starts = jnp.where(row_ids >= ends, ends, starts)
    start_row[...] = starts
    gvec[...] = jnp.zeros((8, 1024), F32)
    gbup[...] = jnp.zeros((1, 2048), F32)

    def stats(values):
        center = values - jnp.mean(values, axis=-1, keepdims=True)
        spread_of = jnp.mean(center * center, axis=-1, keepdims=True)
        scale = lax.rsqrt(spread_of + EPSILON)
        return center * scale, scale

    def norm_one(half):
        def step(i):
            rows = at(half * 8 + i, 32)
            normed, _ = stats(xg[rows, :].astype(F32))
            a1[rows, :] = (normed * vrow[0:1, :] + vrow[1:2, :]).astype(LOW)

        loop(8, step)

    norm_one(t)
    ag_event(0, 1)
    ag_event(1, 1)
    rows_send(1, pcd, arrd)
    cross(0, xg.at[own], xg.at[at(other, 256)]).wait_recv()
    norm_one(other)
    ag_event(0, 2)
    ag_event(1, 2)
    ag_start(2)
    ag_event(0, 3)
    ag_event(1, 3)
    ag_start(3)
    ag_finish(0)

    def project(i):
        cols = at(i, 256)
        value = dot_nn(a1[...], wqkv[:, :, cols].reshape(1024, 256)) + bqkv[:, cols]
        low = value.astype(LOW).astype(F32)
        qkv[:, cols] = low.astype(LOW)
        qkvt[cols, :] = low.T.astype(LOW)

    loop(6, project)
    ag_event(2, 0)

    def slope_of(pair, half):
        head = (t * 8 + pair * 2 + half + 1).astype(F32)
        return jnp.exp2(jnp.full((1, PAIR), -0.5, F32) * head)

    def padded(block, half):
        zero = jnp.zeros_like(block)
        return jnp.concatenate([block, zero] if half == 0 else [zero, block], axis=0)

    def band(qb):
        first = max(0, qb - 2) * 128
        width = (qb + 1) * 128 - first
        keys = lax.broadcasted_iota(jnp.int32, (width, PAIR), 0) + first
        rows = lax.broadcasted_iota(jnp.int32, (width, PAIR), 1) + qb * 128
        allowed = (keys <= rows) & (keys >= start_row[:, qb * 128 : qb * 128 + 128])
        return first, width, allowed, (rows - keys).astype(F32)

    def score(pair, half, qb, first, width, allowed, distance):
        key_rows = qkv[first : first + width, at(pair + 4, PAIR)]
        query = qkvt[at(pair * 2 + half, 64), qb * 128 : qb * 128 + 128] * 0.125
        raw = dot_nn(key_rows, padded(query, half))
        return jnp.where(allowed, raw - slope_of(pair, half) * distance, -1e30)

    def attend(qbs):
        def step(pair):
            for qb in qbs:
                first, width, allowed, distance = band(qb)
                parts = []
                for half in range(2):
                    s = score(pair, half, qb, first, width, allowed, distance)
                    top = jnp.max(s, axis=0, keepdims=True)
                    e = jnp.exp(s - top)
                    total = jnp.sum(e, axis=0, keepdims=True)
                    probs = (e * (1.0 / total)).astype(LOW)
                    lse[pair * 2 + half, :, qb * 128 : qb * 128 + 128] = top + jnp.log(total)
                    value_t = qkvt[at(16 + pair * 2 + half, 64), first : first + width]
                    parts.append(dot_nn(value_t, probs))
                ho[qb * 128 : qb * 128 + 128, at(pair, PAIR)] = (
                    jnp.concatenate(parts, axis=0).T.astype(LOW)
                )

        loop(4, step)

    def out_project(rb):
        rows = slice(rb * 256, rb * 256 + 256)

        def step(i):
            po[rows, at(i, 256)] = dot_nt(ho[rows, :], wo[pl.ds(i * 4, 4)].reshape(256, 512)).astype(LOW)

        loop(4, step)
        cross(2 + rb, po.at[rows], por.at[rows]).start()

    attend((0, 1))
    ag_finish(1)
    out_project(0)
    ag_event(3, 0)
    attend((2, 3))
    out_project(1)
    rows_wait(1, pcd, arrd)
    dyg[own, :] = dot_nn(gather_rows, arrd[...]).astype(LOW)
    cross(1, dyg.at[own], dyg.at[own]).start()
    ag_event(2, 1)
    ag_event(3, 1)
    ag_event(2, 2)
    ag_event(3, 2)
    cross(1, dyg.at[own], dyg.at[at(other, 256)]).wait_recv()
    ag_event(2, 3)
    ag_event(3, 3)
    ag_finish(3)

    def act_back(i):
        cols = at(i, 256)
        dpre[:, cols] = dot_nn(dyg[...], wd[:, :, cols].reshape(1024, 256)).astype(LOW)

    loop(8, act_back)
    ag_finish(2)

    def mlp(rb):
        rows = slice(rb * 256, rb * 256 + 256)
        cross(2 + rb, po.at[rows], por.at[rows]).wait_recv()

        def enter(i):
            part = at(rb * 8 + i, 32)
            value = xg[part, :].astype(F32) + (po[part, :].astype(F32) + por[part, :].astype(F32))
            value = value + vrow[4:5, :]
            res[part, :] = value
            normed, _ = stats(value)
            a2[part, :] = (normed * vrow[5:6, :] + vrow[6:7, :]).astype(LOW)

        loop(8, enter)

        def up(i):
            cols = at(i, 256)
            v = dot_nn(a2[rows, :], wu[:, :, cols].reshape(1024, 256)) + bup[:, cols]
            square = v * v
            bend = jnp.tanh(GELU_SCALE * (v + 0.044715 * (square * v)))
            act[rows, cols] = (0.5 * v * (1.0 + bend)).astype(LOW)
            slope = 0.5 * (1.0 + bend) + 0.5 * v * (1.0 - bend * bend) * (
                GELU_SCALE * (1.0 + 3.0 * 0.044715 * square)
            )
            back = (dpre[rows, cols].astype(F32) * slope).astype(LOW)
            dpre[rows, cols] = back
            gbup[:, cols] += jnp.sum(back.astype(F32), axis=0, keepdims=True)

        loop(8, up)

        def down(i):
            pd[rows, at(i, 256)] = dot_nt(dpre[rows, :], wu[pl.ds(i * 4, 4)].reshape(256, 2048)).astype(LOW)

        loop(4, down)
        cross(5 + rb, pd.at[rows], pdr.at[rows]).start()

    mlp(0)
    mlp(1)
    yb[...] = res[own, :]

    def mlp_out(i):
        pm[:, at(i, 256)] = dot_nt(act[...], wd[pl.ds(i * 4, 4)].reshape(256, 2048)).astype(LOW)

    loop(4, mlp_out)
    cross(4, pm.at[at(other, 256)], pmr).start()
    ag_drain(2)
    ag_drain(3)
    free_for_reduction(ready_one)

    def flip(ref):
        def step(i):
            tbuf[at(i, 256), :] = ref[:, at(i, 256)].T

        loop(4, step)

    def weight_grad(c, first_ref, second_ref, width):
        flip(first_ref)

        def step(i):
            rows = at(i, 256)

            def inner(j):
                cols = at(j, 512)
                grads[c][pl.ds(i * 4, 4), :, cols] = (
                    dot_nn(tbuf[rows, :], second_ref[:, cols]).astype(LOW).reshape(4, 64, 512)
                )

            loop(width // 512, inner)
            rm_copy(c, i * 2).start()
            rm_copy(c, i * 2 + 1).start()

        loop(4, step)

    pl.semaphore_wait(ready_one, 3)
    weight_grad(3, dyg, act, 2048)
    rs_start(3)
    weight_grad(2, a2, dpre, 2048)
    rs_start(2)

    def norm_two_back(rb):
        rows = slice(rb * 256, rb * 256 + 256)
        cross(5 + rb, pd.at[rows], pdr.at[rows]).wait_recv()

        def step(i):
            part = at(rb * 8 + i, 32)
            grad = pd[part, :].astype(F32) + pdr[part, :].astype(F32)
            normed, scale = stats(res[part, :])
            e = grad * vrow[5:6, :]
            inner = e - jnp.mean(e, axis=-1, keepdims=True)
            inner = inner - normed * jnp.mean(e * normed, axis=-1, keepdims=True)
            dy = dyg[part, :].astype(F32)
            full = dy + inner * scale
            res[part, :] = full
            low = full.astype(LOW)
            dattn[part, :] = low
            gvec[4:5, :] += 0.5 * jnp.sum(low.astype(F32), axis=0, keepdims=True)
            gvec[5:6, :] += 0.5 * jnp.sum(grad * normed, axis=0, keepdims=True)
            gvec[6:7, :] += 0.5 * jnp.sum(grad, axis=0, keepdims=True)
            gvec[7:8, :] += 0.5 * jnp.sum(dy, axis=0, keepdims=True)

        loop(8, step)

        def heads(i):
            cols = at(i, 256)
            value = dot_nn(dattn[rows, :], wo[:, :, cols].reshape(1024, 256)).astype(LOW)
            dh[rows, cols] = value
            dht[cols, rows] = value.astype(F32).T.astype(LOW)

        loop(2, heads)

    norm_two_back(0)
    rs_event(3, 0)
    norm_two_back(1)
    rs_event(2, 0)

    lanes = lax.broadcasted_iota(jnp.int32, (1, PAIR), 1) < 64

    def attend_back(first_pair, count):
        def step(index):
            pair = index + first_pair
            dk_acc[...] = jnp.zeros((512, PAIR), F32)
            dv_acc[...] = jnp.zeros((512, PAIR), F32)
            for qb in range(4):
                first, width, allowed, distance = band(qb)
                queries = slice(qb * 128, qb * 128 + 128)
                span = slice(first, first + width)
                values = qkv[span, at(pair + 8, PAIR)]
                query_rows = qkv[queries, at(pair, PAIR)]
                grad_rows = dh[queries, at(pair, PAIR)]
                parts, keys_part, values_part = [], [], []
                for half in range(2):
                    s = score(pair, half, qb, first, width, allowed, distance)
                    probs = jnp.exp(s - lse[pair * 2 + half, :, queries])
                    grad_t = dht[at(pair * 2 + half, 64), queries]
                    grad_p = dot_nn(values, padded(grad_t, half))
                    row_dot = jnp.sum(probs * grad_p, axis=0, keepdims=True)
                    grad_s = (probs * (grad_p - row_dot)).astype(LOW)
                    key_t = qkvt[at(8 + pair * 2 + half, 64), span]
                    parts.append(dot_nn(key_t, grad_s))
                    keys_part.append(dot_nn(grad_s, query_rows))
                    values_part.append(dot_nn(probs.astype(LOW), grad_rows))
                dqkv[queries, at(pair, PAIR)] = (
                    (jnp.concatenate(parts, axis=0) * 0.125).T.astype(LOW)
                )
                dk_acc[span, :] += jnp.where(lanes, keys_part[0], keys_part[1])
                dv_acc[span, :] += jnp.where(lanes, values_part[0], values_part[1])
            dqkv[:, at(pair + 4, PAIR)] = (dk_acc[...] * 0.125).astype(LOW)
            dqkv[:, at(pair + 8, PAIR)] = dv_acc[...].astype(LOW)

        loop(count, step)

    cross(4, pm.at[at(other, 256)], pmr).wait_recv()
    rows_drain(0, pcx, arrx)
    rows_drain(1, pcd, arrd)
    send_back = one_hot(lax.broadcasted_iota(jnp.int32, (256, 256), 0), arr_row[...])
    take_back = one_hot(rank_col[...], lax.broadcasted_iota(jnp.int32, (256, 256), 1))

    def finish_y(i):
        part = at(i, 32)
        mine = at(t * 8 + i, 32)
        value = yb[part, :] + (pm[mine, :].astype(F32) + pmr[part, :].astype(F32)) + vrow[7:8, :]
        tok_v[part, :] = value.astype(LOW)

    loop(8, finish_y)
    pcx[...] = dot_nn(send_back, tok_v[...]).astype(LOW)
    rows_send(2, pcx, backy)

    attend_back(0, 2)
    rs_event(3, 1)
    rs_event(2, 1)
    attend_back(2, 2)
    rs_event(3, 2)
    rs_event(2, 2)

    def attn_in_back(i):
        po[:, at(i, 256)] = dot_nt(dqkv[...], wqkv[pl.ds(i * 4, 4)].reshape(256, 1536)).astype(LOW)

    for rb in range(2):
        rows = slice(rb * 256, rb * 256 + 256)
        cross(2 + rb, po.at[rows], por.at[rows]).wait_send()
    loop(4, attn_in_back)
    cross(7, po.at[at(other, 256)], por.at[pl.ds(0, 256)]).start()
    ag_drain(0)
    ag_drain(1)
    free_for_reduction(ready_two)
    pl.semaphore_wait(ready_two, 3)
    weight_grad(0, a1, dqkv, 1536)
    rs_start(0)
    weight_grad(1, dattn, ho, 512)
    rs_start(1)
    rs_finish(3, gd_out)
    rs_finish(2, gu_out)
    sums = jnp.zeros((1, 1536), F32)
    for i in range(4):
        sums = sums + jnp.sum(dqkv[i * 128 : i * 128 + 128, :].astype(F32), axis=0, keepdims=True)
    gvec[2:3, at(t, 512)] = sums[:, 0:512]
    gvec[3:4, at(t, 512)] = sums[:, 1024:1536]
    cross(7, po.at[at(other, 256)], por.at[pl.ds(0, 256)]).wait_recv()

    def norm_one_back(i):
        part = at(i, 32)
        mine = at(t * 8 + i, 32)
        grad = po[mine, :].astype(F32) + por[part, :].astype(F32)
        normed, scale = stats(xg[mine, :].astype(F32))
        e = grad * vrow[0:1, :]
        inner = e - jnp.mean(e, axis=-1, keepdims=True)
        inner = inner - normed * jnp.mean(e * normed, axis=-1, keepdims=True)
        cot_v[part, :] = (res[mine, :] + inner * scale).astype(LOW)
        gvec[0:1, :] += jnp.sum(grad * normed, axis=0, keepdims=True)
        gvec[1:2, :] += jnp.sum(grad, axis=0, keepdims=True)

    loop(8, norm_one_back)
    rs_event(0, 0)
    rs_event(1, 0)
    a2[0:256, :] = dot_nn(send_back, cot_v[...]).astype(LOW)
    rows_send(3, a2, backd)

    for e in range(16):
        svec[e, 0:8, :] = gvec[:, 128 * (e // 2) : 128 * (e // 2) + 128]
        svec[e, 8:16, :] = jnp.zeros((8, 128), F32)
    for j in range(8):
        svec[8 * t + j, 8:9, :] = gbup[:, 256 * j : 256 * j + 128]
        svec[8 * t + j, 9:10, :] = gbup[:, 256 * j + 128 : 256 * j + 256]
    loop(15, lambda k: tile_copy(5, lambda spot: svec.at[spot], svr, k + 1, False).start())
    svr[d] = svec[d]
    rs_event(0, 1)
    rs_event(1, 1)
    rows_wait(2, pcx, backy)
    y_out[...] = dot_nn(take_back, backy[...]).astype(LOW)
    loop(15, lambda k: tile_copy(5, lambda spot: svec.at[spot], svr, k + 1, True).wait_recv())
    small = jnp.zeros((16, 128), F32)
    for e in range(16):
        small = small + svr[e]
    sown[...] = small
    cross(8, sown, sown_r).start()
    rs_event(0, 2)
    rs_event(1, 2)
    rows_wait(3, a2, backd)
    dx_out[...] = dot_nn(take_back, backd[...]).astype(LOW)
    cross(8, sown, sown_r).wait_recv()
    small_out[...] = sown[...] + sown_r[...]
    rs_finish(0, gqkv_out)
    rs_finish(1, go_out)

    for c in range(4):
        rs_drain(c)
    rows_drain(2, pcx, backy)
    rows_drain(3, a2, backd)
    loop(15, lambda k: tile_copy(4, lambda spot: vgat.at[d], vgat, k + 1, False).wait_send())
    loop(15, lambda k: tile_copy(5, lambda spot: svec.at[spot], svr, k + 1, False).wait_send())
    cross(0, xg.at[own], xg.at[own]).wait_send()
    cross(1, dyg.at[own], dyg.at[own]).wait_send()
    cross(4, pm.at[at(other, 256)], pmr).wait_send()
    for rb in range(2):
        rows = slice(rb * 256, rb * 256 + 256)
        cross(5 + rb, pd.at[rows], pdr.at[rows]).wait_send()
    cross(7, po.at[at(other, 256)], por.at[pl.ds(0, 256)]).wait_send()
    cross(8, sown, sown_r).wait_send()


def fused_body(
    tokens,
    cotangent,
    norm1_gain,
    norm1_shift,
    w_query,
    b_query,
    w_key,
    w_value,
    b_value,
    w_out,
    b_out,
    norm2_gain,
    norm2_shift,
    w_up,
    b_up,
    w_down,
    b_down,
    lengths,
    deal_rank,
    arrival,
):
    odd = lax.rem(lax.axis_index("dp"), 2)
    vectors = jnp.stack(
        (norm1_gain, norm1_shift, b_query, b_value, b_out, norm2_gain, norm2_shift, b_down)
    )
    zero = jnp.zeros_like(vectors)
    vectors = jnp.where(
        odd == 0,
        jnp.concatenate([vectors, zero], axis=1),
        jnp.concatenate([zero, vectors], axis=1),
    )
    vec_tile = jnp.concatenate([vectors, b_up.reshape(2, 128), jnp.zeros((6, 128), LOW)], axis=0)
    rank = deal_rank.reshape(256)
    arrive = arrival.reshape(256)

    def vm(*shape, dtype=LOW):
        return pltpu.VMEM(shape, dtype)

    def dma(*shape):
        return pltpu.SemaphoreType.DMA(shape)

    scratch = [
        vm(16, 64, 1536),
        vm(16, 64, 512),
        vm(16, 64, 2048),
        vm(16, 64, 2048),
        vm(16, 64, 1536),
        vm(16, 64, 512),
        vm(16, 64, 2048),
        vm(16, 64, 2048),
        vm(256, 1024),
        vm(256, 1024),
        vm(256, 1024),
        vm(256, 1024),
        vm(256, 1024),
        vm(256, 1024),
        vm(256, 1024),
        vm(256, 1024),
        vm(512, 1024),
        vm(512, 1024),
        vm(512, 1024),
        vm(512, 1536),
        vm(1536, 512),
        vm(512, 512),
        vm(8, 1, 512, dtype=F32),
        vm(512, 1024),
        vm(512, 1024),
        vm(512, 1024, dtype=F32),
        vm(256, 1024, dtype=F32),
        vm(512, 1024),
        vm(512, 2048),
        vm(512, 2048),
        vm(512, 1024),
        vm(256, 1024),
        vm(512, 1024),
        vm(512, 1024),
        vm(512, 1024),
        vm(512, 512),
        vm(512, 512),
        vm(512, 1536),
        vm(512, 128, dtype=F32),
        vm(512, 128, dtype=F32),
        vm(1024, 512),
        vm(16, 16, 128),
        vm(8, 1024, dtype=F32),
        vm(1, 1536, dtype=F32),
        vm(1, 2048, dtype=F32),
        vm(8, 1024, dtype=F32),
        vm(1, 2048, dtype=F32),
        vm(16, 16, 128, dtype=F32),
        vm(16, 16, 128, dtype=F32),
        vm(16, 128, dtype=F32),
        vm(16, 128, dtype=F32),
        vm(1, 512, dtype=jnp.int32),
        dma(9),
        dma(4, 2, 4),
        dma(4, 2, 4),
        dma(4, 9),
        dma(4, 9),
        dma(6, 16),
        dma(6, 16),
        dma(9),
        dma(9),
        dma(4, 8),
        dma(4, 8),
        dma(4, 2, 4),
        dma(4, 2, 4),
        pltpu.SemaphoreType.REGULAR,
        pltpu.SemaphoreType.REGULAR,
    ]
    anywhere = pl.BlockSpec(memory_space=pl.ANY)
    inside = pl.BlockSpec(memory_space=pltpu.VMEM)
    outs = (
        jax.ShapeDtypeStruct((256, 1024), LOW),
        jax.ShapeDtypeStruct((256, 1024), LOW),
        jax.ShapeDtypeStruct((64, 1536), F32),
        jax.ShapeDtypeStruct((64, 512), F32),
        jax.ShapeDtypeStruct((64, 2048), F32),
        jax.ShapeDtypeStruct((64, 2048), F32),
        jax.ShapeDtypeStruct((16, 128), F32),
    )
    result, grad_tokens, grad_qkv, grad_out, grad_up, grad_down, small = pl.pallas_call(
        fused_kernel,
        name="fused_layer",
        out_shape=outs,
        in_specs=[anywhere] * 9 + [inside] * 4 + [pl.BlockSpec(memory_space=pltpu.SMEM)],
        out_specs=[inside] * 7,
        scratch_shapes=scratch,
        compiler_params=pltpu.CompilerParams(
            collective_id=0, has_side_effects=True, vmem_limit_bytes=67043328
        ),
    )(
        tokens,
        cotangent,
        w_query,
        w_key,
        w_value,
        w_out.T,
        w_up,
        w_down.T,
        vec_tile,
        rank.reshape(1, 256),
        rank.reshape(256, 1),
        arrive.reshape(1, 256),
        arrive.reshape(256, 1),
        lengths,
    )
    picked = jnp.where(odd == 0, small[0:8, 0:64], small[0:8, 64:128])
    return (
        result,
        grad_tokens,
        picked[0],
        picked[1],
        grad_qkv[:, 0:512],
        picked[2],
        grad_qkv[:, 512:1024],
        grad_qkv[:, 1024:1536],
        picked[3],
        grad_out.T,
        picked[4],
        picked[5],
        picked[6],
        grad_up,
        small[8:10].reshape(256),
        grad_down.T,
        picked[7],
    )


def solution(mesh):
    in_specs = (
        P(("dp", "tensor"), None),
        P(("dp", "tensor"), None),
        P("dp"),
        P("dp"),
        P("dp", "tensor"),
        P("dp"),
        P("dp", "tensor"),
        P("dp", "tensor"),
        P("dp"),
        P("tensor", "dp"),
        P("dp"),
        P("dp"),
        P("dp"),
        P("dp", "tensor"),
        P("dp"),
        P("tensor", "dp"),
        P("dp"),
        P("dp", None),
        P("dp", "tensor", None),
        P("dp", "tensor", None),
    )
    out_specs = (
        P(("dp", "tensor"), None),
        P(("dp", "tensor"), None),
        P("dp"),
        P("dp"),
        P("dp", "tensor"),
        P("dp"),
        P("dp", "tensor"),
        P("dp", "tensor"),
        P("dp"),
        P("tensor", "dp"),
        P("dp"),
        P("dp"),
        P("dp"),
        P("dp", "tensor"),
        P("dp"),
        P("tensor", "dp"),
        P("dp"),
    )
    small_slice = mesh.shape["dp"] == 16 and mesh.shape["tensor"] == 2
    program = fused_body if small_slice else body
    return jax.shard_map(program, mesh=mesh, in_specs=in_specs, out_specs=out_specs, check_vma=False)
```

```python
import jax
import jax.numpy as jnp
from jax import lax
from jax.experimental import pallas as pl
from jax.experimental.pallas import tpu as pltpu
from jax.sharding import PartitionSpec as P

D = 1024
HEADS = 16
HEAD_DIM = 64
FF = 4096


EPSILON = 1e-05
GELU_SCALE = 0.7978845608028654


def layer_norm(values, norm_gain, norm_shift):
    center = values - jnp.mean(values, axis=-1, keepdims=True)
    spread = jnp.mean(center * center, axis=-1, keepdims=True)
    return center * lax.rsqrt(spread + EPSILON) * norm_gain + norm_shift


def gelu_tanh(values):
    return jax.nn.gelu(values, approximate=True)


def contract_rows(first_op, second_op):
    return lax.dot_general(
        first_op, second_op, (((0,), (0,)), ((), ())), preferred_element_type=jnp.float32
    )


def contract_cols(first_op, second_op):
    return lax.dot_general(
        first_op, second_op, (((1,), (1,)), ((), ())), preferred_element_type=jnp.float32
    )


def take_block(vector, block_index, block_size):
    return lax.dynamic_slice_in_dim(vector, block_index * block_size, block_size, 0).astype(
        jnp.float32
    )


def place_block(total_size, block_vec, block_index):
    holder = jnp.zeros((total_size,), jnp.float32)
    return lax.dynamic_update_slice_in_dim(holder, block_vec, block_index * block_vec.shape[0], 0)


def sequence_marks(seq_lengths, group_rows):
    seq_ends = jnp.cumsum(seq_lengths)
    seq_starts = seq_ends - seq_lengths
    row_ids = lax.iota(jnp.int32, group_rows)
    inside = (row_ids[:, None] >= seq_starts[None, :]) & (row_ids[:, None] < seq_ends[None, :])
    seq_index = lax.iota(jnp.int32, seq_lengths.shape[0])
    seq_ids = jnp.sum(jnp.where(inside, seq_index[None, :], 0), axis=1)
    seq_start = jnp.sum(jnp.where(inside, seq_starts[None, :], 0), axis=1)
    return (seq_ids, row_ids - seq_start, row_ids)


def body(
    tokens,
    cotangent,
    norm1_gain,
    norm1_shift,
    w_query,
    b_query,
    w_key,
    w_value,
    b_value,
    w_out,
    b_out,
    norm2_gain,
    norm2_shift,
    w_up,
    b_up,
    w_down,
    b_down,
    lengths,
    deal_rank,
    arrival,
):
    dp_count = lax.axis_size("dp")
    tensor_count = lax.axis_size("tensor")
    tensor_rank = lax.axis_index("tensor")
    tok_rows = tokens.shape[0]
    features = tokens.shape[1]
    piece_rows = tok_rows // dp_count
    group_rows = tok_rows * tensor_count
    sending_rank = deal_rank.reshape(tok_rows)
    deal_order = jnp.argsort(sending_rank)
    arrive_order = arrival.reshape(tok_rows)
    return_order = jnp.argsort(arrive_order)

    def relocate(first_part, second_part):
        return (
            lax.all_to_all(first_part, "dp", split_axis=0, concat_axis=0, tiled=True),
            lax.all_to_all(second_part, "dp", split_axis=0, concat_axis=0, tiled=True),
        )

    def to_pieces(row_data, row_order):
        return row_data[row_order].reshape(dp_count, piece_rows, features)

    moved_x, moved_dy = relocate(to_pieces(tokens, deal_order), to_pieces(cotangent, deal_order))
    local_x = moved_x.reshape(tok_rows, features)[arrive_order]
    local_dy = moved_dy.reshape(tok_rows, features)[arrive_order]
    part_rows = w_query.shape[0]
    head_cols = w_query.shape[1]
    hidden_cols = w_up.shape[1]
    vectors = (
        norm1_gain,
        norm1_shift,
        b_query,
        b_value,
        b_out,
        norm2_gain,
        norm2_shift,
        b_down,
    )
    up_wide = b_up.shape[0] // part_rows
    vec_cols = jnp.concatenate(
        [jnp.stack(vectors, axis=1), b_up.reshape(part_rows, up_wide)], axis=1
    )
    vec_cols = jnp.pad(vec_cols, ((0, 0), (0, 128 - vec_cols.shape[1])))
    packed = jnp.concatenate(
        [w_query, w_key, w_value, w_out.T, w_up, w_down.T, vec_cols], axis=1
    )
    packed_all = lax.all_gather(packed, "dp", axis=0, tiled=True)
    edges = [0, head_cols, 2 * head_cols, 3 * head_cols, 4 * head_cols]
    edges += [4 * head_cols + hidden_cols, 4 * head_cols + 2 * hidden_cols]
    query_cols, key_cols, value_cols, out_cols, up_cols, down_cols = (
        packed_all[:, edges[i] : edges[i + 1]] for i in range(6)
    )
    out_rows = out_cols.T
    down_rows = down_cols.T
    vec_all = packed_all[:, edges[6] :]
    (
        gain_one,
        shift_one,
        bias_query,
        bias_value,
        bias_out,
        gain_two,
        shift_two,
        bias_down,
    ) = (vec_all[:, i] for i in range(8))
    bias_up = vec_all[:, 8 : 8 + up_wide].reshape(-1)
    gain_one = gain_one.astype(jnp.float32)
    shift_one = shift_one.astype(jnp.float32)
    gain_two = gain_two.astype(jnp.float32)
    shift_two = shift_two.astype(jnp.float32)
    local_heads = head_cols // HEAD_DIM
    score_scale = HEAD_DIM ** (-0.5)
    query_bias = take_block(bias_query, tensor_rank, head_cols)
    value_bias = take_block(bias_value, tensor_rank, head_cols)
    up_bias = take_block(bias_up, tensor_rank, hidden_cols)
    x_rows = local_x.astype(jnp.float32)
    first_in = layer_norm(x_rows, gain_one, shift_one).astype(jnp.bfloat16)
    group_one = lax.all_gather(first_in, "tensor", axis=0, tiled=True)
    queries = (
        jnp.dot(group_one, query_cols, preferred_element_type=jnp.float32) + query_bias
    ).astype(jnp.bfloat16)
    queries = queries.reshape(group_rows, local_heads, HEAD_DIM)
    keyset = jnp.dot(group_one, key_cols, preferred_element_type=jnp.float32).astype(jnp.bfloat16)
    keyset = keyset.reshape(group_rows, local_heads, HEAD_DIM)
    valset = (
        jnp.dot(group_one, value_cols, preferred_element_type=jnp.float32) + value_bias
    ).astype(jnp.bfloat16)
    valset = valset.reshape(group_rows, local_heads, HEAD_DIM)
    head_ids = tensor_rank * local_heads + lax.iota(jnp.int32, local_heads)
    slopes = jnp.exp2(-8.0 * (head_ids.astype(jnp.float32) + 1.0) / HEADS)
    seq_ids, positions, row_ids = sequence_marks(lengths[0], group_rows)
    qblock = min(512, group_rows)
    blocks = group_rows // qblock
    block_starts = lax.iota(jnp.int32, blocks) * qblock

    def block_scores(row_start):
        query_rows = lax.dynamic_slice_in_dim(queries, row_start, qblock, 0)
        raw_scores = (
            jnp.einsum("qhd,khd->hqk", query_rows, keyset, preferred_element_type=jnp.float32)
            * score_scale
        )
        seq_rows = lax.dynamic_slice_in_dim(seq_ids, row_start, qblock, 0)
        pos_rows = lax.dynamic_slice_in_dim(positions, row_start, qblock, 0)
        row_rows = lax.dynamic_slice_in_dim(row_ids, row_start, qblock, 0)
        distance = (pos_rows[:, None] - positions[None, :]).astype(jnp.float32)
        allowed = (seq_rows[:, None] == seq_ids[None, :]) & (row_rows[:, None] >= row_ids[None, :])
        scores = jnp.where(
            allowed[None], raw_scores - slopes[:, None, None] * distance[None], -1e30
        )
        return (query_rows, scores)

    def attend(row_start):
        query_rows, scores = block_scores(row_start)
        row_max = jnp.max(scores, axis=-1, keepdims=True)
        exponent = jnp.exp(scores - row_max)
        row_total = jnp.sum(exponent, axis=-1, keepdims=True)
        attn_probs = (exponent / row_total).astype(jnp.bfloat16)
        mixed = jnp.einsum("hqk,khd->qhd", attn_probs, valset, preferred_element_type=jnp.float32)
        return (mixed, row_max[..., 0] + jnp.log(row_total[..., 0]))

    mixed_all, log_totals = lax.map(attend, block_starts)
    heads_out = mixed_all.reshape(group_rows, head_cols).astype(jnp.bfloat16)
    attn_out = lax.psum_scatter(
        jnp.dot(heads_out, out_rows, preferred_element_type=jnp.float32).astype(jnp.bfloat16),
        "tensor",
        scatter_dimension=0,
        tiled=True,
    ).astype(jnp.float32) + bias_out.astype(jnp.float32)
    residual = x_rows + attn_out
    second_in = layer_norm(residual, gain_two, shift_two).astype(jnp.bfloat16)
    grad_in = local_dy.astype(jnp.float32)
    down_bias_term = jnp.sum(grad_in, axis=0)
    group_two = lax.all_gather(second_in, "tensor", axis=0, tiled=True)
    pre_act = jnp.dot(group_two, up_cols, preferred_element_type=jnp.float32) + up_bias
    activated = gelu_tanh(pre_act).astype(jnp.bfloat16)
    mlp_out = lax.psum_scatter(
        jnp.dot(activated, down_rows, preferred_element_type=jnp.float32).astype(jnp.bfloat16),
        "tensor",
        scatter_dimension=0,
        tiled=True,
    ).astype(jnp.float32)
    result = residual + mlp_out + bias_down.astype(jnp.float32)
    group_dy = lax.all_gather(local_dy, "tensor", axis=0, tiled=True)
    grad_down = contract_rows(activated, group_dy)
    grad_act = contract_cols(group_dy, down_rows)
    gelu_pull = jax.vjp(gelu_tanh, pre_act)[1]
    grad_pre = gelu_pull(grad_act)[0].astype(jnp.bfloat16)
    grad_up = contract_rows(group_two, grad_pre)
    up_bias_term = place_block(FF, jnp.sum(grad_pre, axis=0, dtype=jnp.float32), tensor_rank)
    grad_two = lax.psum_scatter(
        contract_cols(grad_pre, up_cols).astype(jnp.bfloat16),
        "tensor",
        scatter_dimension=0,
        tiled=True,
    ).astype(jnp.float32)
    result_low = result.astype(jnp.bfloat16)
    norm_two_pull = jax.vjp(layer_norm, residual, gain_two, shift_two)[1]
    grad_res_norm, gain_two_term, shift_two_term = norm_two_pull(grad_two)
    grad_resid = grad_in + grad_res_norm
    grad_attn = grad_resid.astype(jnp.bfloat16)
    out_bias_term = jnp.sum(grad_attn, axis=0, dtype=jnp.float32)
    group_grad = lax.all_gather(grad_attn, "tensor", axis=0, tiled=True)
    grad_out = contract_rows(heads_out, group_grad)
    grad_heads = (
        contract_cols(group_grad, out_rows)
        .astype(jnp.bfloat16)
        .reshape(group_rows, local_heads, HEAD_DIM)
    )

    def attend_back(running, block_item):
        key_accum, value_accum = running
        row_start, log_total = block_item
        query_rows, scores = block_scores(row_start)
        attn_probs = jnp.exp(scores - log_total[..., None])
        grad_rows = lax.dynamic_slice_in_dim(grad_heads, row_start, qblock, 0)
        grad_probs = jnp.einsum(
            "qhd,khd->hqk", grad_rows, valset, preferred_element_type=jnp.float32
        )
        row_dot = jnp.sum(attn_probs * grad_probs, axis=-1, keepdims=True)
        grad_scores = (attn_probs * (grad_probs - row_dot)).astype(jnp.bfloat16)
        grad_query_rows = jnp.einsum(
            "hqk,khd->qhd", grad_scores, keyset, preferred_element_type=jnp.float32
        )
        grad_query_rows = (grad_query_rows * score_scale).astype(jnp.bfloat16)
        key_accum = (
            key_accum
            + jnp.einsum(
                "hqk,qhd->khd", grad_scores, query_rows, preferred_element_type=jnp.float32
            )
            * score_scale
        )
        value_accum = value_accum + jnp.einsum(
            "hqk,qhd->khd",
            attn_probs.astype(jnp.bfloat16),
            grad_rows,
            preferred_element_type=jnp.float32,
        )
        return ((key_accum, value_accum), grad_query_rows)

    zero_heads = jnp.zeros((group_rows, local_heads, HEAD_DIM), jnp.float32)
    (key_accum, value_accum), grad_query_blocks = lax.scan(
        attend_back, (zero_heads, zero_heads), (block_starts, log_totals)
    )
    grad_query = grad_query_blocks.reshape(group_rows, head_cols)
    grad_key = key_accum.reshape(group_rows, head_cols).astype(jnp.bfloat16)
    grad_value = value_accum.reshape(group_rows, head_cols).astype(jnp.bfloat16)
    query_bias_term = place_block(D, jnp.sum(grad_query, axis=0, dtype=jnp.float32), tensor_rank)
    value_bias_term = place_block(D, jnp.sum(grad_value, axis=0, dtype=jnp.float32), tensor_rank)
    grad_wquery = contract_rows(group_one, grad_query)
    grad_wkey = contract_rows(group_one, grad_key)
    grad_wvalue = contract_rows(group_one, grad_value)
    grad_one = lax.psum_scatter(
        (
            contract_cols(grad_query, query_cols)
            + contract_cols(grad_key, key_cols)
            + contract_cols(grad_value, value_cols)
        ).astype(jnp.bfloat16),
        "tensor",
        scatter_dimension=0,
        tiled=True,
    ).astype(jnp.float32)
    norm_one_pull = jax.vjp(layer_norm, x_rows, gain_one, shift_one)[1]
    grad_x_norm, gain_one_term, shift_one_term = norm_one_pull(grad_one)
    grad_tokens = (grad_resid + grad_x_norm).astype(jnp.bfloat16)
    small_terms = jnp.stack(
        (
            gain_one_term,
            shift_one_term,
            query_bias_term,
            value_bias_term,
            out_bias_term,
            gain_two_term,
            shift_two_term,
            down_bias_term,
        ),
        axis=1,
    )
    small_terms = jnp.concatenate([small_terms, up_bias_term.reshape(-1, up_wide)], axis=1)
    small_terms = jnp.pad(small_terms, ((0, 0), (0, 128 - small_terms.shape[1])))
    terms = (grad_wquery, grad_wkey, grad_wvalue, grad_out.T, grad_up, grad_down.T, small_terms)
    packed_grads = jnp.concatenate([term.astype(jnp.bfloat16) for term in terms], axis=1)
    reduced = lax.psum_scatter(packed_grads, "dp", scatter_dimension=0, tiled=True).astype(
        jnp.float32
    )
    shards = [reduced[:, edges[i] : edges[i + 1]] for i in range(6)]
    shards[3] = shards[3].T
    shards[5] = shards[5].T
    sums = lax.psum(reduced[:, edges[6] : edges[6] + 8 + up_wide], "tensor")
    smalls = [sums[:, i] for i in range(7)] + [sums[:, 8:].reshape(-1), sums[:, 7]]
    back_y, back_dx = relocate(
        to_pieces(result_low, return_order), to_pieces(grad_tokens, return_order)
    )
    given_y = back_y.reshape(tok_rows, features)[sending_rank]
    given_dx = back_dx.reshape(tok_rows, features)[sending_rank]
    return (
        given_y,
        given_dx,
        smalls[0],
        smalls[1],
        shards[0],
        smalls[2],
        shards[1],
        shards[2],
        smalls[3],
        shards[3],
        smalls[4],
        smalls[5],
        smalls[6],
        shards[4],
        smalls[7],
        shards[5],
        smalls[8],
    )


MESH = pl.DeviceIdType.MESH
F32 = jnp.float32
LOW = jnp.bfloat16
RING = 8
PAIR = 128


def dot_nn(first_op, second_op):
    return lax.dot_general(
        first_op, second_op, (((1,), (0,)), ((), ())), preferred_element_type=F32
    )


def dot_nt(first_op, second_op):
    return lax.dot_general(
        first_op, second_op, (((1,), (1,)), ((), ())), preferred_element_type=F32
    )


def loop(count, step):
    def run(i, carry):
        step(i)
        return carry

    lax.fori_loop(0, count, run, 0)


def at(index, size):
    return pl.ds(pl.multiple_of(index * size, size), size)


def fused_kernel(
    tok_ref,
    cot_ref,
    wq_ref,
    wk_ref,
    wv_ref,
    wot_ref,
    wup_ref,
    wdt_ref,
    *refs,
):
    vectors, refs = refs[:9], refs[9:]
    rank_ref, arrive_ref, len_ref = refs[:3]
    homes, refs = refs[3:12], refs[12:]
    fused_layer(
        (tok_ref, cot_ref, wq_ref, wk_ref, wv_ref, wot_ref, wup_ref, wdt_ref),
        vectors,
        rank_ref,
        arrive_ref,
        len_ref,
        homes,
        *refs,
    )


def fused_layer(
    given,
    vectors,
    rank_ref,
    arrive_ref,
    len_ref,
    homes,
    gq_out,
    gk_out,
    gv_out,
    go_out,
    gu_out,
    gd_out,
    small_out,
    wqkv,
    wo,
    wu,
    wd,
    ga,
    gb,
    go,
    gu,
    gd,
    land,
    tok_v,
    cot_v,
    pcx,
    pcd,
    arrx,
    arrd,
    backy,
    backd,
    xg,
    dyg,
    a1,
    qkv,
    qkvt,
    ho,
    lse,
    po,
    por,
    res,
    yb,
    a2,
    act,
    dpre,
    pm,
    pmr,
    pd,
    pdr,
    dattn,
    dh,
    dht,
    dk_acc,
    dv_acc,
    tbuf,
    vgat,
    vrow,
    bqkv,
    bup,
    gvec,
    gbup,
    svec,
    svr,
    sown,
    sown_r,
    start_row,
    ld,
    st,
    ag_s,
    ag_r,
    mt_s,
    mt_r,
    aa_s,
    aa_r,
    y_s,
    y_r,
    rm_s,
    rm_r,
    rr_s,
    rr_r,
    ready_one,
    ready_two,
):
    tok_ref, cot_ref, wq_ref, wk_ref, wv_ref, wot_ref, wup_ref, wdt_ref = given
    d = lax.axis_index("dp")
    t = lax.axis_index("tensor")
    other = 1 - t
    core = lax.rem(d, 2)
    chip = lax.div(d, 2)
    xc = lax.rem(chip, 2)
    zc = lax.div(chip, 2)
    p = zc + xc * (7 - 2 * zc)

    def chip_at(pos):
        pos = lax.rem(pos + 2 * RING, RING)
        xx = lax.div(pos, 4)
        zz = pos + xx * (7 - 2 * pos)
        return zz * 2 + xx

    def dev(pos):
        return chip_at(pos) * 2 + core

    def mdev(pos):
        return chip_at(pos) * 2 + 1 - core

    mate = d + 1 - 2 * core
    sides = (dev(p + 1), dev(p - 1))
    weights = (wqkv, wo, wu, wd)
    grads = (ga, go, gu, gd, gb)
    widths = (768, 512, 2048, 2048, 768)
    landing = (wd, wd, wu, land, wd)
    offsets = (0, 1536, 0, 0, 768)
    dqkv = act

    def remote(src, dst, send, recv, device):
        return pltpu.make_async_remote_copy(
            src_ref=src,
            dst_ref=dst,
            send_sem=send,
            recv_sem=recv,
            device_id=device,
            device_id_type=MESH,
        )

    def signal(sem, device):
        pl.semaphore_signal(sem, inc=1, device_id=device, device_id_type=MESH)

    loads = [
        pltpu.make_async_copy(tok_ref, tok_v, ld.at[0]),
        pltpu.make_async_copy(cot_ref, cot_v, ld.at[1]),
        pltpu.make_async_copy(wq_ref, wqkv.at[d, :, pl.ds(0, 512)], ld.at[2]),
        pltpu.make_async_copy(wk_ref, wqkv.at[d, :, pl.ds(512, 512)], ld.at[3]),
        pltpu.make_async_copy(wv_ref, wqkv.at[d, :, pl.ds(1024, 512)], ld.at[4]),
        pltpu.make_async_copy(wot_ref, wo.at[d], ld.at[5]),
        pltpu.make_async_copy(wup_ref, wu.at[d], ld.at[6]),
        pltpu.make_async_copy(wdt_ref, wd.at[d], ld.at[7]),
    ]
    for load in loads:
        load.start()
    barrier = pltpu.get_barrier_semaphore()

    def store(i, src):
        return pltpu.make_async_copy(src, homes[i], st.at[i])

    def greet(k):
        signal(barrier, {"dp": lax.rem(d + k + 1, 16)})

    loop(15, greet)
    signal(barrier, {"tensor": other})

    def rows_copy(kind, src, dst, k, receive):
        if receive:
            spot = lax.rem(d + 16 - k, 16)
            return remote(
                src.at[at(spot, 16)],
                dst.at[at(spot, 16)],
                aa_s.at[kind, k],
                aa_r.at[kind, k],
                {"dp": spot},
            )
        spot = lax.rem(d + k, 16)
        return remote(
            src.at[at(spot, 16)],
            dst.at[at(d, 16)],
            aa_s.at[kind, k],
            aa_r.at[kind, k],
            {"dp": spot},
        )

    def rows_send(kind, src, dst):
        loop(15, lambda k: rows_copy(kind, src, dst, k + 1, False).start())
        dst[at(d, 16), :] = src[at(d, 16), :]

    def rows_wait(kind, src, dst):
        loop(15, lambda k: rows_copy(kind, src, dst, k + 1, True).wait_recv())

    def rows_drain(kind, src, dst):
        loop(15, lambda k: rows_copy(kind, src, dst, k + 1, False).wait_send())

    def tile_copy(kind, src_of, dst, k, receive):
        spot = lax.rem(d + 16 - k, 16) if receive else lax.rem(d + k, 16)
        return remote(
            src_of(spot),
            dst.at[spot if receive else d],
            aa_s.at[kind, k],
            aa_r.at[kind, k],
            {"dp": spot},
        )

    def cross(i, src, dst):
        return remote(src, dst, y_s.at[i], y_r.at[i], {"tensor": other})

    def ring_part(ref, slot, way, step):
        if step == 3:
            return ref.at[slot, pl.ds(32 * way, 32)]
        return ref.at[slot]

    def turn(way, steps):
        return p - steps if way == 0 else p + steps

    def ag_copy(c, way, step):
        part = ring_part(weights[c], dev(turn(way, step)), way, step)
        return remote(
            part, part, ag_s.at[c, way, step], ag_r.at[c, way, step], {"dp": sides[way]}
        )

    def ag_arrival(c, way, step):
        part = ring_part(weights[c], dev(turn(way, step + 1)), way, step)
        return remote(
            part, part, ag_s.at[c, way, step], ag_r.at[c, way, step], {"dp": sides[way]}
        )

    def mate_copy(c, k, place):
        if k == 0:
            part = weights[c].at[place(p)]
        else:
            way, step = (k - 1) // 4, (k - 1) % 4
            part = ring_part(weights[c], place(turn(way, step + 1)), way, step)
        return remote(part, part, mt_s.at[c, k], mt_r.at[c, k], {"dp": mate})

    def ag_start(c):
        for way in range(2):
            ag_copy(c, way, 0).start()
        mate_copy(c, 0, dev).start()

    def ag_event(c, step):
        for way in range(2):
            ag_arrival(c, way, step).wait_recv()
            if step < 3:
                ag_copy(c, way, step + 1).start()
            mate_copy(c, 1 + 4 * way + step, dev).start()

    def ag_finish(c):
        for k in range(9):
            mate_copy(c, k, mdev).wait_recv()

    def ag_drain(c):
        for way in range(2):
            for step in range(4):
                ag_copy(c, way, step).wait_send()
        for k in range(9):
            mate_copy(c, k, dev).wait_send()

    def inbox(c, slot, rows=pl.ds(0, 64)):
        return landing[c].at[slot, rows, pl.ds(offsets[c], widths[c])]

    def arrived(c, slot, rows):
        return landing[c][slot, rows, offsets[c] : offsets[c] + widths[c]].astype(F32)

    def rm_copy(c, spot):
        return remote(
            grads[c].at[spot * 2 + 1 - core],
            inbox(c, spot),
            rm_s.at[c, spot],
            rm_r.at[c, spot],
            {"dp": mate},
        )

    def rs_copy(c, way, step):
        dest = dev(p + 4 - step if way == 0 else p - 4 + step)
        slot = 8 + way * 4 + step
        if step == 0:
            half = pl.ds(32 * way, 32)
            src, dst = grads[c].at[dest, half], inbox(c, slot, half)
        else:
            src, dst = grads[c].at[dest], inbox(c, slot)
        return remote(src, dst, rr_s.at[c, way, step], rr_r.at[c, way, step], {"dp": sides[way]})

    def rs_add(c, slot, rows, boxes):
        total = grads[c][slot, rows, :].astype(F32)
        for box in boxes:
            total += arrived(c, box, rows)
        return total

    def rs_start(c):
        far = chip_at(p + 4)
        rm_copy(c, far).wait_recv()
        slot = far * 2 + core

        def add(i):
            rows = at(i, 16)
            grads[c][slot, rows, :] = rs_add(c, slot, rows, (far,)).astype(LOW)

        loop(4, add)
        for way in range(2):
            rs_copy(c, way, 0).start()

    def rs_event(c, step):
        for way in range(2):
            pos = p + 3 - step if way == 0 else p - 3 + step
            spot = chip_at(pos)
            slot = spot * 2 + core
            box = 8 + way * 4 + step
            rs_copy(c, way, step).wait_recv()
            rm_copy(c, spot).wait_recv()

            def add(i, boxes):
                rows = at(i, 16)
                grads[c][slot, rows, :] = rs_add(c, slot, rows, boxes).astype(LOW)

            if step == 0:
                loop(2, lambda i: add(i + 2 * way, (spot, box)))
                loop(2, lambda i: add(i + 2 - 2 * way, (spot,)))
            else:
                loop(4, lambda i: add(i, (spot, box)))
            rs_copy(c, way, step + 1).start()

    def rs_finish(c, keep):
        for way in range(2):
            rs_copy(c, way, 3).wait_recv()
        rm_copy(c, chip).wait_recv()

        def add(i):
            rows = at(i, 16)
            keep(rows, rs_add(c, d, rows, (chip, 11, 15)))

        loop(4, add)

    def keep_in(ref):
        def keep(rows, total):
            ref[rows, :] = total

        return keep

    def keep_heads(first):
        def keep(rows, total):
            for j, ref in enumerate((gq_out, gk_out, gv_out)):
                ref[rows, first : first + 256] = total[:, 256 * j : 256 * j + 256]

        return keep

    def rs_drain(c):
        for way in range(2):
            for step in range(4):
                rs_copy(c, way, step).wait_send()
        loop(8, lambda i: rm_copy(c, i).wait_send())

    def free_for_reduction(sem):
        signal(sem, {"dp": mate})
        for side in sides:
            signal(sem, {"dp": side})

    def picks(ref):
        slots = lax.broadcasted_iota(jnp.int32, (256, 256), 0)
        return jnp.where(slots == ref[0, :, :], 1.0, 0.0)

    zeros = jnp.zeros((1, 64), F32)
    for i in range(8):
        row = vectors[i][...].astype(F32).reshape(1, 64)
        early = jnp.concatenate([row, zeros], axis=1)
        late = jnp.concatenate([zeros, row], axis=1)
        vgat[d, i : i + 1, :] = jnp.where(core == 0, early, late)
    row = vectors[8][...].astype(F32).reshape(1, 256)
    vgat[d, 8:9, :] = row[:, 0:128]
    vgat[d, 9:10, :] = row[:, 128:256]
    vgat[d, 10:16, :] = jnp.zeros((6, 128), F32)
    loads[0].wait()
    spread = picks(rank_ref).astype(LOW)
    pcx[...] = dot_nn(spread, tok_v[...]).astype(LOW)
    pl.semaphore_wait(barrier, 16)
    rows_send(0, pcx, arrx)
    loop(15, lambda k: tile_copy(4, lambda spot: vgat.at[d], vgat, k + 1, False).start())
    for i in range(2, 6):
        loads[i].wait()
    ag_start(0)
    ag_start(1)
    loads[1].wait()
    pcd[...] = dot_nn(spread, cot_v[...]).astype(LOW)
    for i in range(6, 8):
        loads[i].wait()

    own = at(t, 256)
    gather_rows = picks(arrive_ref).T.astype(LOW)
    rows_wait(0, pcx, arrx)
    xg[own, :] = dot_nn(gather_rows, arrx[...]).astype(LOW)
    cross(0, xg.at[own], xg.at[own]).start()
    ag_event(0, 0)
    ag_event(1, 0)

    loop(15, lambda k: tile_copy(4, lambda spot: vgat.at[d], vgat, k + 1, True).wait_recv())
    for m in range(8):
        both = vgat[2 * m, :, :] + vgat[2 * m + 1, :, :]
        vrow[:, 128 * m : 128 * (m + 1)] = both[0:8, :]
    for j in range(8):
        block = vgat[8 * t + j, :, :]
        bup[:, 256 * j : 256 * j + 128] = block[8:9, :]
        bup[:, 256 * j + 128 : 256 * j + 256] = block[9:10, :]
    bqkv[:, 0:512] = vrow[2:3, at(t, 512)]
    bqkv[:, 512:1024] = jnp.zeros((1, 512), F32)
    bqkv[:, 1024:1536] = vrow[3:4, at(t, 512)]
    ends = jnp.int32(0)
    row_ids = lax.broadcasted_iota(jnp.int32, (1, 512), 1)
    starts = jnp.zeros((1, 512), jnp.int32)
    for i in range(3):
        ends = ends + len_ref[0, i]
        starts = jnp.where(row_ids >= ends, ends, starts)
    start_row[...] = starts
    gvec[...] = jnp.zeros((8, 1024), F32)

    def stats(values):
        center = values - jnp.mean(values, axis=-1, keepdims=True)
        spread_of = jnp.mean(center * center, axis=-1, keepdims=True)
        scale = lax.rsqrt(spread_of + EPSILON)
        return center * scale, scale

    def norm_one(half):
        def step(i):
            rows = at(half * 8 + i, 32)
            normed, _ = stats(xg[rows, :].astype(F32))
            a1[rows, :] = (normed * vrow[0:1, :] + vrow[1:2, :]).astype(LOW)

        loop(8, step)

    norm_one(t)
    ag_event(0, 1)
    ag_event(1, 1)
    cross(0, xg.at[own], xg.at[at(other, 256)]).wait_recv()
    norm_one(other)
    ag_event(0, 2)
    ag_event(1, 2)
    ag_start(2)
    rows_send(1, pcd, arrd)
    ag_event(0, 3)
    ag_event(1, 3)
    ag_finish(0)

    def project(i):
        cols = at(i, 256)
        value = dot_nn(a1[...], wqkv[:, :, cols].reshape(1024, 256)) + bqkv[:, cols]
        low = value.astype(LOW).astype(F32)
        qkv[:, cols] = low.astype(LOW)
        qkvt[cols, :] = low.T.astype(LOW)

    loop(6, project)
    ag_event(2, 0)
    ag_start(3)

    def slope_of(pair, half):
        head = (t * 8 + pair * 2 + half + 1).astype(F32)
        return jnp.exp2(jnp.full((1, PAIR), -0.5, F32) * head)

    def padded(block, half):
        zero = jnp.zeros_like(block)
        return jnp.concatenate([block, zero] if half == 0 else [zero, block], axis=0)

    def band(qb):
        first = max(0, qb - 2) * 128
        width = (qb + 1) * 128 - first
        keys = lax.broadcasted_iota(jnp.int32, (width, PAIR), 0) + first
        rows = lax.broadcasted_iota(jnp.int32, (width, PAIR), 1) + qb * 128
        allowed = (keys <= rows) & (keys >= start_row[:, qb * 128 : qb * 128 + 128])
        return first, width, allowed, (rows - keys).astype(F32)

    def score(pair, half, qb, first, width, allowed, distance):
        key_rows = qkv[first : first + width, at(pair + 4, PAIR)]
        query = qkvt[at(pair * 2 + half, 64), qb * 128 : qb * 128 + 128] * 0.125
        raw = dot_nn(key_rows, padded(query, half))
        return jnp.where(allowed, raw - slope_of(pair, half) * distance, -1e30)

    def attend(qbs):
        def step(pair):
            for qb in qbs:
                first, width, allowed, distance = band(qb)
                parts = []
                for half in range(2):
                    s = score(pair, half, qb, first, width, allowed, distance)
                    top = jnp.max(s, axis=0, keepdims=True)
                    e = jnp.exp(s - top)
                    total = jnp.sum(e, axis=0, keepdims=True)
                    probs = (e * (1.0 / total)).astype(LOW)
                    lse[pair * 2 + half, :, qb * 128 : qb * 128 + 128] = top + jnp.log(total)
                    value_t = qkvt[at(16 + pair * 2 + half, 64), first : first + width]
                    parts.append(dot_nn(value_t, probs))
                ho[qb * 128 : qb * 128 + 128, at(pair, PAIR)] = (
                    jnp.concatenate(parts, axis=0).T.astype(LOW)
                )

        loop(4, step)

    def out_project(rb):
        rows = slice(rb * 256, rb * 256 + 256)

        def step(i):
            po[rows, at(i, 256)] = dot_nt(ho[rows, :], wo[pl.ds(i * 4, 4)].reshape(256, 512)).astype(LOW)

        loop(4, step)
        cross(2 + rb, po.at[rows], por.at[rows]).start()

    attend((0, 1))
    ag_finish(1)
    out_project(0)
    ag_event(2, 1)
    attend((2, 3))
    out_project(1)
    ag_event(3, 0)
    ag_event(2, 2)
    rows_wait(1, pcd, arrd)
    dyg[own, :] = dot_nn(gather_rows, arrd[...]).astype(LOW)
    cross(1, dyg.at[own], dyg.at[own]).start()
    ag_event(3, 1)
    ag_event(2, 3)
    ag_finish(2)

    def mlp_up(rb):
        rows = slice(rb * 256, rb * 256 + 256)
        cross(2 + rb, po.at[rows], por.at[rows]).wait_recv()

        def enter(i):
            part = at(rb * 8 + i, 32)
            value = xg[part, :].astype(F32) + (po[part, :].astype(F32) + por[part, :].astype(F32))
            value = value + vrow[4:5, :]
            res[part, :] = value
            normed, _ = stats(value)
            a2[part, :] = (normed * vrow[5:6, :] + vrow[6:7, :]).astype(LOW)

        loop(8, enter)

        def up(i):
            cols = at(i, 256)
            v = dot_nn(a2[rows, :], wu[:, :, cols].reshape(1024, 256)) + bup[:, cols]
            square = v * v
            bend = jnp.tanh(GELU_SCALE * (v + 0.044715 * (square * v)))
            act[rows, cols] = (0.5 * v * (1.0 + bend)).astype(LOW)
            slope = 0.5 * (1.0 + bend) + 0.5 * v * (1.0 - bend * bend) * (
                GELU_SCALE * (1.0 + 3.0 * 0.044715 * square)
            )
            dpre[rows, cols] = slope.astype(LOW)

        loop(8, up)

    def act_back(i):
        cols = at(i, 256)
        grad = dot_nn(dyg[...], wd[:, :, cols].reshape(1024, 256))
        back = (grad * dpre[:, cols].astype(F32)).astype(LOW)
        dpre[:, cols] = back
        gbup[:, cols] = jnp.sum(back.astype(F32), axis=0, keepdims=True)

    def mlp_back(rb):
        rows = slice(rb * 256, rb * 256 + 256)

        def down(i):
            pd[rows, at(i, 256)] = dot_nt(dpre[rows, :], wu[pl.ds(i * 4, 4)].reshape(256, 2048)).astype(LOW)

        loop(4, down)
        cross(5 + rb, pd.at[rows], pdr.at[rows]).start()

    def mlp_out(i):
        pm[:, at(i, 256)] = dot_nt(act[...], wd[pl.ds(i * 4, 4)].reshape(256, 2048)).astype(LOW)

    def flip(ref):
        def step(i):
            tbuf[at(i, 256), :] = ref[:, at(i, 256)].T

        loop(4, step)

    def plain(ref):
        return lambda j: ref[:, at(j, 512)]

    def weight_grad(c, second, count, wide):
        def step(i):
            rows = at(i, 256)

            def inner(j):
                grads[c][pl.ds(i * 4, 4), :, at(j, wide)] = (
                    dot_nn(tbuf[rows, :], second(j)).astype(LOW).reshape(4, 64, wide)
                )

            loop(count, inner)
            rm_copy(c, i * 2).start()
            rm_copy(c, i * 2 + 1).start()

        loop(4, step)

    mlp_up(0)
    ag_event(3, 2)
    mlp_up(1)
    yb[...] = res[own, :]
    ag_event(3, 3)
    ag_finish(3)
    cross(1, dyg.at[own], dyg.at[at(other, 256)]).wait_recv()
    loop(8, act_back)
    mlp_back(0)
    mlp_back(1)
    ag_drain(2)
    free_for_reduction(ready_one)
    flip(dyg)
    weight_grad(3, plain(act), 4, 512)
    rs_start(3)
    loop(4, mlp_out)
    ag_drain(3)
    free_for_reduction(ready_two)
    rs_event(3, 0)
    pl.semaphore_wait(ready_one, 3)
    flip(a2)
    weight_grad(2, plain(dpre), 4, 512)
    rs_start(2)
    rs_event(3, 1)

    def norm_two_back(rb):
        rows = slice(rb * 256, rb * 256 + 256)
        cross(5 + rb, pd.at[rows], pdr.at[rows]).wait_recv()

        def step(i):
            part = at(rb * 8 + i, 32)
            grad = pd[part, :].astype(F32) + pdr[part, :].astype(F32)
            normed, scale = stats(res[part, :])
            e = grad * vrow[5:6, :]
            inner = e - jnp.mean(e, axis=-1, keepdims=True)
            inner = inner - normed * jnp.mean(e * normed, axis=-1, keepdims=True)
            dy = dyg[part, :].astype(F32)
            full = dy + inner * scale
            res[part, :] = full
            low = full.astype(LOW)
            dattn[part, :] = low
            gvec[4:5, :] += 0.5 * jnp.sum(low.astype(F32), axis=0, keepdims=True)
            gvec[5:6, :] += 0.5 * jnp.sum(grad * normed, axis=0, keepdims=True)
            gvec[6:7, :] += 0.5 * jnp.sum(grad, axis=0, keepdims=True)
            gvec[7:8, :] += 0.5 * jnp.sum(dy, axis=0, keepdims=True)

        loop(8, step)

        def heads(i):
            cols = at(i, 256)
            value = dot_nn(dattn[rows, :], wo[:, :, cols].reshape(1024, 256)).astype(LOW)
            dh[rows, cols] = value
            dht[cols, rows] = value.astype(F32).T.astype(LOW)

        loop(2, heads)

    lanes = lax.broadcasted_iota(jnp.int32, (1, PAIR), 1) < 64

    def attend_back(qbs, first_pair, count):
        def step(index):
            pair = index + first_pair
            for qb in qbs:
                first, width, allowed, distance = band(qb)
                queries = slice(qb * 128, qb * 128 + 128)
                span = slice(first, first + width)
                values = qkv[span, at(pair + 8, PAIR)]
                query_rows = qkv[queries, at(pair, PAIR)]
                grad_rows = dh[queries, at(pair, PAIR)]
                parts, keys_part, values_part = [], [], []
                for half in range(2):
                    s = score(pair, half, qb, first, width, allowed, distance)
                    probs = jnp.exp(s - lse[pair * 2 + half, :, queries])
                    grad_t = dht[at(pair * 2 + half, 64), queries]
                    grad_p = dot_nn(values, padded(grad_t, half))
                    row_dot = jnp.sum(probs * grad_p, axis=0, keepdims=True)
                    grad_s = (probs * (grad_p - row_dot)).astype(LOW)
                    key_t = qkvt[at(8 + pair * 2 + half, 64), span]
                    parts.append(dot_nn(key_t, grad_s))
                    keys_part.append(dot_nn(grad_s, query_rows))
                    values_part.append(dot_nn(probs.astype(LOW), grad_rows))
                dqkv[queries, at(pair, PAIR)] = (
                    (jnp.concatenate(parts, axis=0) * 0.125).T.astype(LOW)
                )
                dk_acc[span, at(pair, PAIR)] += jnp.where(lanes, keys_part[0], keys_part[1])
                dv_acc[span, at(pair, PAIR)] += jnp.where(lanes, values_part[0], values_part[1])
            if 3 in qbs:
                dqkv[:, at(pair + 4, PAIR)] = (dk_acc[:, at(pair, PAIR)] * 0.125).astype(LOW)
                dqkv[:, at(pair + 8, PAIR)] = dv_acc[:, at(pair, PAIR)].astype(LOW)

        loop(count, step)

    def heads_part(h):
        return lambda j: dqkv[:, pl.ds(pl.multiple_of(j * 512 + h * 256, 256), 256)]

    norm_two_back(0)
    cross(4, pm.at[at(other, 256)], pmr).start()
    rs_event(2, 0)
    dk_acc[...] = jnp.zeros((512, 512), F32)
    dv_acc[...] = jnp.zeros((512, 512), F32)
    attend_back((0, 1), 0, 4)
    rs_event(3, 2)
    norm_two_back(1)
    pl.semaphore_wait(ready_two, 3)
    flip(dattn)
    weight_grad(1, plain(ho), 1, 512)
    rs_start(1)
    rs_event(2, 1)
    attend_back((2, 3), 0, 2)
    flip(a1)
    weight_grad(0, heads_part(0), 3, 256)
    rs_start(0)
    rs_event(2, 2)

    rows_drain(0, pcx, arrx)
    rows_drain(1, pcd, arrd)
    send_back = picks(arrive_ref).astype(LOW)
    take_back = picks(rank_ref).T.astype(LOW)
    cross(4, pm.at[at(other, 256)], pmr).wait_recv()

    def finish_y(i):
        part = at(i, 32)
        mine = at(t * 8 + i, 32)
        value = yb[part, :] + (pm[mine, :].astype(F32) + pmr[part, :].astype(F32)) + vrow[7:8, :]
        tok_v[part, :] = value.astype(LOW)

    loop(8, finish_y)
    pcx[...] = dot_nn(send_back, tok_v[...]).astype(LOW)
    rows_send(2, pcx, backy)

    attend_back((2, 3), 2, 2)

    def attn_in_back(i):
        po[:, at(i, 256)] = dot_nt(
            dqkv[:, 0:1536], wqkv[pl.ds(i * 4, 4)].reshape(256, 1536)
        ).astype(LOW)

    for rb in range(2):
        rows = slice(rb * 256, rb * 256 + 256)
        cross(2 + rb, po.at[rows], por.at[rows]).wait_send()
    loop(4, attn_in_back)
    cross(7, po.at[at(other, 256)], por.at[pl.ds(0, 256)]).start()
    weight_grad(4, heads_part(1), 3, 256)
    rs_start(4)
    rs_event(1, 0)
    rs_event(0, 0)
    rs_finish(3, keep_in(gd_out))
    store(7, gd_out).start()
    sums = jnp.zeros((1, 1536), F32)
    for i in range(4):
        sums = sums + jnp.sum(
            dqkv[i * 128 : i * 128 + 128, 0:1536].astype(F32), axis=0, keepdims=True
        )
    gvec[2:3, at(t, 512)] = sums[:, 0:512]
    gvec[3:4, at(t, 512)] = sums[:, 1024:1536]
    rs_event(4, 0)
    rs_event(1, 1)
    rs_event(0, 1)
    cross(7, po.at[at(other, 256)], por.at[pl.ds(0, 256)]).wait_recv()

    def norm_one_back(i):
        part = at(i, 32)
        mine = at(t * 8 + i, 32)
        grad = po[mine, :].astype(F32) + por[part, :].astype(F32)
        normed, scale = stats(xg[mine, :].astype(F32))
        e = grad * vrow[0:1, :]
        inner = e - jnp.mean(e, axis=-1, keepdims=True)
        inner = inner - normed * jnp.mean(e * normed, axis=-1, keepdims=True)
        cot_v[part, :] = (res[mine, :] + inner * scale).astype(LOW)
        gvec[0:1, :] += jnp.sum(grad * normed, axis=0, keepdims=True)
        gvec[1:2, :] += jnp.sum(grad, axis=0, keepdims=True)

    loop(8, norm_one_back)
    a2[0:256, :] = dot_nn(send_back, cot_v[...]).astype(LOW)
    rows_send(3, a2, backd)

    for e in range(16):
        svec[e, 0:8, :] = gvec[:, 128 * (e // 2) : 128 * (e // 2) + 128]
        svec[e, 8:16, :] = jnp.zeros((8, 128), F32)
    for j in range(8):
        svec[8 * t + j, 8:9, :] = gbup[:, 256 * j : 256 * j + 128]
        svec[8 * t + j, 9:10, :] = gbup[:, 256 * j + 128 : 256 * j + 256]
    loop(15, lambda k: tile_copy(5, lambda spot: svec.at[spot], svr, k + 1, False).start())
    svr[d] = svec[d]
    rs_event(4, 1)
    rs_event(1, 2)
    rs_event(0, 2)
    rs_finish(2, keep_in(gu_out))
    store(6, gu_out).start()
    rows_wait(2, pcx, backy)
    tok_v[...] = dot_nn(take_back, backy[...]).astype(LOW)
    store(0, tok_v).start()
    rs_event(4, 2)
    loop(15, lambda k: tile_copy(5, lambda spot: svec.at[spot], svr, k + 1, True).wait_recv())
    small = jnp.zeros((16, 128), F32)
    for e in range(16):
        small = small + svr[e]
    sown[...] = small
    cross(8, sown, sown_r).start()
    rs_finish(1, keep_in(go_out))
    store(5, go_out).start()
    rs_finish(0, keep_heads(0))
    rows_wait(3, a2, backd)
    cot_v[...] = dot_nn(take_back, backd[...]).astype(LOW)
    store(1, cot_v).start()
    cross(8, sown, sown_r).wait_recv()
    small_out[...] = sown[...] + sown_r[...]
    store(8, small_out).start()
    rs_finish(4, keep_heads(256))
    for i, ref in enumerate((gq_out, gk_out, gv_out)):
        store(2 + i, ref).start()
    ag_drain(0)
    ag_drain(1)

    for c in range(5):
        rs_drain(c)
    rows_drain(2, pcx, backy)
    rows_drain(3, a2, backd)
    loop(15, lambda k: tile_copy(4, lambda spot: vgat.at[d], vgat, k + 1, False).wait_send())
    loop(15, lambda k: tile_copy(5, lambda spot: svec.at[spot], svr, k + 1, False).wait_send())
    cross(0, xg.at[own], xg.at[own]).wait_send()
    cross(1, dyg.at[own], dyg.at[own]).wait_send()
    cross(4, pm.at[at(other, 256)], pmr).wait_send()
    for rb in range(2):
        rows = slice(rb * 256, rb * 256 + 256)
        cross(5 + rb, pd.at[rows], pdr.at[rows]).wait_send()
    cross(7, po.at[at(other, 256)], por.at[pl.ds(0, 256)]).wait_send()
    cross(8, sown, sown_r).wait_send()
    stored = (tok_v, cot_v, gq_out, gk_out, gv_out, go_out, gu_out, gd_out, small_out)
    for i, ref in enumerate(stored):
        store(i, ref).wait()


def settle_kernel(*refs):
    sources, small, homes, short = refs[:8], refs[8], refs[9:17], refs[17:26]
    held, in_sem, out_sem = refs[26:34], refs[34], refs[35]
    ins = [pltpu.make_async_copy(sources[i], held[i], in_sem.at[i]) for i in range(8)]
    outs = [pltpu.make_async_copy(held[i], homes[i], out_sem.at[i]) for i in range(8)]
    for copy in ins:
        copy.start()
    core = lax.rem(lax.axis_index("dp"), 2)
    for i in range(8):
        row = small[i : i + 1, :]
        short[i][...] = jnp.where(core == 0, row[:, 0:64], row[:, 64:128]).reshape(64)
    short[8][0:128] = small[8:9, :].reshape(128)
    short[8][128:256] = small[9:10, :].reshape(128)
    for i in range(8):
        ins[i].wait()
        outs[i].start()
    for copy in outs:
        copy.wait()


def fused_body(
    tokens,
    cotangent,
    norm1_gain,
    norm1_shift,
    w_query,
    b_query,
    w_key,
    w_value,
    b_value,
    w_out,
    b_out,
    norm2_gain,
    norm2_shift,
    w_up,
    b_up,
    w_down,
    b_down,
    lengths,
    deal_rank,
    arrival,
):
    def vm(*shape, dtype=LOW):
        return pltpu.VMEM(shape, dtype)

    def dma(*shape):
        return pltpu.SemaphoreType.DMA(shape)

    scratch = [
        vm(64, 512, dtype=F32),
        vm(64, 512, dtype=F32),
        vm(64, 512, dtype=F32),
        vm(64, 512, dtype=F32),
        vm(64, 2048, dtype=F32),
        vm(64, 2048, dtype=F32),
        vm(16, 128, dtype=F32),
        vm(16, 64, 1536),
        vm(16, 64, 512),
        vm(16, 64, 2048),
        vm(16, 64, 2048),
        vm(16, 64, 768),
        vm(16, 64, 768),
        vm(16, 64, 512),
        vm(16, 64, 2048),
        vm(16, 64, 2048),
        vm(16, 64, 2048),
        vm(256, 1024),
        vm(256, 1024),
        vm(256, 1024),
        vm(256, 1024),
        vm(256, 1024),
        vm(256, 1024),
        vm(256, 1024),
        vm(256, 1024),
        vm(512, 1024),
        vm(512, 1024),
        vm(512, 1024),
        vm(512, 1536),
        vm(1536, 512),
        vm(512, 512),
        vm(8, 1, 512, dtype=F32),
        vm(512, 1024),
        vm(512, 1024),
        vm(512, 1024, dtype=F32),
        vm(256, 1024, dtype=F32),
        vm(512, 1024),
        vm(512, 2048),
        vm(512, 2048),
        vm(512, 1024),
        vm(256, 1024),
        vm(512, 1024),
        vm(512, 1024),
        vm(512, 1024),
        vm(512, 512),
        vm(512, 512),
        vm(512, 512, dtype=F32),
        vm(512, 512, dtype=F32),
        vm(1024, 512),
        vm(16, 16, 128, dtype=F32),
        vm(8, 1024, dtype=F32),
        vm(1, 1536, dtype=F32),
        vm(1, 2048, dtype=F32),
        vm(8, 1024, dtype=F32),
        vm(1, 2048, dtype=F32),
        vm(16, 16, 128, dtype=F32),
        vm(16, 16, 128, dtype=F32),
        vm(16, 128, dtype=F32),
        vm(16, 128, dtype=F32),
        vm(1, 512, dtype=jnp.int32),
        dma(8),
        dma(9),
        dma(4, 2, 4),
        dma(4, 2, 4),
        dma(4, 9),
        dma(4, 9),
        dma(6, 16),
        dma(6, 16),
        dma(9),
        dma(9),
        dma(5, 8),
        dma(5, 8),
        dma(5, 2, 4),
        dma(5, 2, 4),
        pltpu.SemaphoreType.REGULAR,
        pltpu.SemaphoreType.REGULAR,
    ]
    anywhere = pl.BlockSpec(memory_space=pl.ANY)
    inside = pl.BlockSpec(memory_space=pltpu.VMEM)
    outs = (
        jax.ShapeDtypeStruct((256, 1024), LOW),
        jax.ShapeDtypeStruct((256, 1024), LOW),
        jax.ShapeDtypeStruct((64, 512), F32),
        jax.ShapeDtypeStruct((64, 512), F32),
        jax.ShapeDtypeStruct((64, 512), F32),
        jax.ShapeDtypeStruct((64, 512), F32),
        jax.ShapeDtypeStruct((64, 2048), F32),
        jax.ShapeDtypeStruct((64, 2048), F32),
        jax.ShapeDtypeStruct((16, 128), F32),
    )
    parts = pl.pallas_call(
        fused_kernel,
        name="fused_layer",
        out_shape=outs,
        in_specs=[anywhere] * 8 + [inside] * 11 + [pl.BlockSpec(memory_space=pltpu.SMEM)],
        out_specs=[anywhere] * 9,
        scratch_shapes=scratch,
        compiler_params=pltpu.CompilerParams(
            collective_id=0, has_side_effects=True, vmem_limit_bytes=67043328
        ),
    )(
        tokens,
        cotangent,
        w_query,
        w_key,
        w_value,
        w_out.T,
        w_up,
        w_down.T,
        norm1_gain,
        norm1_shift,
        b_query,
        b_value,
        b_out,
        norm2_gain,
        norm2_shift,
        b_down,
        b_up,
        deal_rank,
        arrival,
        lengths,
    )
    short = jax.ShapeDtypeStruct((64,), F32)
    finals = outs[:8] + (short,) * 8 + (jax.ShapeDtypeStruct((256,), F32),)
    done = pl.pallas_call(
        settle_kernel,
        name="settle",
        out_shape=finals,
        in_specs=[anywhere] * 8 + [inside],
        out_specs=[anywhere] * 8 + [inside] * 9,
        scratch_shapes=[vm(*out.shape, dtype=out.dtype) for out in outs[:8]] + [dma(8), dma(8)],
    )(*parts)
    result, grad_tokens, grad_q, grad_k, grad_v, grad_out, grad_up, grad_down = done[:8]
    gain_one, shift_one, bias_q, bias_v, bias_out, gain_two, shift_two, bias_down, bias_up = done[8:]
    return (
        result,
        grad_tokens,
        gain_one,
        shift_one,
        grad_q,
        bias_q,
        grad_k,
        grad_v,
        bias_v,
        grad_out.T,
        bias_out,
        gain_two,
        shift_two,
        grad_up,
        bias_up,
        grad_down.T,
        bias_down,
    )


def solution(mesh):
    in_specs = (
        P(("dp", "tensor"), None),
        P(("dp", "tensor"), None),
        P("dp"),
        P("dp"),
        P("dp", "tensor"),
        P("dp"),
        P("dp", "tensor"),
        P("dp", "tensor"),
        P("dp"),
        P("tensor", "dp"),
        P("dp"),
        P("dp"),
        P("dp"),
        P("dp", "tensor"),
        P("dp"),
        P("tensor", "dp"),
        P("dp"),
        P("dp", None),
        P("dp", "tensor", None),
        P("dp", "tensor", None),
    )
    out_specs = (
        P(("dp", "tensor"), None),
        P(("dp", "tensor"), None),
        P("dp"),
        P("dp"),
        P("dp", "tensor"),
        P("dp"),
        P("dp", "tensor"),
        P("dp", "tensor"),
        P("dp"),
        P("tensor", "dp"),
        P("dp"),
        P("dp"),
        P("dp"),
        P("dp", "tensor"),
        P("dp"),
        P("tensor", "dp"),
        P("dp"),
    )
    small_slice = mesh.shape["dp"] == 16 and mesh.shape["tensor"] == 2
    program = fused_body if small_slice else body
    return jax.shard_map(program, mesh=mesh, in_specs=in_specs, out_specs=out_specs, check_vma=False)
```

```python
import jax
import jax.numpy as jnp
from jax import lax
from jax.experimental import pallas as pl
from jax.experimental.pallas import tpu as pltpu
from jax.sharding import PartitionSpec as P

D = 1024
HEADS = 16
HEAD_DIM = 64
FF = 4096


EPSILON = 1e-05
GELU_SCALE = 0.7978845608028654


def layer_norm(values, norm_gain, norm_shift):
    center = values - jnp.mean(values, axis=-1, keepdims=True)
    spread = jnp.mean(center * center, axis=-1, keepdims=True)
    return center * lax.rsqrt(spread + EPSILON) * norm_gain + norm_shift


def gelu_tanh(values):
    return jax.nn.gelu(values, approximate=True)


def contract_rows(first_op, second_op):
    return lax.dot_general(
        first_op, second_op, (((0,), (0,)), ((), ())), preferred_element_type=jnp.float32
    )


def contract_cols(first_op, second_op):
    return lax.dot_general(
        first_op, second_op, (((1,), (1,)), ((), ())), preferred_element_type=jnp.float32
    )


def take_block(vector, block_index, block_size):
    return lax.dynamic_slice_in_dim(vector, block_index * block_size, block_size, 0).astype(
        jnp.float32
    )


def place_block(total_size, block_vec, block_index):
    holder = jnp.zeros((total_size,), jnp.float32)
    return lax.dynamic_update_slice_in_dim(holder, block_vec, block_index * block_vec.shape[0], 0)


def sequence_marks(seq_lengths, group_rows):
    seq_ends = jnp.cumsum(seq_lengths)
    seq_starts = seq_ends - seq_lengths
    row_ids = lax.iota(jnp.int32, group_rows)
    inside = (row_ids[:, None] >= seq_starts[None, :]) & (row_ids[:, None] < seq_ends[None, :])
    seq_index = lax.iota(jnp.int32, seq_lengths.shape[0])
    seq_ids = jnp.sum(jnp.where(inside, seq_index[None, :], 0), axis=1)
    seq_start = jnp.sum(jnp.where(inside, seq_starts[None, :], 0), axis=1)
    return (seq_ids, row_ids - seq_start, row_ids)


def body(
    tokens,
    cotangent,
    norm1_gain,
    norm1_shift,
    w_query,
    b_query,
    w_key,
    w_value,
    b_value,
    w_out,
    b_out,
    norm2_gain,
    norm2_shift,
    w_up,
    b_up,
    w_down,
    b_down,
    lengths,
    deal_rank,
    arrival,
):
    dp_count = lax.axis_size("dp")
    tensor_count = lax.axis_size("tensor")
    tensor_rank = lax.axis_index("tensor")
    tok_rows = tokens.shape[0]
    features = tokens.shape[1]
    piece_rows = tok_rows // dp_count
    group_rows = tok_rows * tensor_count
    sending_rank = deal_rank.reshape(tok_rows)
    deal_order = jnp.argsort(sending_rank)
    arrive_order = arrival.reshape(tok_rows)
    return_order = jnp.argsort(arrive_order)

    def relocate(first_part, second_part):
        return (
            lax.all_to_all(first_part, "dp", split_axis=0, concat_axis=0, tiled=True),
            lax.all_to_all(second_part, "dp", split_axis=0, concat_axis=0, tiled=True),
        )

    def to_pieces(row_data, row_order):
        return row_data[row_order].reshape(dp_count, piece_rows, features)

    moved_x, moved_dy = relocate(to_pieces(tokens, deal_order), to_pieces(cotangent, deal_order))
    local_x = moved_x.reshape(tok_rows, features)[arrive_order]
    local_dy = moved_dy.reshape(tok_rows, features)[arrive_order]
    part_rows = w_query.shape[0]
    head_cols = w_query.shape[1]
    hidden_cols = w_up.shape[1]
    vectors = (
        norm1_gain,
        norm1_shift,
        b_query,
        b_value,
        b_out,
        norm2_gain,
        norm2_shift,
        b_down,
    )
    up_wide = b_up.shape[0] // part_rows
    vec_cols = jnp.concatenate(
        [jnp.stack(vectors, axis=1), b_up.reshape(part_rows, up_wide)], axis=1
    )
    vec_cols = jnp.pad(vec_cols, ((0, 0), (0, 128 - vec_cols.shape[1])))
    packed = jnp.concatenate(
        [w_query, w_key, w_value, w_out.T, w_up, w_down.T, vec_cols], axis=1
    )
    packed_all = lax.all_gather(packed, "dp", axis=0, tiled=True)
    edges = [0, head_cols, 2 * head_cols, 3 * head_cols, 4 * head_cols]
    edges += [4 * head_cols + hidden_cols, 4 * head_cols + 2 * hidden_cols]
    query_cols, key_cols, value_cols, out_cols, up_cols, down_cols = (
        packed_all[:, edges[i] : edges[i + 1]] for i in range(6)
    )
    out_rows = out_cols.T
    down_rows = down_cols.T
    vec_all = packed_all[:, edges[6] :]
    (
        gain_one,
        shift_one,
        bias_query,
        bias_value,
        bias_out,
        gain_two,
        shift_two,
        bias_down,
    ) = (vec_all[:, i] for i in range(8))
    bias_up = vec_all[:, 8 : 8 + up_wide].reshape(-1)
    gain_one = gain_one.astype(jnp.float32)
    shift_one = shift_one.astype(jnp.float32)
    gain_two = gain_two.astype(jnp.float32)
    shift_two = shift_two.astype(jnp.float32)
    local_heads = head_cols // HEAD_DIM
    score_scale = HEAD_DIM ** (-0.5)
    query_bias = take_block(bias_query, tensor_rank, head_cols)
    value_bias = take_block(bias_value, tensor_rank, head_cols)
    up_bias = take_block(bias_up, tensor_rank, hidden_cols)
    x_rows = local_x.astype(jnp.float32)
    first_in = layer_norm(x_rows, gain_one, shift_one).astype(jnp.bfloat16)
    group_one = lax.all_gather(first_in, "tensor", axis=0, tiled=True)
    queries = (
        jnp.dot(group_one, query_cols, preferred_element_type=jnp.float32) + query_bias
    ).astype(jnp.bfloat16)
    queries = queries.reshape(group_rows, local_heads, HEAD_DIM)
    keyset = jnp.dot(group_one, key_cols, preferred_element_type=jnp.float32).astype(jnp.bfloat16)
    keyset = keyset.reshape(group_rows, local_heads, HEAD_DIM)
    valset = (
        jnp.dot(group_one, value_cols, preferred_element_type=jnp.float32) + value_bias
    ).astype(jnp.bfloat16)
    valset = valset.reshape(group_rows, local_heads, HEAD_DIM)
    head_ids = tensor_rank * local_heads + lax.iota(jnp.int32, local_heads)
    slopes = jnp.exp2(-8.0 * (head_ids.astype(jnp.float32) + 1.0) / HEADS)
    seq_ids, positions, row_ids = sequence_marks(lengths[0], group_rows)
    qblock = min(512, group_rows)
    blocks = group_rows // qblock
    block_starts = lax.iota(jnp.int32, blocks) * qblock

    def block_scores(row_start):
        query_rows = lax.dynamic_slice_in_dim(queries, row_start, qblock, 0)
        raw_scores = (
            jnp.einsum("qhd,khd->hqk", query_rows, keyset, preferred_element_type=jnp.float32)
            * score_scale
        )
        seq_rows = lax.dynamic_slice_in_dim(seq_ids, row_start, qblock, 0)
        pos_rows = lax.dynamic_slice_in_dim(positions, row_start, qblock, 0)
        row_rows = lax.dynamic_slice_in_dim(row_ids, row_start, qblock, 0)
        distance = (pos_rows[:, None] - positions[None, :]).astype(jnp.float32)
        allowed = (seq_rows[:, None] == seq_ids[None, :]) & (row_rows[:, None] >= row_ids[None, :])
        scores = jnp.where(
            allowed[None], raw_scores - slopes[:, None, None] * distance[None], -1e30
        )
        return (query_rows, scores)

    def attend(row_start):
        query_rows, scores = block_scores(row_start)
        row_max = jnp.max(scores, axis=-1, keepdims=True)
        exponent = jnp.exp(scores - row_max)
        row_total = jnp.sum(exponent, axis=-1, keepdims=True)
        attn_probs = (exponent / row_total).astype(jnp.bfloat16)
        mixed = jnp.einsum("hqk,khd->qhd", attn_probs, valset, preferred_element_type=jnp.float32)
        return (mixed, row_max[..., 0] + jnp.log(row_total[..., 0]))

    mixed_all, log_totals = lax.map(attend, block_starts)
    heads_out = mixed_all.reshape(group_rows, head_cols).astype(jnp.bfloat16)
    attn_out = lax.psum_scatter(
        jnp.dot(heads_out, out_rows, preferred_element_type=jnp.float32).astype(jnp.bfloat16),
        "tensor",
        scatter_dimension=0,
        tiled=True,
    ).astype(jnp.float32) + bias_out.astype(jnp.float32)
    residual = x_rows + attn_out
    second_in = layer_norm(residual, gain_two, shift_two).astype(jnp.bfloat16)
    grad_in = local_dy.astype(jnp.float32)
    down_bias_term = jnp.sum(grad_in, axis=0)
    group_two = lax.all_gather(second_in, "tensor", axis=0, tiled=True)
    pre_act = jnp.dot(group_two, up_cols, preferred_element_type=jnp.float32) + up_bias
    activated = gelu_tanh(pre_act).astype(jnp.bfloat16)
    mlp_out = lax.psum_scatter(
        jnp.dot(activated, down_rows, preferred_element_type=jnp.float32).astype(jnp.bfloat16),
        "tensor",
        scatter_dimension=0,
        tiled=True,
    ).astype(jnp.float32)
    result = residual + mlp_out + bias_down.astype(jnp.float32)
    group_dy = lax.all_gather(local_dy, "tensor", axis=0, tiled=True)
    grad_down = contract_rows(activated, group_dy)
    grad_act = contract_cols(group_dy, down_rows)
    gelu_pull = jax.vjp(gelu_tanh, pre_act)[1]
    grad_pre = gelu_pull(grad_act)[0].astype(jnp.bfloat16)
    grad_up = contract_rows(group_two, grad_pre)
    up_bias_term = place_block(FF, jnp.sum(grad_pre, axis=0, dtype=jnp.float32), tensor_rank)
    grad_two = lax.psum_scatter(
        contract_cols(grad_pre, up_cols).astype(jnp.bfloat16),
        "tensor",
        scatter_dimension=0,
        tiled=True,
    ).astype(jnp.float32)
    result_low = result.astype(jnp.bfloat16)
    norm_two_pull = jax.vjp(layer_norm, residual, gain_two, shift_two)[1]
    grad_res_norm, gain_two_term, shift_two_term = norm_two_pull(grad_two)
    grad_resid = grad_in + grad_res_norm
    grad_attn = grad_resid.astype(jnp.bfloat16)
    out_bias_term = jnp.sum(grad_attn, axis=0, dtype=jnp.float32)
    group_grad = lax.all_gather(grad_attn, "tensor", axis=0, tiled=True)
    grad_out = contract_rows(heads_out, group_grad)
    grad_heads = (
        contract_cols(group_grad, out_rows)
        .astype(jnp.bfloat16)
        .reshape(group_rows, local_heads, HEAD_DIM)
    )

    def attend_back(running, block_item):
        key_accum, value_accum = running
        row_start, log_total = block_item
        query_rows, scores = block_scores(row_start)
        attn_probs = jnp.exp(scores - log_total[..., None])
        grad_rows = lax.dynamic_slice_in_dim(grad_heads, row_start, qblock, 0)
        grad_probs = jnp.einsum(
            "qhd,khd->hqk", grad_rows, valset, preferred_element_type=jnp.float32
        )
        row_dot = jnp.sum(attn_probs * grad_probs, axis=-1, keepdims=True)
        grad_scores = (attn_probs * (grad_probs - row_dot)).astype(jnp.bfloat16)
        grad_query_rows = jnp.einsum(
            "hqk,khd->qhd", grad_scores, keyset, preferred_element_type=jnp.float32
        )
        grad_query_rows = (grad_query_rows * score_scale).astype(jnp.bfloat16)
        key_accum = (
            key_accum
            + jnp.einsum(
                "hqk,qhd->khd", grad_scores, query_rows, preferred_element_type=jnp.float32
            )
            * score_scale
        )
        value_accum = value_accum + jnp.einsum(
            "hqk,qhd->khd",
            attn_probs.astype(jnp.bfloat16),
            grad_rows,
            preferred_element_type=jnp.float32,
        )
        return ((key_accum, value_accum), grad_query_rows)

    zero_heads = jnp.zeros((group_rows, local_heads, HEAD_DIM), jnp.float32)
    (key_accum, value_accum), grad_query_blocks = lax.scan(
        attend_back, (zero_heads, zero_heads), (block_starts, log_totals)
    )
    grad_query = grad_query_blocks.reshape(group_rows, head_cols)
    grad_key = key_accum.reshape(group_rows, head_cols).astype(jnp.bfloat16)
    grad_value = value_accum.reshape(group_rows, head_cols).astype(jnp.bfloat16)
    query_bias_term = place_block(D, jnp.sum(grad_query, axis=0, dtype=jnp.float32), tensor_rank)
    value_bias_term = place_block(D, jnp.sum(grad_value, axis=0, dtype=jnp.float32), tensor_rank)
    grad_wquery = contract_rows(group_one, grad_query)
    grad_wkey = contract_rows(group_one, grad_key)
    grad_wvalue = contract_rows(group_one, grad_value)
    grad_one = lax.psum_scatter(
        (
            contract_cols(grad_query, query_cols)
            + contract_cols(grad_key, key_cols)
            + contract_cols(grad_value, value_cols)
        ).astype(jnp.bfloat16),
        "tensor",
        scatter_dimension=0,
        tiled=True,
    ).astype(jnp.float32)
    norm_one_pull = jax.vjp(layer_norm, x_rows, gain_one, shift_one)[1]
    grad_x_norm, gain_one_term, shift_one_term = norm_one_pull(grad_one)
    grad_tokens = (grad_resid + grad_x_norm).astype(jnp.bfloat16)
    small_terms = jnp.stack(
        (
            gain_one_term,
            shift_one_term,
            query_bias_term,
            value_bias_term,
            out_bias_term,
            gain_two_term,
            shift_two_term,
            down_bias_term,
        ),
        axis=1,
    )
    small_terms = jnp.concatenate([small_terms, up_bias_term.reshape(-1, up_wide)], axis=1)
    small_terms = jnp.pad(small_terms, ((0, 0), (0, 128 - small_terms.shape[1])))
    terms = (grad_wquery, grad_wkey, grad_wvalue, grad_out.T, grad_up, grad_down.T, small_terms)
    packed_grads = jnp.concatenate([term.astype(jnp.bfloat16) for term in terms], axis=1)
    reduced = lax.psum_scatter(packed_grads, "dp", scatter_dimension=0, tiled=True).astype(
        jnp.float32
    )
    shards = [reduced[:, edges[i] : edges[i + 1]] for i in range(6)]
    shards[3] = shards[3].T
    shards[5] = shards[5].T
    sums = lax.psum(reduced[:, edges[6] : edges[6] + 8 + up_wide], "tensor")
    smalls = [sums[:, i] for i in range(7)] + [sums[:, 8:].reshape(-1), sums[:, 7]]
    back_y, back_dx = relocate(
        to_pieces(result_low, return_order), to_pieces(grad_tokens, return_order)
    )
    given_y = back_y.reshape(tok_rows, features)[sending_rank]
    given_dx = back_dx.reshape(tok_rows, features)[sending_rank]
    return (
        given_y,
        given_dx,
        smalls[0],
        smalls[1],
        shards[0],
        smalls[2],
        shards[1],
        shards[2],
        smalls[3],
        shards[3],
        smalls[4],
        smalls[5],
        smalls[6],
        shards[4],
        smalls[7],
        shards[5],
        smalls[8],
    )


MESH = pl.DeviceIdType.MESH
F32 = jnp.float32
LOW = jnp.bfloat16
RING = 8
PAIR = 128


def dot_nn(first_op, second_op):
    return lax.dot_general(
        first_op, second_op, (((1,), (0,)), ((), ())), preferred_element_type=F32
    )


def dot_nt(first_op, second_op):
    return lax.dot_general(
        first_op, second_op, (((1,), (1,)), ((), ())), preferred_element_type=F32
    )


def loop(count, step):
    def run(i, carry):
        step(i)
        return carry

    lax.fori_loop(0, count, run, 0)


def at(index, size):
    return pl.ds(pl.multiple_of(index * size, size), size)


def fused_kernel(
    tok_ref,
    cot_ref,
    wq_ref,
    wk_ref,
    wv_ref,
    wot_ref,
    wup_ref,
    wdt_ref,
    *refs,
):
    vectors, refs = refs[:9], refs[9:]
    rank_ref, arrive_ref, len_ref = refs[:3]
    homes, refs = refs[3:12], refs[12:]
    fused_layer(
        (tok_ref, cot_ref, wq_ref, wk_ref, wv_ref, wot_ref, wup_ref, wdt_ref),
        vectors,
        rank_ref,
        arrive_ref,
        len_ref,
        homes,
        *refs,
    )


def fused_layer(
    given,
    vectors,
    rank_ref,
    arrive_ref,
    len_ref,
    homes,
    gq_out,
    gk_out,
    gv_out,
    go_out,
    gu_out,
    gd_out,
    small_out,
    wqkv,
    wo,
    wu,
    wd,
    ga,
    gb,
    go,
    gu,
    gd,
    land,
    tok_v,
    cot_v,
    pcx,
    pcd,
    arrx,
    arrd,
    backy,
    backd,
    xg,
    dyg,
    a1,
    qkv,
    qkvt,
    ho,
    lse,
    po,
    por,
    res,
    yb,
    rstd,
    a2,
    act,
    dpre,
    pm,
    pmr,
    pd,
    pdr,
    dattn,
    dh,
    dht,
    dk_acc,
    dv_acc,
    tbuf,
    vgat,
    vrow,
    bqkv,
    bup,
    gvec,
    gbup,
    svec,
    svr,
    sown,
    sown_r,
    start_row,
    ld,
    st,
    ag_s,
    ag_r,
    mt_s,
    mt_r,
    aa_s,
    aa_r,
    y_s,
    y_r,
    rm_s,
    rm_r,
    rr_s,
    rr_r,
    ax_r,
    rx_r,
    ready_one,
    ready_two,
):
    tok_ref, cot_ref, wq_ref, wk_ref, wv_ref, wot_ref, wup_ref, wdt_ref = given
    d = lax.axis_index("dp")
    t = lax.axis_index("tensor")
    other = 1 - t
    core = lax.rem(d, 2)
    chip = lax.div(d, 2)
    xc = lax.rem(chip, 2)
    zc = lax.div(chip, 2)
    p = zc + xc * (7 - 2 * zc)

    def chip_at(pos):
        pos = lax.rem(pos + 2 * RING, RING)
        xx = lax.div(pos, 4)
        zz = pos + xx * (7 - 2 * pos)
        return zz * 2 + xx

    def dev(pos):
        return chip_at(pos) * 2 + core

    def mdev(pos):
        return chip_at(pos) * 2 + 1 - core

    def outer(pos):
        spot = lax.rem(pos + 2 * RING, 4)
        return (spot == 0) | (spot == 3)

    inner = ~outer(p)
    even = lax.rem(p, 2) == 0
    over = dev(7 - p)
    mate = d + 1 - 2 * core
    sides = (dev(p + 1), dev(p - 1))
    weights = (wqkv, wo, wu, wd)
    grads = (ga, go, gu, gd, gb)
    widths = (768, 512, 2048, 2048, 768)
    landing = (wd, wd, wu, land, wd)
    offsets = (0, 1536, 0, 0, 768)
    dqkv = act

    def remote(src, dst, send, recv, device):
        return pltpu.make_async_remote_copy(
            src_ref=src,
            dst_ref=dst,
            send_sem=send,
            recv_sem=recv,
            device_id=device,
            device_id_type=MESH,
        )

    def signal(sem, device):
        pl.semaphore_signal(sem, inc=1, device_id=device, device_id_type=MESH)

    loads = [
        pltpu.make_async_copy(tok_ref, tok_v, ld.at[0]),
        pltpu.make_async_copy(cot_ref, cot_v, ld.at[1]),
        pltpu.make_async_copy(wq_ref, wqkv.at[d, :, pl.ds(0, 512)], ld.at[2]),
        pltpu.make_async_copy(wk_ref, wqkv.at[d, :, pl.ds(512, 512)], ld.at[3]),
        pltpu.make_async_copy(wv_ref, wqkv.at[d, :, pl.ds(1024, 512)], ld.at[4]),
        pltpu.make_async_copy(wot_ref, wo.at[d], ld.at[5]),
        pltpu.make_async_copy(wup_ref, wu.at[d], ld.at[6]),
        pltpu.make_async_copy(wdt_ref, wd.at[d], ld.at[7]),
    ]
    for load in loads:
        load.start()
    barrier = pltpu.get_barrier_semaphore()

    def store(i, src):
        return pltpu.make_async_copy(src, homes[i], st.at[i])

    def greet(k):
        signal(barrier, {"dp": lax.rem(d + k + 1, 16)})

    loop(15, greet)
    signal(barrier, {"tensor": other})

    def rows_send(kind, src, dst):
        def step(k):
            spot = lax.rem(d + k + 1, 16)
            remote(
                src.at[at(spot, 16)],
                dst.at[at(d, 16)],
                aa_s.at[kind],
                aa_r.at[kind],
                {"dp": spot},
            ).start()

        loop(15, step)
        dst[at(d, 16), :] = src[at(d, 16), :]

    def rows_all(kind, src, dst):
        bulk = pl.ds(0, 240)
        return remote(src.at[bulk], dst.at[bulk], aa_s.at[kind], aa_r.at[kind], {"dp": mate})

    def rows_wait(kind, src, dst):
        rows_all(kind, src, dst).wait_recv()

    def rows_drain(kind, src, dst):
        rows_all(kind, src, dst).wait_send()

    def tiles_send(kind, src_of, dst):
        def step(k):
            spot = lax.rem(d + k + 1, 16)
            remote(src_of(spot), dst.at[d], aa_s.at[kind], aa_r.at[kind], {"dp": spot}).start()

        loop(15, step)

    def tiles_all(kind, dst):
        bulk = dst.at[pl.ds(0, 15)]
        return remote(bulk, bulk, aa_s.at[kind], aa_r.at[kind], {"dp": mate})

    def cross(i, src, dst):
        return remote(src, dst, y_s.at[i], y_r.at[i], {"tensor": other})

    def ring_part(ref, slot, way, step):
        if step == 3:
            return ref.at[slot, pl.ds(32 * way, 32)]
        return ref.at[slot]

    def turn(way, steps):
        return p - steps if way == 0 else p + steps

    def ag_copy(c, way, step):
        part = ring_part(weights[c], dev(turn(way, step)), way, step)
        return remote(
            part, part, ag_s.at[c], ag_r.at[c, way, step], {"dp": sides[way]}
        )

    def ag_arrival(c, way, step):
        part = ring_part(weights[c], dev(turn(way, step + 1)), way, step)
        return remote(
            part, part, ag_s.at[c], ag_r.at[c, way, step], {"dp": sides[way]}
        )

    def mate_copy(c, k, place):
        if k == 0:
            part = weights[c].at[place(p)]
        else:
            way, step = (k - 1) // 4, (k - 1) % 4
            part = ring_part(weights[c], place(turn(way, step + 1)), way, step)
        return remote(part, part, mt_s.at[c], mt_r.at[c], {"dp": mate})

    def ag_start(c):
        for way in range(2):
            ag_copy(c, way, 0).start()
        mate_copy(c, 0, dev).start()

    def ag_over(c):
        part = weights[c].at[dev(jnp.where(even, p - 1, p + 1))]
        return remote(part, part, ag_s.at[c], ax_r.at[c], {"dp": over})

    def ag_event(c, step):
        if step == 3:

            @pl.when(inner)
            def _():
                part = weights[c].at[dev(p + 4)]
                remote(part, part, ag_s.at[c], ax_r.at[c], {"dp": over}).wait_recv()

        for way in range(2):
            if step == 3:

                @pl.when(outer(p))
                def _():
                    ag_arrival(c, way, step).wait_recv()

            else:
                ag_arrival(c, way, step).wait_recv()
            if step == 2:

                @pl.when(outer(turn(1 - way, 1)))
                def _():
                    ag_copy(c, way, 3).start()

            elif step < 2:
                ag_copy(c, way, step + 1).start()
            mate_copy(c, 1 + 4 * way + step, dev).start()
        if step == 0:

            @pl.when(inner)
            def _():
                ag_over(c).start()

    def mate_all(c):
        bulk = weights[c].at[pl.ds(0, 8)]
        return remote(bulk, bulk, mt_s.at[c], mt_r.at[c], {"dp": mate})

    def ag_finish(c):
        mate_all(c).wait_recv()

    def ag_drain(c):
        def sent(halves):
            bulk = weights[c].at[pl.ds(0, halves), pl.ds(0, 32)]
            remote(bulk, bulk, ag_s.at[c], ag_r.at[c, 0, 0], {"dp": over}).wait_send()

        pl.when(inner)(lambda: sent(15))
        pl.when(outer(p))(lambda: sent(13))
        mate_all(c).wait_send()

    def inbox(c, slot, rows=pl.ds(0, 64)):
        return landing[c].at[slot, rows, pl.ds(offsets[c], widths[c])]

    def arrived(c, slot, rows):
        return landing[c][slot, rows, offsets[c] : offsets[c] + widths[c]].astype(F32)

    halves = (1 - lax.div(zc, 2), lax.div(zc, 2))

    def rm_send(c, half):
        for i in range(4):
            spot = half * 4 + i
            remote(
                grads[c].at[spot * 2 + 1 - core],
                inbox(c, spot),
                rm_s.at[c],
                rm_r.at[c, half],
                {"dp": mate},
            ).start()

    def rm_wait(c, half):
        bulk = landing[c].at[pl.ds(half * 4, 4), pl.ds(0, 64), pl.ds(offsets[c], widths[c])]
        remote(bulk, bulk, rm_s.at[c], rm_r.at[c, half], {"dp": mate}).wait_recv()

    def rs_copy(c, way, step):
        dest = dev(p + 4 - step if way == 0 else p - 4 + step)
        slot = 8 + way * 4 + step
        if step == 0:
            half = pl.ds(32 * way, 32)
            src, dst = grads[c].at[dest, half], inbox(c, slot, half)
        else:
            src, dst = grads[c].at[dest], inbox(c, slot)
        return remote(src, dst, rr_s.at[c], rr_r.at[c, way, step], {"dp": sides[way]})

    def rs_add(c, slot, rows, boxes):
        total = grads[c][slot, rows, :].astype(F32)
        for box in boxes:
            total += arrived(c, box, rows)
        return total

    def rs_over(c, slot):
        return remote(
            grads[c].at[dev(p + 4)], inbox(c, slot), rr_s.at[c], rx_r.at[c], {"dp": over}
        )

    def rs_fold(c, slot, first, count, boxes):
        def add(i):
            rows = at(i + first, 16)
            grads[c][slot, rows, :] = rs_add(c, slot, rows, boxes).astype(LOW)

        loop(count, add)

    def rs_start(c):
        far = chip_at(p + 4)
        rm_wait(c, halves[0])
        rs_fold(c, far * 2 + core, 0, 4, (far,))

        @pl.when(outer(p))
        def _():
            for way in range(2):
                rs_copy(c, way, 0).start()

        @pl.when(inner)
        def _():
            rs_over(c, jnp.where(even, 12, 8)).start()

    def rs_event(c, step):
        if step == 2:

            @pl.when(inner)
            def _():
                box = jnp.where(even, 8, 12)
                rs_over(c, box).wait_recv()
                rs_fold(c, dev(jnp.where(even, p - 1, p + 1)), 0, 4, (box,))

        for way in range(2):
            pos = p + 3 - step if way == 0 else p - 3 + step
            spot = chip_at(pos)
            slot = spot * 2 + core
            box = 8 + way * 4 + step
            if step == 0 and way == 0:
                rm_wait(c, halves[1])
            if step == 0:

                @pl.when(outer(pos))
                def _():
                    rs_copy(c, way, 0).wait_recv()
                    rs_fold(c, slot, 2 * way, 2, (spot, box))
                    rs_fold(c, slot, 2 - 2 * way, 2, (spot,))

                @pl.when(~outer(pos))
                def _():
                    rs_fold(c, slot, 0, 4, (spot,))

            else:
                rs_copy(c, way, step).wait_recv()
                rs_fold(c, slot, 0, 4, (spot, box))
            rs_copy(c, way, step + 1).start()

    def rs_finish(c, keep):
        for way in range(2):
            rs_copy(c, way, 3).wait_recv()

        def add(i):
            rows = at(i, 16)
            keep(rows, rs_add(c, d, rows, (chip, 11, 15)))

        loop(4, add)

    def keep_in(ref):
        def keep(rows, total):
            ref[rows, :] = total

        return keep

    def keep_heads(first):
        def keep(rows, total):
            for j, ref in enumerate((gq_out, gk_out, gv_out)):
                ref[rows, first : first + 256] = total[:, 256 * j : 256 * j + 256]

        return keep

    def rs_drain(c):
        sent = grads[c].at[pl.ds(0, 7)]
        remote(sent, sent, rr_s.at[c], rr_r.at[c, 0, 1], {"dp": over}).wait_send()
        sent = grads[c].at[pl.ds(0, 8)]
        remote(sent, sent, rm_s.at[c], rm_r.at[c, 0], {"dp": mate}).wait_send()

    def free_for_reduction(sem):
        signal(sem, {"dp": mate})
        for side in sides:
            signal(sem, {"dp": side})

        @pl.when(inner)
        def _():
            signal(sem, {"dp": over})

    def others_free(sem):
        pl.when(inner)(lambda: pl.semaphore_wait(sem, 4))
        pl.when(outer(p))(lambda: pl.semaphore_wait(sem, 3))

    def picks(ref):
        slots = lax.broadcasted_iota(jnp.int32, (256, 256), 0)
        return jnp.where(slots == ref[0, :, :], 1.0, 0.0)

    zeros = jnp.zeros((1, 64), F32)
    for i in range(8):
        row = vectors[i][...].astype(F32).reshape(1, 64)
        early = jnp.concatenate([row, zeros], axis=1)
        late = jnp.concatenate([zeros, row], axis=1)
        vgat[d, i : i + 1, :] = jnp.where(core == 0, early, late)
    row = vectors[8][...].astype(F32).reshape(1, 256)
    vgat[d, 8:9, :] = row[:, 0:128]
    vgat[d, 9:10, :] = row[:, 128:256]
    vgat[d, 10:16, :] = jnp.zeros((6, 128), F32)
    loads[0].wait()
    spread = picks(rank_ref).astype(LOW)
    pcx[...] = dot_nn(spread, tok_v[...]).astype(LOW)
    pl.semaphore_wait(barrier, 16)
    rows_send(0, pcx, arrx)
    tiles_send(4, lambda spot: vgat.at[d], vgat)
    for i in range(2, 6):
        loads[i].wait()
    ag_start(0)
    ag_start(1)
    loads[1].wait()
    pcd[...] = dot_nn(spread, cot_v[...]).astype(LOW)
    for i in range(6, 8):
        loads[i].wait()

    own = at(t, 256)
    gather_rows = picks(arrive_ref).T.astype(LOW)
    rows_wait(0, pcx, arrx)
    xg[own, :] = dot_nn(gather_rows, arrx[...]).astype(LOW)
    cross(0, xg.at[own], xg.at[own]).start()
    ag_event(0, 0)
    ag_event(1, 0)

    tiles_all(4, vgat).wait_recv()
    for m in range(8):
        both = vgat[2 * m, :, :] + vgat[2 * m + 1, :, :]
        vrow[:, 128 * m : 128 * (m + 1)] = both[0:8, :]
    for j in range(8):
        block = vgat[8 * t + j, :, :]
        bup[:, 256 * j : 256 * j + 128] = block[8:9, :]
        bup[:, 256 * j + 128 : 256 * j + 256] = block[9:10, :]
    bqkv[:, 0:512] = vrow[2:3, at(t, 512)]
    bqkv[:, 512:1024] = jnp.zeros((1, 512), F32)
    bqkv[:, 1024:1536] = vrow[3:4, at(t, 512)]
    ends = jnp.int32(0)
    row_ids = lax.broadcasted_iota(jnp.int32, (1, 512), 1)
    starts = jnp.zeros((1, 512), jnp.int32)
    for i in range(3):
        ends = ends + len_ref[0, i]
        starts = jnp.where(row_ids >= ends, ends, starts)
    start_row[...] = starts
    gvec[...] = jnp.zeros((8, 1024), F32)

    def stats(values):
        center = values - jnp.mean(values, axis=-1, keepdims=True)
        spread_of = jnp.mean(center * center, axis=-1, keepdims=True)
        scale = lax.rsqrt(spread_of + EPSILON)
        return center * scale, scale

    def norm_one(half):
        def step(i):
            rows = at(half * 8 + i, 32)
            normed, _ = stats(xg[rows, :].astype(F32))
            a1[rows, :] = (normed * vrow[0:1, :] + vrow[1:2, :]).astype(LOW)

        loop(8, step)

    norm_one(t)
    ag_event(0, 1)
    ag_event(1, 1)
    cross(0, xg.at[own], xg.at[at(other, 256)]).wait_recv()
    norm_one(other)
    ag_event(0, 2)
    ag_event(1, 2)
    ag_start(2)
    rows_send(1, pcd, arrd)
    ag_event(0, 3)
    ag_event(1, 3)
    ag_finish(0)

    def project(i):
        cols = at(i, 256)
        value = dot_nn(a1[...], wqkv[:, :, cols].reshape(1024, 256)) + bqkv[:, cols]
        low = value.astype(LOW).astype(F32)
        qkv[:, cols] = low.astype(LOW)
        qkvt[cols, :] = low.T.astype(LOW)

    loop(6, project)
    ag_event(2, 0)
    ag_start(3)

    def slope_of(pair, half):
        head = (t * 8 + pair * 2 + half + 1).astype(F32)
        return jnp.exp2(jnp.full((1, PAIR), -0.5, F32) * head)

    def padded(block, half):
        zero = jnp.zeros_like(block)
        return jnp.concatenate([block, zero] if half == 0 else [zero, block], axis=0)

    def band(qb):
        first = max(0, qb - 2) * 128
        width = (qb + 1) * 128 - first
        keys = lax.broadcasted_iota(jnp.int32, (width, PAIR), 0) + first
        rows = lax.broadcasted_iota(jnp.int32, (width, PAIR), 1) + qb * 128
        allowed = (keys <= rows) & (keys >= start_row[:, qb * 128 : qb * 128 + 128])
        return first, width, allowed, (rows - keys).astype(F32)

    def score(pair, half, qb, first, width, allowed, distance):
        key_rows = qkv[first : first + width, at(pair + 4, PAIR)]
        query = qkvt[at(pair * 2 + half, 64), qb * 128 : qb * 128 + 128] * 0.125
        raw = dot_nn(key_rows, padded(query, half))
        return jnp.where(allowed, raw - slope_of(pair, half) * distance, -1e30)

    def attend(qbs):
        def step(pair):
            for qb in qbs:
                first, width, allowed, distance = band(qb)
                parts = []
                for half in range(2):
                    s = score(pair, half, qb, first, width, allowed, distance)
                    top = jnp.max(s, axis=0, keepdims=True)
                    e = jnp.exp(s - top)
                    total = jnp.sum(e, axis=0, keepdims=True)
                    probs = (e * (1.0 / total)).astype(LOW)
                    lse[pair * 2 + half, :, qb * 128 : qb * 128 + 128] = top + jnp.log(total)
                    value_t = qkvt[at(16 + pair * 2 + half, 64), first : first + width]
                    parts.append(dot_nn(value_t, probs))
                ho[qb * 128 : qb * 128 + 128, at(pair, PAIR)] = (
                    jnp.concatenate(parts, axis=0).T.astype(LOW)
                )

        loop(4, step)

    def out_project(rb):
        rows = slice(rb * 256, rb * 256 + 256)

        def step(i):
            po[rows, at(i, 256)] = dot_nt(ho[rows, :], wo[pl.ds(i * 4, 4)].reshape(256, 512)).astype(LOW)

        loop(4, step)
        cross(2 + rb, po.at[rows], por.at[rows]).start()

    attend((0, 1))
    ag_finish(1)
    out_project(0)
    ag_event(2, 1)
    attend((2, 3))
    out_project(1)
    ag_event(3, 0)
    ag_event(2, 2)
    rows_wait(1, pcd, arrd)
    own_dy = dot_nn(gather_rows, arrd[...])
    dyg[own, :] = own_dy.astype(LOW)
    gvec[7:8, :] = jnp.sum(own_dy, axis=0, keepdims=True)
    cross(1, dyg.at[own], dyg.at[own]).start()
    ag_event(3, 1)
    ag_event(2, 3)
    ag_finish(2)

    def mlp_enter(rb):
        rows = slice(rb * 256, rb * 256 + 256)
        cross(2 + rb, po.at[rows], por.at[rows]).wait_recv()

        def enter(i):
            part = at(rb * 8 + i, 32)
            value = xg[part, :].astype(F32) + (po[part, :].astype(F32) + por[part, :].astype(F32))
            value = value + vrow[4:5, :]

            @pl.when(t == rb)
            def _():
                yb[at(i, 32), :] = value

            normed, scale = stats(value)
            res[part, :] = normed
            rstd[part, :] = jnp.broadcast_to(scale, (32, 128))
            a2[part, :] = (normed * vrow[5:6, :] + vrow[6:7, :]).astype(LOW)

        loop(8, enter)

    def up(i):
        cols = at(i, 256)
        v = dot_nn(a2[...], wu[:, :, cols].reshape(1024, 256)) + bup[:, cols]
        square = v * v
        bend = jnp.tanh(GELU_SCALE * (v + 0.044715 * (square * v)))
        half_v = 0.5 * v
        both = 1.0 + bend
        act[:, cols] = (half_v * both).astype(LOW)
        slope = 0.5 * both + (half_v * (1.0 - bend * bend)) * (
            GELU_SCALE + (GELU_SCALE * 3.0 * 0.044715) * square
        )
        dpre[:, cols] = slope.astype(LOW)

    def act_back(i):
        cols = at(i, 256)
        grad = dot_nn(dyg[...], wd[:, :, cols].reshape(1024, 256))
        back = (grad * dpre[:, cols].astype(F32)).astype(LOW)
        dpre[:, cols] = back
        gbup[:, cols] = jnp.sum(back.astype(F32), axis=0, keepdims=True)

    def mlp_back(rb):
        rows = slice(rb * 256, rb * 256 + 256)

        def down(i):
            pd[rows, at(i, 256)] = dot_nt(dpre[rows, :], wu[pl.ds(i * 4, 4)].reshape(256, 2048)).astype(LOW)

        loop(4, down)
        cross(5 + rb, pd.at[rows], pdr.at[rows]).start()

    def mlp_out(i):
        pm[:, at(i, 256)] = dot_nt(act[...], wd[pl.ds(i * 4, 4)].reshape(256, 2048)).astype(LOW)

    def flip(ref):
        def step(i):
            tbuf[at(i, 256), :] = ref[:, at(i, 256)].T

        loop(4, step)

    def plain(ref):
        return lambda j: ref[:, at(j, 512)]

    def weight_grad(c, second, count, wide):
        def half_grad(half):
            rows = at(half, 512)

            def inner(j):
                grads[c][pl.ds(half * 8, 8), :, at(j, wide)] = (
                    dot_nn(tbuf[rows, :], second(j)).astype(LOW).reshape(8, 64, wide)
                )

            loop(count, inner)
            rm_send(c, half)

        half_grad(halves[0])
        rs_start(c)
        half_grad(halves[1])

    mlp_enter(0)
    mlp_enter(1)
    loop(4, up)
    ag_event(3, 2)
    loop(4, lambda i: up(i + 4))
    ag_event(3, 3)
    ag_finish(3)
    loop(4, mlp_out)
    cross(4, pm.at[at(other, 256)], pmr).start()
    cross(1, dyg.at[own], dyg.at[at(other, 256)]).wait_recv()
    flip(dyg)
    weight_grad(3, plain(act), 4, 512)
    loop(8, act_back)
    rs_event(3, 0)
    mlp_back(0)
    mlp_back(1)
    ag_drain(2)
    free_for_reduction(ready_one)
    ag_drain(3)
    free_for_reduction(ready_two)

    rows_drain(0, pcx, arrx)
    rows_drain(1, pcd, arrd)
    send_back = picks(arrive_ref).astype(LOW)
    cross(4, pm.at[at(other, 256)], pmr).wait_recv()

    def finish_y(i):
        part = at(i, 32)
        mine = at(t * 8 + i, 32)
        value = yb[part, :] + (pm[mine, :].astype(F32) + pmr[part, :].astype(F32)) + vrow[7:8, :]
        tok_v[part, :] = value.astype(LOW)

    loop(8, finish_y)
    pcx[...] = dot_nn(send_back, tok_v[...]).astype(LOW)
    rows_send(2, pcx, backy)
    others_free(ready_one)
    flip(a2)
    weight_grad(2, plain(dpre), 4, 512)
    rs_event(3, 1)

    def norm_two_back(rb):
        rows = slice(rb * 256, rb * 256 + 256)
        cross(5 + rb, pd.at[rows], pdr.at[rows]).wait_recv()

        def step(i):
            part = at(rb * 8 + i, 32)
            grad = pd[part, :].astype(F32) + pdr[part, :].astype(F32)
            normed, scale = res[part, :], rstd[part, 0:1]
            e = grad * vrow[5:6, :]
            inner = e - jnp.mean(e, axis=-1, keepdims=True)
            inner = inner - normed * jnp.mean(e * normed, axis=-1, keepdims=True)
            dy = dyg[part, :].astype(F32)
            full = dy + inner * scale
            res[part, :] = full
            low = full.astype(LOW)
            dattn[part, :] = low
            gvec[4:5, :] += 0.5 * jnp.sum(low.astype(F32), axis=0, keepdims=True)
            gvec[5:6, :] += 0.5 * jnp.sum(grad * normed, axis=0, keepdims=True)
            gvec[6:7, :] += 0.5 * jnp.sum(grad, axis=0, keepdims=True)

        loop(8, step)

        def heads(i):
            cols = at(i, 256)
            value = dot_nn(dattn[rows, :], wo[:, :, cols].reshape(1024, 256)).astype(LOW)
            dh[rows, cols] = value
            dht[cols, rows] = value.astype(F32).T.astype(LOW)

        loop(2, heads)

    lanes = lax.broadcasted_iota(jnp.int32, (1, PAIR), 1) < 64

    def attend_back(qbs, first_pair, count):
        def step(index):
            pair = index + first_pair
            for qb in qbs:
                first, width, allowed, distance = band(qb)
                queries = slice(qb * 128, qb * 128 + 128)
                span = slice(first, first + width)
                values = qkv[span, at(pair + 8, PAIR)]
                query_rows = qkv[queries, at(pair, PAIR)]
                grad_rows = dh[queries, at(pair, PAIR)]
                parts, keys_part, values_part = [], [], []
                for half in range(2):
                    s = score(pair, half, qb, first, width, allowed, distance)
                    probs = jnp.exp(s - lse[pair * 2 + half, :, queries])
                    grad_t = dht[at(pair * 2 + half, 64), queries]
                    grad_p = dot_nn(values, padded(grad_t, half))
                    row_dot = jnp.sum(probs * grad_p, axis=0, keepdims=True)
                    grad_s = (probs * (grad_p - row_dot)).astype(LOW)
                    key_t = qkvt[at(8 + pair * 2 + half, 64), span]
                    parts.append(dot_nn(key_t, grad_s))
                    keys_part.append(dot_nn(grad_s, query_rows))
                    values_part.append(dot_nn(probs.astype(LOW), grad_rows))
                dqkv[queries, at(pair, PAIR)] = (
                    (jnp.concatenate(parts, axis=0) * 0.125).T.astype(LOW)
                )
                dk_acc[span, at(pair, PAIR)] += jnp.where(lanes, keys_part[0], keys_part[1])
                dv_acc[span, at(pair, PAIR)] += jnp.where(lanes, values_part[0], values_part[1])
            if 3 in qbs:
                dqkv[:, at(pair + 4, PAIR)] = (dk_acc[:, at(pair, PAIR)] * 0.125).astype(LOW)
                dqkv[:, at(pair + 8, PAIR)] = dv_acc[:, at(pair, PAIR)].astype(LOW)

        loop(count, step)

    def heads_part(h):
        return lambda j: dqkv[:, pl.ds(pl.multiple_of(j * 512 + h * 256, 256), 256)]

    norm_two_back(0)
    dk_acc[...] = jnp.zeros((512, 512), F32)
    dv_acc[...] = jnp.zeros((512, 512), F32)
    attend_back((0, 1), 0, 4)
    rs_event(3, 2)
    rs_event(2, 0)
    norm_two_back(1)
    others_free(ready_two)
    flip(dattn)
    weight_grad(1, plain(ho), 1, 512)
    attend_back((2, 3), 0, 2)
    rs_event(2, 1)
    flip(a1)
    weight_grad(0, heads_part(0), 3, 256)
    rs_finish(3, keep_in(gd_out))
    store(7, gd_out).start()
    rs_event(1, 0)
    attend_back((2, 3), 2, 2)
    rs_event(2, 2)
    rs_event(0, 0)

    def attn_in_back(i):
        po[:, at(i, 256)] = dot_nt(
            dqkv[:, 0:1536], wqkv[pl.ds(i * 4, 4)].reshape(256, 1536)
        ).astype(LOW)

    for rb in range(2):
        rows = slice(rb * 256, rb * 256 + 256)
        cross(2 + rb, po.at[rows], por.at[rows]).wait_send()
    loop(4, attn_in_back)
    cross(7, po.at[at(other, 256)], por.at[pl.ds(0, 256)]).start()
    rs_event(1, 1)
    weight_grad(4, heads_part(1), 3, 256)
    rs_event(0, 1)
    rs_event(1, 2)
    rs_event(4, 0)
    sums = jnp.zeros((1, 1536), F32)
    for i in range(4):
        sums = sums + jnp.sum(
            dqkv[i * 128 : i * 128 + 128, 0:1536].astype(F32), axis=0, keepdims=True
        )
    gvec[2:3, at(t, 512)] = sums[:, 0:512]
    gvec[3:4, at(t, 512)] = sums[:, 1024:1536]
    take_back = picks(rank_ref).T.astype(LOW)
    rows_wait(2, pcx, backy)
    tok_v[...] = dot_nn(take_back, backy[...]).astype(LOW)
    store(0, tok_v).start()
    rs_finish(2, keep_in(gu_out))
    store(6, gu_out).start()
    rs_event(0, 2)
    rs_event(4, 1)

    def norm_one_again(i):
        part = at(i, 32)
        normed, scale = stats(xg[at(t * 8 + i, 32), :].astype(F32))
        yb[part, :] = normed
        rstd[part, :] = jnp.broadcast_to(scale, (32, 128))

    loop(8, norm_one_again)
    cross(7, po.at[at(other, 256)], por.at[pl.ds(0, 256)]).wait_recv()

    def norm_one_back(i):
        part = at(i, 32)
        mine = at(t * 8 + i, 32)
        grad = po[mine, :].astype(F32) + por[part, :].astype(F32)
        normed, scale = yb[part, :], rstd[part, 0:1]
        e = grad * vrow[0:1, :]
        inner = e - jnp.mean(e, axis=-1, keepdims=True)
        inner = inner - normed * jnp.mean(e * normed, axis=-1, keepdims=True)
        cot_v[part, :] = (res[mine, :] + inner * scale).astype(LOW)
        gvec[0:1, :] += jnp.sum(grad * normed, axis=0, keepdims=True)
        gvec[1:2, :] += jnp.sum(grad, axis=0, keepdims=True)

    loop(8, norm_one_back)

    for e in range(16):
        svec[e, 0:8, :] = gvec[:, 128 * (e // 2) : 128 * (e // 2) + 128]
        svec[e, 8:16, :] = jnp.zeros((8, 128), F32)
    for j in range(8):
        svec[8 * t + j, 8:9, :] = gbup[:, 256 * j : 256 * j + 128]
        svec[8 * t + j, 9:10, :] = gbup[:, 256 * j + 128 : 256 * j + 256]
    tiles_send(5, lambda spot: svec.at[spot], svr)
    a2[0:256, :] = dot_nn(send_back, cot_v[...]).astype(LOW)
    rows_send(3, a2, backd)
    svr[d] = svec[d]
    rs_event(4, 2)
    rs_finish(1, keep_in(go_out))
    store(5, go_out).start()
    rs_finish(0, keep_heads(0))
    tiles_all(5, svr).wait_recv()
    small = jnp.zeros((16, 128), F32)
    for e in range(16):
        small = small + svr[e]
    sown[...] = small
    cross(8, sown, sown_r).start()
    rs_finish(4, keep_heads(256))
    for i, ref in enumerate((gq_out, gk_out, gv_out)):
        store(2 + i, ref).start()
    cross(8, sown, sown_r).wait_recv()
    small_out[...] = sown[...] + sown_r[...]
    store(8, small_out).start()
    ag_drain(0)
    ag_drain(1)
    rows_wait(3, a2, backd)
    cot_v[...] = dot_nn(take_back, backd[...]).astype(LOW)
    store(1, cot_v).start()

    for c in range(5):
        rs_drain(c)
    rows_drain(2, pcx, backy)
    rows_drain(3, a2, backd)
    tiles_all(4, vgat).wait_send()
    tiles_all(5, svr).wait_send()
    cross(0, xg.at[own], xg.at[own]).wait_send()
    cross(1, dyg.at[own], dyg.at[own]).wait_send()
    cross(4, pm.at[at(other, 256)], pmr).wait_send()
    for rb in range(2):
        rows = slice(rb * 256, rb * 256 + 256)
        cross(5 + rb, pd.at[rows], pdr.at[rows]).wait_send()
    cross(7, po.at[at(other, 256)], por.at[pl.ds(0, 256)]).wait_send()
    cross(8, sown, sown_r).wait_send()
    stored = (tok_v, cot_v, gq_out, gk_out, gv_out, go_out, gu_out, gd_out, small_out)
    for i, ref in enumerate(stored):
        store(i, ref).wait()


def settle_kernel(*refs):
    sources, small, homes, short = refs[:8], refs[8], refs[9:17], refs[17:26]
    held, in_sem, out_sem = refs[26:34], refs[34], refs[35]
    ins = [pltpu.make_async_copy(sources[i], held[i], in_sem.at[i]) for i in range(8)]
    outs = [pltpu.make_async_copy(held[i], homes[i], out_sem.at[i]) for i in range(8)]
    for copy in ins:
        copy.start()
    core = lax.rem(lax.axis_index("dp"), 2)
    for i in range(8):
        row = small[i : i + 1, :]
        short[i][...] = jnp.where(core == 0, row[:, 0:64], row[:, 64:128]).reshape(64)
    short[8][0:128] = small[8:9, :].reshape(128)
    short[8][128:256] = small[9:10, :].reshape(128)
    for i in range(8):
        ins[i].wait()
        outs[i].start()
    for copy in outs:
        copy.wait()


def fused_body(
    tokens,
    cotangent,
    norm1_gain,
    norm1_shift,
    w_query,
    b_query,
    w_key,
    w_value,
    b_value,
    w_out,
    b_out,
    norm2_gain,
    norm2_shift,
    w_up,
    b_up,
    w_down,
    b_down,
    lengths,
    deal_rank,
    arrival,
):
    def vm(*shape, dtype=LOW):
        return pltpu.VMEM(shape, dtype)

    def dma(*shape):
        return pltpu.SemaphoreType.DMA(shape)

    scratch = [
        vm(64, 512, dtype=F32),
        vm(64, 512, dtype=F32),
        vm(64, 512, dtype=F32),
        vm(64, 512, dtype=F32),
        vm(64, 2048, dtype=F32),
        vm(64, 2048, dtype=F32),
        vm(16, 128, dtype=F32),
        vm(16, 64, 1536),
        vm(16, 64, 512),
        vm(16, 64, 2048),
        vm(16, 64, 2048),
        vm(16, 64, 768),
        vm(16, 64, 768),
        vm(16, 64, 512),
        vm(16, 64, 2048),
        vm(16, 64, 2048),
        vm(16, 64, 2048),
        vm(256, 1024),
        vm(256, 1024),
        vm(256, 1024),
        vm(256, 1024),
        vm(256, 1024),
        vm(256, 1024),
        vm(256, 1024),
        vm(256, 1024),
        vm(512, 1024),
        vm(512, 1024),
        vm(512, 1024),
        vm(512, 1536),
        vm(1536, 512),
        vm(512, 512),
        vm(8, 1, 512, dtype=F32),
        vm(512, 1024),
        vm(512, 1024),
        vm(512, 1024, dtype=F32),
        vm(256, 1024, dtype=F32),
        vm(512, 128, dtype=F32),
        vm(512, 1024),
        vm(512, 2048),
        vm(512, 2048),
        vm(512, 1024),
        vm(256, 1024),
        vm(512, 1024),
        vm(512, 1024),
        vm(512, 1024),
        vm(512, 512),
        vm(512, 512),
        vm(512, 512, dtype=F32),
        vm(512, 512, dtype=F32),
        vm(1024, 512),
        vm(16, 16, 128, dtype=F32),
        vm(8, 1024, dtype=F32),
        vm(1, 1536, dtype=F32),
        vm(1, 2048, dtype=F32),
        vm(8, 1024, dtype=F32),
        vm(1, 2048, dtype=F32),
        vm(16, 16, 128, dtype=F32),
        vm(16, 16, 128, dtype=F32),
        vm(16, 128, dtype=F32),
        vm(16, 128, dtype=F32),
        vm(1, 512, dtype=jnp.int32),
        dma(8),
        dma(9),
        dma(4),
        dma(4, 2, 4),
        dma(4),
        dma(4),
        dma(6),
        dma(6),
        dma(9),
        dma(9),
        dma(5),
        dma(5, 2),
        dma(5),
        dma(5, 2, 4),
        dma(4),
        dma(5),
        pltpu.SemaphoreType.REGULAR,
        pltpu.SemaphoreType.REGULAR,
    ]
    anywhere = pl.BlockSpec(memory_space=pl.ANY)
    inside = pl.BlockSpec(memory_space=pltpu.VMEM)
    outs = (
        jax.ShapeDtypeStruct((256, 1024), LOW),
        jax.ShapeDtypeStruct((256, 1024), LOW),
        jax.ShapeDtypeStruct((64, 512), F32),
        jax.ShapeDtypeStruct((64, 512), F32),
        jax.ShapeDtypeStruct((64, 512), F32),
        jax.ShapeDtypeStruct((64, 512), F32),
        jax.ShapeDtypeStruct((64, 2048), F32),
        jax.ShapeDtypeStruct((64, 2048), F32),
        jax.ShapeDtypeStruct((16, 128), F32),
    )
    parts = pl.pallas_call(
        fused_kernel,
        name="fused_layer",
        out_shape=outs,
        in_specs=[anywhere] * 8 + [inside] * 11 + [pl.BlockSpec(memory_space=pltpu.SMEM)],
        out_specs=[anywhere] * 9,
        scratch_shapes=scratch,
        compiler_params=pltpu.CompilerParams(
            collective_id=0, has_side_effects=True, vmem_limit_bytes=67043328
        ),
    )(
        tokens,
        cotangent,
        w_query,
        w_key,
        w_value,
        w_out.T,
        w_up,
        w_down.T,
        norm1_gain,
        norm1_shift,
        b_query,
        b_value,
        b_out,
        norm2_gain,
        norm2_shift,
        b_down,
        b_up,
        deal_rank,
        arrival,
        lengths,
    )
    short = jax.ShapeDtypeStruct((64,), F32)
    finals = outs[:8] + (short,) * 8 + (jax.ShapeDtypeStruct((256,), F32),)
    done = pl.pallas_call(
        settle_kernel,
        name="settle",
        out_shape=finals,
        in_specs=[anywhere] * 8 + [inside],
        out_specs=[anywhere] * 8 + [inside] * 9,
        scratch_shapes=[vm(*out.shape, dtype=out.dtype) for out in outs[:8]] + [dma(8), dma(8)],
    )(*parts)
    result, grad_tokens, grad_q, grad_k, grad_v, grad_out, grad_up, grad_down = done[:8]
    gain_one, shift_one, bias_q, bias_v, bias_out, gain_two, shift_two, bias_down, bias_up = done[8:]
    return (
        result,
        grad_tokens,
        gain_one,
        shift_one,
        grad_q,
        bias_q,
        grad_k,
        grad_v,
        bias_v,
        grad_out.T,
        bias_out,
        gain_two,
        shift_two,
        grad_up,
        bias_up,
        grad_down.T,
        bias_down,
    )


def solution(mesh):
    in_specs = (
        P(("dp", "tensor"), None),
        P(("dp", "tensor"), None),
        P("dp"),
        P("dp"),
        P("dp", "tensor"),
        P("dp"),
        P("dp", "tensor"),
        P("dp", "tensor"),
        P("dp"),
        P("tensor", "dp"),
        P("dp"),
        P("dp"),
        P("dp"),
        P("dp", "tensor"),
        P("dp"),
        P("tensor", "dp"),
        P("dp"),
        P("dp", None),
        P("dp", "tensor", None),
        P("dp", "tensor", None),
    )
    out_specs = (
        P(("dp", "tensor"), None),
        P(("dp", "tensor"), None),
        P("dp"),
        P("dp"),
        P("dp", "tensor"),
        P("dp"),
        P("dp", "tensor"),
        P("dp", "tensor"),
        P("dp"),
        P("tensor", "dp"),
        P("dp"),
        P("dp"),
        P("dp"),
        P("dp", "tensor"),
        P("dp"),
        P("tensor", "dp"),
        P("dp"),
    )
    small_slice = mesh.shape["dp"] == 16 and mesh.shape["tensor"] == 2
    program = fused_body if small_slice else body
    return jax.shard_map(program, mesh=mesh, in_specs=in_specs, out_specs=out_specs, check_vma=False)
```

```python
import jax
import jax.numpy as jnp
from jax import lax
from jax.experimental import pallas as pl
from jax.experimental.pallas import tpu as pltpu
from jax.sharding import PartitionSpec as P

D = 1024
HEADS = 16
HEAD_DIM = 64
FF = 4096


EPSILON = 1e-05
GELU_SCALE = 0.7978845608028654


def layer_norm(values, norm_gain, norm_shift):
    center = values - jnp.mean(values, axis=-1, keepdims=True)
    spread = jnp.mean(center * center, axis=-1, keepdims=True)
    return center * lax.rsqrt(spread + EPSILON) * norm_gain + norm_shift


def gelu_tanh(values):
    return jax.nn.gelu(values, approximate=True)


def contract_rows(first_op, second_op):
    return lax.dot_general(
        first_op, second_op, (((0,), (0,)), ((), ())), preferred_element_type=jnp.float32
    )


def contract_cols(first_op, second_op):
    return lax.dot_general(
        first_op, second_op, (((1,), (1,)), ((), ())), preferred_element_type=jnp.float32
    )


def take_block(vector, block_index, block_size):
    return lax.dynamic_slice_in_dim(vector, block_index * block_size, block_size, 0).astype(
        jnp.float32
    )


def place_block(total_size, block_vec, block_index):
    holder = jnp.zeros((total_size,), jnp.float32)
    return lax.dynamic_update_slice_in_dim(holder, block_vec, block_index * block_vec.shape[0], 0)


def sequence_marks(seq_lengths, group_rows):
    seq_ends = jnp.cumsum(seq_lengths)
    seq_starts = seq_ends - seq_lengths
    row_ids = lax.iota(jnp.int32, group_rows)
    inside = (row_ids[:, None] >= seq_starts[None, :]) & (row_ids[:, None] < seq_ends[None, :])
    seq_index = lax.iota(jnp.int32, seq_lengths.shape[0])
    seq_ids = jnp.sum(jnp.where(inside, seq_index[None, :], 0), axis=1)
    seq_start = jnp.sum(jnp.where(inside, seq_starts[None, :], 0), axis=1)
    return (seq_ids, row_ids - seq_start, row_ids)


def body(
    tokens,
    cotangent,
    norm1_gain,
    norm1_shift,
    w_query,
    b_query,
    w_key,
    w_value,
    b_value,
    w_out,
    b_out,
    norm2_gain,
    norm2_shift,
    w_up,
    b_up,
    w_down,
    b_down,
    lengths,
    deal_rank,
    arrival,
):
    dp_count = lax.axis_size("dp")
    tensor_count = lax.axis_size("tensor")
    tensor_rank = lax.axis_index("tensor")
    tok_rows = tokens.shape[0]
    features = tokens.shape[1]
    piece_rows = tok_rows // dp_count
    group_rows = tok_rows * tensor_count
    sending_rank = deal_rank.reshape(tok_rows)
    deal_order = jnp.argsort(sending_rank)
    arrive_order = arrival.reshape(tok_rows)
    return_order = jnp.argsort(arrive_order)

    def relocate(first_part, second_part):
        return (
            lax.all_to_all(first_part, "dp", split_axis=0, concat_axis=0, tiled=True),
            lax.all_to_all(second_part, "dp", split_axis=0, concat_axis=0, tiled=True),
        )

    def to_pieces(row_data, row_order):
        return row_data[row_order].reshape(dp_count, piece_rows, features)

    moved_x, moved_dy = relocate(to_pieces(tokens, deal_order), to_pieces(cotangent, deal_order))
    local_x = moved_x.reshape(tok_rows, features)[arrive_order]
    local_dy = moved_dy.reshape(tok_rows, features)[arrive_order]
    part_rows = w_query.shape[0]
    head_cols = w_query.shape[1]
    hidden_cols = w_up.shape[1]
    vectors = (
        norm1_gain,
        norm1_shift,
        b_query,
        b_value,
        b_out,
        norm2_gain,
        norm2_shift,
        b_down,
    )
    up_wide = b_up.shape[0] // part_rows
    vec_cols = jnp.concatenate(
        [jnp.stack(vectors, axis=1), b_up.reshape(part_rows, up_wide)], axis=1
    )
    vec_cols = jnp.pad(vec_cols, ((0, 0), (0, 128 - vec_cols.shape[1])))
    packed = jnp.concatenate(
        [w_query, w_key, w_value, w_out.T, w_up, w_down.T, vec_cols], axis=1
    )
    packed_all = lax.all_gather(packed, "dp", axis=0, tiled=True)
    edges = [0, head_cols, 2 * head_cols, 3 * head_cols, 4 * head_cols]
    edges += [4 * head_cols + hidden_cols, 4 * head_cols + 2 * hidden_cols]
    query_cols, key_cols, value_cols, out_cols, up_cols, down_cols = (
        packed_all[:, edges[i] : edges[i + 1]] for i in range(6)
    )
    out_rows = out_cols.T
    down_rows = down_cols.T
    vec_all = packed_all[:, edges[6] :]
    (
        gain_one,
        shift_one,
        bias_query,
        bias_value,
        bias_out,
        gain_two,
        shift_two,
        bias_down,
    ) = (vec_all[:, i] for i in range(8))
    bias_up = vec_all[:, 8 : 8 + up_wide].reshape(-1)
    gain_one = gain_one.astype(jnp.float32)
    shift_one = shift_one.astype(jnp.float32)
    gain_two = gain_two.astype(jnp.float32)
    shift_two = shift_two.astype(jnp.float32)
    local_heads = head_cols // HEAD_DIM
    score_scale = HEAD_DIM ** (-0.5)
    query_bias = take_block(bias_query, tensor_rank, head_cols)
    value_bias = take_block(bias_value, tensor_rank, head_cols)
    up_bias = take_block(bias_up, tensor_rank, hidden_cols)
    x_rows = local_x.astype(jnp.float32)
    first_in = layer_norm(x_rows, gain_one, shift_one).astype(jnp.bfloat16)
    group_one = lax.all_gather(first_in, "tensor", axis=0, tiled=True)
    queries = (
        jnp.dot(group_one, query_cols, preferred_element_type=jnp.float32) + query_bias
    ).astype(jnp.bfloat16)
    queries = queries.reshape(group_rows, local_heads, HEAD_DIM)
    keyset = jnp.dot(group_one, key_cols, preferred_element_type=jnp.float32).astype(jnp.bfloat16)
    keyset = keyset.reshape(group_rows, local_heads, HEAD_DIM)
    valset = (
        jnp.dot(group_one, value_cols, preferred_element_type=jnp.float32) + value_bias
    ).astype(jnp.bfloat16)
    valset = valset.reshape(group_rows, local_heads, HEAD_DIM)
    head_ids = tensor_rank * local_heads + lax.iota(jnp.int32, local_heads)
    slopes = jnp.exp2(-8.0 * (head_ids.astype(jnp.float32) + 1.0) / HEADS)
    seq_ids, positions, row_ids = sequence_marks(lengths[0], group_rows)
    qblock = min(512, group_rows)
    blocks = group_rows // qblock
    block_starts = lax.iota(jnp.int32, blocks) * qblock

    def block_scores(row_start):
        query_rows = lax.dynamic_slice_in_dim(queries, row_start, qblock, 0)
        raw_scores = (
            jnp.einsum("qhd,khd->hqk", query_rows, keyset, preferred_element_type=jnp.float32)
            * score_scale
        )
        seq_rows = lax.dynamic_slice_in_dim(seq_ids, row_start, qblock, 0)
        pos_rows = lax.dynamic_slice_in_dim(positions, row_start, qblock, 0)
        row_rows = lax.dynamic_slice_in_dim(row_ids, row_start, qblock, 0)
        distance = (pos_rows[:, None] - positions[None, :]).astype(jnp.float32)
        allowed = (seq_rows[:, None] == seq_ids[None, :]) & (row_rows[:, None] >= row_ids[None, :])
        scores = jnp.where(
            allowed[None], raw_scores - slopes[:, None, None] * distance[None], -1e30
        )
        return (query_rows, scores)

    def attend(row_start):
        query_rows, scores = block_scores(row_start)
        row_max = jnp.max(scores, axis=-1, keepdims=True)
        exponent = jnp.exp(scores - row_max)
        row_total = jnp.sum(exponent, axis=-1, keepdims=True)
        attn_probs = (exponent / row_total).astype(jnp.bfloat16)
        mixed = jnp.einsum("hqk,khd->qhd", attn_probs, valset, preferred_element_type=jnp.float32)
        return (mixed, row_max[..., 0] + jnp.log(row_total[..., 0]))

    mixed_all, log_totals = lax.map(attend, block_starts)
    heads_out = mixed_all.reshape(group_rows, head_cols).astype(jnp.bfloat16)
    attn_out = lax.psum_scatter(
        jnp.dot(heads_out, out_rows, preferred_element_type=jnp.float32).astype(jnp.bfloat16),
        "tensor",
        scatter_dimension=0,
        tiled=True,
    ).astype(jnp.float32) + bias_out.astype(jnp.float32)
    residual = x_rows + attn_out
    second_in = layer_norm(residual, gain_two, shift_two).astype(jnp.bfloat16)
    grad_in = local_dy.astype(jnp.float32)
    down_bias_term = jnp.sum(grad_in, axis=0)
    group_two = lax.all_gather(second_in, "tensor", axis=0, tiled=True)
    pre_act = jnp.dot(group_two, up_cols, preferred_element_type=jnp.float32) + up_bias
    activated = gelu_tanh(pre_act).astype(jnp.bfloat16)
    mlp_out = lax.psum_scatter(
        jnp.dot(activated, down_rows, preferred_element_type=jnp.float32).astype(jnp.bfloat16),
        "tensor",
        scatter_dimension=0,
        tiled=True,
    ).astype(jnp.float32)
    result = residual + mlp_out + bias_down.astype(jnp.float32)
    group_dy = lax.all_gather(local_dy, "tensor", axis=0, tiled=True)
    grad_down = contract_rows(activated, group_dy)
    grad_act = contract_cols(group_dy, down_rows)
    gelu_pull = jax.vjp(gelu_tanh, pre_act)[1]
    grad_pre = gelu_pull(grad_act)[0].astype(jnp.bfloat16)
    grad_up = contract_rows(group_two, grad_pre)
    up_bias_term = place_block(FF, jnp.sum(grad_pre, axis=0, dtype=jnp.float32), tensor_rank)
    grad_two = lax.psum_scatter(
        contract_cols(grad_pre, up_cols).astype(jnp.bfloat16),
        "tensor",
        scatter_dimension=0,
        tiled=True,
    ).astype(jnp.float32)
    result_low = result.astype(jnp.bfloat16)
    norm_two_pull = jax.vjp(layer_norm, residual, gain_two, shift_two)[1]
    grad_res_norm, gain_two_term, shift_two_term = norm_two_pull(grad_two)
    grad_resid = grad_in + grad_res_norm
    grad_attn = grad_resid.astype(jnp.bfloat16)
    out_bias_term = jnp.sum(grad_attn, axis=0, dtype=jnp.float32)
    group_grad = lax.all_gather(grad_attn, "tensor", axis=0, tiled=True)
    grad_out = contract_rows(heads_out, group_grad)
    grad_heads = (
        contract_cols(group_grad, out_rows)
        .astype(jnp.bfloat16)
        .reshape(group_rows, local_heads, HEAD_DIM)
    )

    def attend_back(running, block_item):
        key_accum, value_accum = running
        row_start, log_total = block_item
        query_rows, scores = block_scores(row_start)
        attn_probs = jnp.exp(scores - log_total[..., None])
        grad_rows = lax.dynamic_slice_in_dim(grad_heads, row_start, qblock, 0)
        grad_probs = jnp.einsum(
            "qhd,khd->hqk", grad_rows, valset, preferred_element_type=jnp.float32
        )
        row_dot = jnp.sum(attn_probs * grad_probs, axis=-1, keepdims=True)
        grad_scores = (attn_probs * (grad_probs - row_dot)).astype(jnp.bfloat16)
        grad_query_rows = jnp.einsum(
            "hqk,khd->qhd", grad_scores, keyset, preferred_element_type=jnp.float32
        )
        grad_query_rows = (grad_query_rows * score_scale).astype(jnp.bfloat16)
        key_accum = (
            key_accum
            + jnp.einsum(
                "hqk,qhd->khd", grad_scores, query_rows, preferred_element_type=jnp.float32
            )
            * score_scale
        )
        value_accum = value_accum + jnp.einsum(
            "hqk,qhd->khd",
            attn_probs.astype(jnp.bfloat16),
            grad_rows,
            preferred_element_type=jnp.float32,
        )
        return ((key_accum, value_accum), grad_query_rows)

    zero_heads = jnp.zeros((group_rows, local_heads, HEAD_DIM), jnp.float32)
    (key_accum, value_accum), grad_query_blocks = lax.scan(
        attend_back, (zero_heads, zero_heads), (block_starts, log_totals)
    )
    grad_query = grad_query_blocks.reshape(group_rows, head_cols)
    grad_key = key_accum.reshape(group_rows, head_cols).astype(jnp.bfloat16)
    grad_value = value_accum.reshape(group_rows, head_cols).astype(jnp.bfloat16)
    query_bias_term = place_block(D, jnp.sum(grad_query, axis=0, dtype=jnp.float32), tensor_rank)
    value_bias_term = place_block(D, jnp.sum(grad_value, axis=0, dtype=jnp.float32), tensor_rank)
    grad_wquery = contract_rows(group_one, grad_query)
    grad_wkey = contract_rows(group_one, grad_key)
    grad_wvalue = contract_rows(group_one, grad_value)
    grad_one = lax.psum_scatter(
        (
            contract_cols(grad_query, query_cols)
            + contract_cols(grad_key, key_cols)
            + contract_cols(grad_value, value_cols)
        ).astype(jnp.bfloat16),
        "tensor",
        scatter_dimension=0,
        tiled=True,
    ).astype(jnp.float32)
    norm_one_pull = jax.vjp(layer_norm, x_rows, gain_one, shift_one)[1]
    grad_x_norm, gain_one_term, shift_one_term = norm_one_pull(grad_one)
    grad_tokens = (grad_resid + grad_x_norm).astype(jnp.bfloat16)
    small_terms = jnp.stack(
        (
            gain_one_term,
            shift_one_term,
            query_bias_term,
            value_bias_term,
            out_bias_term,
            gain_two_term,
            shift_two_term,
            down_bias_term,
        ),
        axis=1,
    )
    small_terms = jnp.concatenate([small_terms, up_bias_term.reshape(-1, up_wide)], axis=1)
    small_terms = jnp.pad(small_terms, ((0, 0), (0, 128 - small_terms.shape[1])))
    terms = (grad_wquery, grad_wkey, grad_wvalue, grad_out.T, grad_up, grad_down.T, small_terms)
    packed_grads = jnp.concatenate([term.astype(jnp.bfloat16) for term in terms], axis=1)
    reduced = lax.psum_scatter(packed_grads, "dp", scatter_dimension=0, tiled=True).astype(
        jnp.float32
    )
    shards = [reduced[:, edges[i] : edges[i + 1]] for i in range(6)]
    shards[3] = shards[3].T
    shards[5] = shards[5].T
    sums = lax.psum(reduced[:, edges[6] : edges[6] + 8 + up_wide], "tensor")
    smalls = [sums[:, i] for i in range(7)] + [sums[:, 8:].reshape(-1), sums[:, 7]]
    back_y, back_dx = relocate(
        to_pieces(result_low, return_order), to_pieces(grad_tokens, return_order)
    )
    given_y = back_y.reshape(tok_rows, features)[sending_rank]
    given_dx = back_dx.reshape(tok_rows, features)[sending_rank]
    return (
        given_y,
        given_dx,
        smalls[0],
        smalls[1],
        shards[0],
        smalls[2],
        shards[1],
        shards[2],
        smalls[3],
        shards[3],
        smalls[4],
        smalls[5],
        smalls[6],
        shards[4],
        smalls[7],
        shards[5],
        smalls[8],
    )


MESH = pl.DeviceIdType.MESH
F32 = jnp.float32
LOW = jnp.bfloat16
RING = 8
PAIR = 128


def dot_nn(first_op, second_op):
    return lax.dot_general(
        first_op, second_op, (((1,), (0,)), ((), ())), preferred_element_type=F32
    )


def dot_nt(first_op, second_op):
    return lax.dot_general(
        first_op, second_op, (((1,), (1,)), ((), ())), preferred_element_type=F32
    )


def loop(count, step):
    def run(i, carry):
        step(i)
        return carry

    lax.fori_loop(0, count, run, 0)


def at(index, size):
    return pl.ds(pl.multiple_of(index * size, size), size)


def fused_kernel(
    tok_ref,
    cot_ref,
    wq_ref,
    wk_ref,
    wv_ref,
    wot_ref,
    wup_ref,
    wdt_ref,
    *refs,
):
    vectors, refs = refs[:9], refs[9:]
    rank_ref, arrive_ref, len_ref = refs[:3]
    homes, refs = refs[3:12], refs[12:]
    little, refs = refs[:11], refs[11:]
    fused_layer(
        (tok_ref, cot_ref, wq_ref, wk_ref, wv_ref, wot_ref, wup_ref, wdt_ref),
        vectors + (rank_ref, arrive_ref),
        little,
        len_ref,
        homes,
        *refs,
    )


def fused_layer(
    given,
    far_little,
    little,
    len_ref,
    homes,
    gq_out,
    gk_out,
    gv_out,
    go_out,
    gu_out,
    gd_out,
    small_out,
    wqkv,
    wo,
    wu,
    wd,
    ga,
    gb,
    go,
    gu,
    gd,
    land,
    tok_v,
    cot_v,
    pcx,
    pcd,
    arrx,
    arrd,
    backy,
    backd,
    xg,
    dyg,
    a1,
    qkv,
    qkvt,
    ho,
    lse,
    po,
    por,
    res,
    yb,
    rstd,
    a2,
    act,
    dpre,
    pm,
    pmr,
    pd,
    pdr,
    dattn,
    dh,
    dht,
    dk_acc,
    dv_acc,
    tbuf,
    vgat,
    vrow,
    bqkv,
    bup,
    gvec,
    gbup,
    svec,
    svr,
    sown,
    sown_r,
    start_row,
    ld,
    st,
    ag_s,
    ag_r,
    mt_s,
    mt_r,
    aa_s,
    aa_r,
    y_s,
    y_r,
    rm_s,
    rm_r,
    rr_s,
    rr_r,
    ax_r,
    rx_r,
    ready_one,
    ready_two,
):
    tok_ref, cot_ref, wq_ref, wk_ref, wv_ref, wot_ref, wup_ref, wdt_ref = given
    vectors, rank_ref, arrive_ref = little[:9], little[9], little[10]
    d = lax.axis_index("dp")
    t = lax.axis_index("tensor")
    other = 1 - t
    core = lax.rem(d, 2)
    chip = lax.div(d, 2)
    xc = lax.rem(chip, 2)
    zc = lax.div(chip, 2)
    p = zc + xc * (7 - 2 * zc)

    def chip_at(pos):
        pos = lax.rem(pos + 2 * RING, RING)
        xx = lax.div(pos, 4)
        zz = pos + xx * (7 - 2 * pos)
        return zz * 2 + xx

    def dev(pos):
        return chip_at(pos) * 2 + core

    def mdev(pos):
        return chip_at(pos) * 2 + 1 - core

    def outer(pos):
        spot = lax.rem(pos + 2 * RING, 4)
        return (spot == 0) | (spot == 3)

    inner = ~outer(p)
    even = lax.rem(p, 2) == 0
    over = dev(7 - p)
    mate = d + 1 - 2 * core
    sides = (dev(p + 1), dev(p - 1))
    weights = (wqkv, wo, wu, wu, wd, wd)
    firsts = (0, 0, 0, 1024, 0, 1024)
    spans = (1536, 512, 1024, 1024, 1024, 1024)
    grads = (ga, go, gu, gd, gb, gu, gd)
    starts_at = (0, 0, 0, 0, 0, 1024, 1024)
    widths = (768, 512, 1024, 1024, 768, 1024, 1024)
    landing = (wd, wd, wu, land, wd, wu, land)
    offsets = (0, 1536, 0, 0, 768, 1024, 1024)
    dqkv = act

    def remote(src, dst, send, recv, device):
        return pltpu.make_async_remote_copy(
            src_ref=src,
            dst_ref=dst,
            send_sem=send,
            recv_sem=recv,
            device_id=device,
            device_id_type=MESH,
        )

    def signal(sem, device):
        pl.semaphore_signal(sem, inc=1, device_id=device, device_id_type=MESH)

    loads = [
        pltpu.make_async_copy(tok_ref, tok_v, ld.at[0]),
        pltpu.make_async_copy(cot_ref, cot_v, ld.at[1]),
        pltpu.make_async_copy(wq_ref, wqkv.at[d, :, pl.ds(0, 512)], ld.at[2]),
        pltpu.make_async_copy(wk_ref, wqkv.at[d, :, pl.ds(512, 512)], ld.at[3]),
        pltpu.make_async_copy(wv_ref, wqkv.at[d, :, pl.ds(1024, 512)], ld.at[4]),
        pltpu.make_async_copy(wot_ref, wo.at[d], ld.at[5]),
        pltpu.make_async_copy(wup_ref, wu.at[d], ld.at[6]),
        pltpu.make_async_copy(wdt_ref, wd.at[d], ld.at[7]),
    ]
    for i in range(2):
        loads[i].start()
    fetches = [
        pltpu.make_async_copy(far_little[i], little[i], ld.at[9 + i]) for i in range(11)
    ]
    for fetch in fetches:
        fetch.start()
    for i in range(2, 8):
        loads[i].start()
    barrier = pltpu.get_barrier_semaphore()

    def store(i, src):
        return pltpu.make_async_copy(src, homes[i], st.at[i])

    def greet(k):
        signal(barrier, {"dp": lax.rem(d + k + 1, 16)})

    loop(15, greet)
    signal(barrier, {"tensor": other})

    def rows_send(kind, src, dst, low=0, high=15):
        def step(k):
            spot = lax.rem(d + low + k + 1, 16)
            remote(
                src.at[at(spot, 16)],
                dst.at[at(d, 16)],
                aa_s.at[kind],
                aa_r.at[kind],
                {"dp": spot},
            ).start()

        loop(high - low, step)
        if low == 0:
            dst[at(d, 16), :] = src[at(d, 16), :]

    def rows_all(kind, src, dst):
        bulk = pl.ds(0, 240)
        return remote(src.at[bulk], dst.at[bulk], aa_s.at[kind], aa_r.at[kind], {"dp": mate})

    def rows_wait(kind, src, dst):
        rows_all(kind, src, dst).wait_recv()

    def rows_drain(kind, src, dst):
        rows_all(kind, src, dst).wait_send()

    def tiles_send(kind, src_of, dst):
        def step(k):
            spot = lax.rem(d + k + 1, 16)
            remote(src_of(spot), dst.at[d], aa_s.at[kind], aa_r.at[kind], {"dp": spot}).start()

        loop(15, step)

    def tiles_all(kind, dst):
        bulk = dst.at[pl.ds(0, 15)]
        return remote(bulk, bulk, aa_s.at[kind], aa_r.at[kind], {"dp": mate})

    def cross(i, src, dst):
        return remote(src, dst, y_s.at[i], y_r.at[i], {"tensor": other})

    def shard(c, slot, rows=pl.ds(0, 64)):
        return weights[c].at[slot, rows, pl.ds(firsts[c], spans[c])]

    def ring_part(c, slot, way, step):
        if step == 3:
            return shard(c, slot, pl.ds(32 * way, 32))
        return shard(c, slot)

    def turn(way, steps):
        return p - steps if way == 0 else p + steps

    def ag_copy(c, way, step):
        part = ring_part(c, dev(turn(way, step)), way, step)
        return remote(
            part, part, ag_s.at[c], ag_r.at[c, way, step], {"dp": sides[way]}
        )

    def ag_arrival(c, way, step):
        part = ring_part(c, dev(turn(way, step + 1)), way, step)
        return remote(
            part, part, ag_s.at[c], ag_r.at[c, way, step], {"dp": sides[way]}
        )

    def mate_copy(c, k, place):
        if k == 0:
            part = shard(c, place(p))
        else:
            way, step = (k - 1) // 4, (k - 1) % 4
            part = ring_part(c, place(turn(way, step + 1)), way, step)
        return remote(part, part, mt_s.at[c], mt_r.at[c], {"dp": mate})

    def ag_start(c):
        for way in range(2):
            ag_copy(c, way, 0).start()
        mate_copy(c, 0, dev).start()

    def ag_over(c):
        part = shard(c, dev(jnp.where(even, p - 1, p + 1)))
        return remote(part, part, ag_s.at[c], ax_r.at[c], {"dp": over})

    def ag_event(c, step):
        if step == 3:

            @pl.when(inner)
            def _():
                part = shard(c, dev(p + 4))
                remote(part, part, ag_s.at[c], ax_r.at[c], {"dp": over}).wait_recv()

        for way in range(2):
            if step == 3:

                @pl.when(outer(p))
                def _():
                    ag_arrival(c, way, step).wait_recv()

            else:
                ag_arrival(c, way, step).wait_recv()
            if step == 2:

                @pl.when(outer(turn(1 - way, 1)))
                def _():
                    ag_copy(c, way, 3).start()

            elif step < 2:
                ag_copy(c, way, step + 1).start()
            mate_copy(c, 1 + 4 * way + step, dev).start()
        if step == 0:

            @pl.when(inner)
            def _():
                ag_over(c).start()

    def mate_all(c):
        bulk = weights[c].at[pl.ds(0, 8), pl.ds(0, 64), pl.ds(firsts[c], spans[c])]
        return remote(bulk, bulk, mt_s.at[c], mt_r.at[c], {"dp": mate})

    def ag_finish(c):
        mate_all(c).wait_recv()

    def ag_drain(c):
        def sent(halves):
            bulk = weights[c].at[pl.ds(0, halves), pl.ds(0, 32), pl.ds(firsts[c], spans[c])]
            remote(bulk, bulk, ag_s.at[c], ag_r.at[c, 0, 0], {"dp": over}).wait_send()

        pl.when(inner)(lambda: sent(15))
        pl.when(outer(p))(lambda: sent(13))
        mate_all(c).wait_send()

    def inbox(c, slot, rows=pl.ds(0, 64)):
        return landing[c].at[slot, rows, pl.ds(offsets[c], widths[c])]

    def arrived(c, slot, rows):
        return landing[c][slot, rows, offsets[c] : offsets[c] + widths[c]].astype(F32)

    halves = (1 - lax.div(zc, 2), lax.div(zc, 2))

    def rm_send(c, half):
        for i in range(4):
            spot = half * 4 + i
            remote(
                owed(c, spot * 2 + 1 - core),
                inbox(c, spot),
                rm_s.at[c],
                rm_r.at[c, half],
                {"dp": mate},
            ).start()

    def rm_wait(c, half):
        bulk = landing[c].at[pl.ds(half * 4, 4), pl.ds(0, 64), pl.ds(offsets[c], widths[c])]
        remote(bulk, bulk, rm_s.at[c], rm_r.at[c, half], {"dp": mate}).wait_recv()

    def owed(c, slot, rows=pl.ds(0, 64)):
        return grads[c].at[slot, rows, pl.ds(starts_at[c], widths[c])]

    def rs_copy(c, way, step):
        dest = dev(p + 4 - step if way == 0 else p - 4 + step)
        slot = 8 + way * 4 + step
        if step == 0:
            half = pl.ds(32 * way, 32)
            src, dst = owed(c, dest, half), inbox(c, slot, half)
        else:
            src, dst = owed(c, dest), inbox(c, slot)
        return remote(src, dst, rr_s.at[c], rr_r.at[c, way, step], {"dp": sides[way]})

    def rs_add(c, slot, rows, boxes):
        total = grads[c][slot, rows, starts_at[c] : starts_at[c] + widths[c]].astype(F32)
        for box in boxes:
            total += arrived(c, box, rows)
        return total

    def rs_over(c, slot):
        return remote(
            owed(c, dev(p + 4)), inbox(c, slot), rr_s.at[c], rx_r.at[c], {"dp": over}
        )

    def rs_fold(c, slot, first, count, boxes):
        def add(i):
            rows = at(i + first, 16)
            total = rs_add(c, slot, rows, boxes).astype(LOW)
            grads[c][slot, rows, starts_at[c] : starts_at[c] + widths[c]] = total

        loop(count, add)

    def rs_start(c):
        far = chip_at(p + 4)
        rm_wait(c, halves[0])
        rs_fold(c, far * 2 + core, 0, 4, (far,))

        @pl.when(outer(p))
        def _():
            for way in range(2):
                rs_copy(c, way, 0).start()

        @pl.when(inner)
        def _():
            rs_over(c, jnp.where(even, 12, 8)).start()

    def rs_event(c, step):
        if step == 2:

            @pl.when(inner)
            def _():
                box = jnp.where(even, 8, 12)
                rs_over(c, box).wait_recv()
                rs_fold(c, dev(jnp.where(even, p - 1, p + 1)), 0, 4, (box,))

        for way in range(2):
            pos = p + 3 - step if way == 0 else p - 3 + step
            spot = chip_at(pos)
            slot = spot * 2 + core
            box = 8 + way * 4 + step
            if step == 0 and way == 0:
                rm_wait(c, halves[1])
            if step == 0:

                @pl.when(outer(pos))
                def _():
                    rs_copy(c, way, 0).wait_recv()
                    rs_fold(c, slot, 2 * way, 2, (spot, box))
                    rs_fold(c, slot, 2 - 2 * way, 2, (spot,))

                @pl.when(~outer(pos))
                def _():
                    rs_fold(c, slot, 0, 4, (spot,))

            else:
                rs_copy(c, way, step).wait_recv()
                rs_fold(c, slot, 0, 4, (spot, box))
            rs_copy(c, way, step + 1).start()

    def rs_finish(c, keep):
        for way in range(2):
            rs_copy(c, way, 3).wait_recv()

        def add(i):
            rows = at(i, 16)
            keep(rows, rs_add(c, d, rows, (chip, 11, 15)))

        loop(4, add)

    def keep_in(ref, first=0):
        def keep(rows, total):
            ref[rows, first : first + total.shape[1]] = total

        return keep

    def keep_heads(first):
        def keep(rows, total):
            for j, ref in enumerate((gq_out, gk_out, gv_out)):
                ref[rows, first : first + 256] = total[:, 256 * j : 256 * j + 256]

        return keep

    def rs_drain(c):
        columns = pl.ds(starts_at[c], widths[c])
        sent = grads[c].at[pl.ds(0, 7), pl.ds(0, 64), columns]
        remote(sent, sent, rr_s.at[c], rr_r.at[c, 0, 1], {"dp": over}).wait_send()
        sent = grads[c].at[pl.ds(0, 8), pl.ds(0, 64), columns]
        remote(sent, sent, rm_s.at[c], rm_r.at[c, 0], {"dp": mate}).wait_send()

    def free_for_reduction(sem):
        signal(sem, {"dp": mate})
        for side in sides:
            signal(sem, {"dp": side})

        @pl.when(inner)
        def _():
            signal(sem, {"dp": over})

    def others_free(sem):
        pl.when(inner)(lambda: pl.semaphore_wait(sem, 4))
        pl.when(outer(p))(lambda: pl.semaphore_wait(sem, 3))

    def picks(ref):
        slots = lax.broadcasted_iota(jnp.int32, (256, 256), 0)
        return jnp.where(slots == ref[0, :, :], 1.0, 0.0)

    for fetch in fetches:
        fetch.wait()
    zeros = jnp.zeros((1, 64), F32)
    for i in range(8):
        row = vectors[i][...].astype(F32).reshape(1, 64)
        early = jnp.concatenate([row, zeros], axis=1)
        late = jnp.concatenate([zeros, row], axis=1)
        vgat[d, i : i + 1, :] = jnp.where(core == 0, early, late)
    row = vectors[8][...].astype(F32).reshape(1, 256)
    vgat[d, 8:9, :] = row[:, 0:128]
    vgat[d, 9:10, :] = row[:, 128:256]
    vgat[d, 10:16, :] = jnp.zeros((6, 128), F32)
    loads[0].wait()
    spread = picks(rank_ref).astype(LOW)
    pcx[...] = dot_nn(spread, tok_v[...]).astype(LOW)
    pl.semaphore_wait(barrier, 16)
    rows_send(0, pcx, arrx)
    tiles_send(4, lambda spot: vgat.at[d], vgat)
    for i in range(2, 6):
        loads[i].wait()
    ag_start(0)
    ag_start(1)
    loads[1].wait()
    pcd[...] = dot_nn(spread, cot_v[...]).astype(LOW)
    for i in range(6, 8):
        loads[i].wait()

    own = at(t, 256)
    gather_rows = picks(arrive_ref).T.astype(LOW)
    rows_wait(0, pcx, arrx)
    xg[own, :] = dot_nn(gather_rows, arrx[...]).astype(LOW)
    cross(0, xg.at[own], xg.at[own]).start()
    ag_event(0, 0)
    ag_event(1, 0)

    tiles_all(4, vgat).wait_recv()
    for m in range(8):
        both = vgat[2 * m, :, :] + vgat[2 * m + 1, :, :]
        vrow[:, 128 * m : 128 * (m + 1)] = both[0:8, :]
    for j in range(8):
        block = vgat[8 * t + j, :, :]
        bup[:, 256 * j : 256 * j + 128] = block[8:9, :]
        bup[:, 256 * j + 128 : 256 * j + 256] = block[9:10, :]
    bqkv[:, 0:512] = vrow[2:3, at(t, 512)]
    bqkv[:, 512:1024] = jnp.zeros((1, 512), F32)
    bqkv[:, 1024:1536] = vrow[3:4, at(t, 512)]
    ends = jnp.int32(0)
    row_ids = lax.broadcasted_iota(jnp.int32, (1, 512), 1)
    starts = jnp.zeros((1, 512), jnp.int32)
    for i in range(3):
        ends = ends + len_ref[0, i]
        starts = jnp.where(row_ids >= ends, ends, starts)
    start_row[...] = starts
    gvec[...] = jnp.zeros((8, 1024), F32)

    def stats(values):
        center = values - jnp.mean(values, axis=-1, keepdims=True)
        spread_of = jnp.mean(center * center, axis=-1, keepdims=True)
        scale = lax.rsqrt(spread_of + EPSILON)
        return center * scale, scale

    def norm_one(half):
        def step(i):
            rows = at(half * 8 + i, 32)
            normed, _ = stats(xg[rows, :].astype(F32))
            a1[rows, :] = (normed * vrow[0:1, :] + vrow[1:2, :]).astype(LOW)

        loop(8, step)

    norm_one(t)
    ag_event(0, 1)
    ag_event(1, 1)
    cross(0, xg.at[own], xg.at[at(other, 256)]).wait_recv()
    norm_one(other)
    ag_event(0, 2)
    ag_event(1, 2)
    ag_start(2)
    ag_start(3)
    rows_send(1, pcd, arrd, 0, 5)
    ag_event(0, 3)
    ag_event(1, 3)
    ag_finish(0)

    def project(i):
        cols = at(i, 256)
        value = dot_nn(a1[...], wqkv[:, :, cols].reshape(1024, 256)) + bqkv[:, cols]
        low = value.astype(LOW).astype(F32)
        qkv[:, cols] = low.astype(LOW)
        qkvt[cols, :] = low.T.astype(LOW)

    loop(6, project)
    rows_send(1, pcd, arrd, 5, 10)

    def slope_of(pair, half):
        head = (t * 8 + pair * 2 + half + 1).astype(F32)
        return jnp.exp2(jnp.full((1, PAIR), -0.5, F32) * head)

    def padded(block, half):
        zero = jnp.zeros_like(block)
        return jnp.concatenate([block, zero] if half == 0 else [zero, block], axis=0)

    def band(qb):
        first = max(0, qb - 2) * 128
        width = (qb + 1) * 128 - first
        keys = lax.broadcasted_iota(jnp.int32, (width, PAIR), 0) + first
        rows = lax.broadcasted_iota(jnp.int32, (width, PAIR), 1) + qb * 128
        allowed = (keys <= rows) & (keys >= start_row[:, qb * 128 : qb * 128 + 128])
        return first, width, allowed, (rows - keys).astype(F32)

    def score(pair, half, qb, first, width, allowed, distance):
        key_rows = qkv[first : first + width, at(pair + 4, PAIR)]
        query = qkvt[at(pair * 2 + half, 64), qb * 128 : qb * 128 + 128] * 0.125
        raw = dot_nn(key_rows, padded(query, half))
        return jnp.where(allowed, raw - slope_of(pair, half) * distance, -1e30)

    def attend(qbs, first_pair, count):
        def step(index):
            pair = index + first_pair
            for qb in qbs:
                first, width, allowed, distance = band(qb)
                parts = []
                for half in range(2):
                    s = score(pair, half, qb, first, width, allowed, distance)
                    top = jnp.max(s, axis=0, keepdims=True)
                    e = jnp.exp(s - top)
                    total = jnp.sum(e, axis=0, keepdims=True)
                    probs = (e * (1.0 / total)).astype(LOW)
                    lse[pair * 2 + half, :, qb * 128 : qb * 128 + 128] = top + jnp.log(total)
                    value_t = qkvt[at(16 + pair * 2 + half, 64), first : first + width]
                    parts.append(dot_nn(value_t, probs))
                ho[qb * 128 : qb * 128 + 128, at(pair, PAIR)] = (
                    jnp.concatenate(parts, axis=0).T.astype(LOW)
                )

        loop(count, step)

    def out_project(rb):
        rows = slice(rb * 256, rb * 256 + 256)

        def step(i):
            po[rows, at(i, 256)] = dot_nt(ho[rows, :], wo[pl.ds(i * 4, 4)].reshape(256, 512)).astype(LOW)

        loop(4, step)
        cross(2 + rb, po.at[rows], por.at[rows]).start()

    attend((0, 1), 0, 4)
    ag_finish(1)
    out_project(0)
    ag_event(2, 0)
    attend((2, 3), 0, 2)
    ag_event(3, 0)
    attend((2, 3), 2, 2)
    out_project(1)
    rows_send(1, pcd, arrd, 10, 15)
    ag_event(2, 1)
    ag_event(3, 1)
    ag_start(4)
    ag_event(2, 2)
    ag_start(5)
    rows_wait(1, pcd, arrd)
    own_dy = dot_nn(gather_rows, arrd[...])
    dyg[own, :] = own_dy.astype(LOW)
    gvec[7:8, :] = jnp.sum(own_dy, axis=0, keepdims=True)
    cross(1, dyg.at[own], dyg.at[own]).start()
    ag_event(3, 2)
    ag_event(4, 0)
    ag_event(2, 3)

    def mlp_enter(rb):
        rows = slice(rb * 256, rb * 256 + 256)
        cross(2 + rb, po.at[rows], por.at[rows]).wait_recv()

        def enter(i):
            part = at(rb * 8 + i, 32)
            value = xg[part, :].astype(F32) + (po[part, :].astype(F32) + por[part, :].astype(F32))
            value = value + vrow[4:5, :]

            @pl.when(t == rb)
            def _():
                yb[at(i, 32), :] = value

            normed, scale = stats(value)
            res[part, :] = normed
            rstd[part, :] = jnp.broadcast_to(scale, (32, 128))
            a2[part, :] = (normed * vrow[5:6, :] + vrow[6:7, :]).astype(LOW)

        loop(8, enter)

    def up(i):
        cols = at(i, 256)
        v = dot_nn(a2[...], wu[:, :, cols].reshape(1024, 256)) + bup[:, cols]
        square = v * v
        bend = jnp.tanh(GELU_SCALE * (v + 0.044715 * (square * v)))
        half_v = 0.5 * v
        both = 1.0 + bend
        act[:, cols] = (half_v * both).astype(LOW)
        slope = 0.5 * both + (half_v * (1.0 - bend * bend)) * (
            GELU_SCALE + (GELU_SCALE * 3.0 * 0.044715) * square
        )
        dpre[:, cols] = slope.astype(LOW)

    def act_back(i):
        cols = at(i, 256)
        grad = dot_nn(dyg[...], wd[:, :, cols].reshape(1024, 256))
        back = (grad * dpre[:, cols].astype(F32)).astype(LOW)
        dpre[:, cols] = back
        gbup[:, cols] = jnp.sum(back.astype(F32), axis=0, keepdims=True)

    def mlp_back(rb):
        rows = slice(rb * 256, rb * 256 + 256)

        def down(i):
            pd[rows, at(i, 256)] = dot_nt(dpre[rows, :], wu[pl.ds(i * 4, 4)].reshape(256, 2048)).astype(LOW)

        loop(4, down)
        cross(5 + rb, pd.at[rows], pdr.at[rows]).start()

    def mlp_out(i):
        pm[:, at(i, 256)] = dot_nt(act[...], wd[pl.ds(i * 4, 4)].reshape(256, 2048)).astype(LOW)

    def flip(ref):
        def step(i):
            tbuf[at(i, 256), :] = ref[:, at(i, 256)].T

        loop(4, step)

    def plain(ref, first=0):
        return lambda j: ref[:, at(j + first, 512)]

    def weight_grad(c, second, count, wide):
        def half_grad(half):
            rows = at(half, 512)

            def inner(j):
                grads[c][pl.ds(half * 8, 8), :, at(j + starts_at[c] // wide, wide)] = (
                    dot_nn(tbuf[rows, :], second(j)).astype(LOW).reshape(8, 64, wide)
                )

            loop(count, inner)
            rm_send(c, half)

        half_grad(halves[0])
        rs_start(c)
        half_grad(halves[1])

    mlp_enter(0)
    mlp_enter(1)
    ag_event(5, 0)
    ag_finish(2)
    loop(4, up)
    ag_event(4, 1)
    ag_event(3, 3)
    ag_finish(3)
    loop(4, lambda i: up(i + 4))
    ag_event(5, 1)
    cross(1, dyg.at[own], dyg.at[at(other, 256)]).wait_recv()
    flip(dyg)
    weight_grad(3, plain(act), 2, 512)
    ag_event(4, 2)
    ag_event(5, 2)
    weight_grad(6, plain(act, 2), 2, 512)
    ag_event(4, 3)
    ag_event(5, 3)
    ag_finish(4)
    ag_finish(5)
    rs_event(3, 0)
    loop(8, act_back)
    rs_event(6, 0)
    mlp_back(0)
    mlp_back(1)
    rs_event(3, 1)
    for c in range(2, 4):
        ag_drain(c)
    free_for_reduction(ready_one)
    loop(4, mlp_out)
    for c in range(4, 6):
        ag_drain(c)
    free_for_reduction(ready_two)
    others_free(ready_one)
    flip(a2)
    weight_grad(2, plain(dpre), 2, 512)
    rs_event(6, 1)

    rs_event(3, 2)
    weight_grad(5, plain(dpre, 2), 2, 512)
    rs_event(6, 2)

    def norm_two_back(rb):
        rows = slice(rb * 256, rb * 256 + 256)
        cross(5 + rb, pd.at[rows], pdr.at[rows]).wait_recv()

        def step(i):
            part = at(rb * 8 + i, 32)
            grad = pd[part, :].astype(F32) + pdr[part, :].astype(F32)
            normed, scale = res[part, :], rstd[part, 0:1]
            e = grad * vrow[5:6, :]
            inner = e - jnp.mean(e, axis=-1, keepdims=True)
            inner = inner - normed * jnp.mean(e * normed, axis=-1, keepdims=True)
            dy = dyg[part, :].astype(F32)
            full = dy + inner * scale
            res[part, :] = full
            low = full.astype(LOW)
            dattn[part, :] = low
            gvec[4:5, :] += 0.5 * jnp.sum(low.astype(F32), axis=0, keepdims=True)
            gvec[5:6, :] += 0.5 * jnp.sum(grad * normed, axis=0, keepdims=True)
            gvec[6:7, :] += 0.5 * jnp.sum(grad, axis=0, keepdims=True)

        loop(8, step)

        def heads(i):
            cols = at(i, 256)
            value = dot_nn(dattn[rows, :], wo[:, :, cols].reshape(1024, 256)).astype(LOW)
            dh[rows, cols] = value
            dht[cols, rows] = value.astype(F32).T.astype(LOW)

        loop(2, heads)

    lanes = lax.broadcasted_iota(jnp.int32, (1, PAIR), 1) < 64

    def attend_back(qbs, first_pair, count):
        def step(index):
            pair = index + first_pair
            for qb in qbs:
                first, width, allowed, distance = band(qb)
                queries = slice(qb * 128, qb * 128 + 128)
                span = slice(first, first + width)
                values = qkv[span, at(pair + 8, PAIR)]
                query_rows = qkv[queries, at(pair, PAIR)]
                grad_rows = dh[queries, at(pair, PAIR)]
                parts, keys_part, values_part = [], [], []
                for half in range(2):
                    s = score(pair, half, qb, first, width, allowed, distance)
                    probs = jnp.exp(s - lse[pair * 2 + half, :, queries])
                    grad_t = dht[at(pair * 2 + half, 64), queries]
                    grad_p = dot_nn(values, padded(grad_t, half))
                    row_dot = jnp.sum(probs * grad_p, axis=0, keepdims=True)
                    grad_s = (probs * (grad_p - row_dot)).astype(LOW)
                    key_t = qkvt[at(8 + pair * 2 + half, 64), span]
                    parts.append(dot_nn(key_t, grad_s))
                    keys_part.append(dot_nn(grad_s, query_rows))
                    values_part.append(dot_nn(probs.astype(LOW), grad_rows))
                dqkv[queries, at(pair, PAIR)] = (
                    (jnp.concatenate(parts, axis=0) * 0.125).T.astype(LOW)
                )
                dk_acc[span, at(pair, PAIR)] += jnp.where(lanes, keys_part[0], keys_part[1])
                dv_acc[span, at(pair, PAIR)] += jnp.where(lanes, values_part[0], values_part[1])
            if 3 in qbs:
                dqkv[:, at(pair + 4, PAIR)] = (dk_acc[:, at(pair, PAIR)] * 0.125).astype(LOW)
                dqkv[:, at(pair + 8, PAIR)] = dv_acc[:, at(pair, PAIR)].astype(LOW)

        loop(count, step)

    def heads_part(h):
        return lambda j: dqkv[:, pl.ds(pl.multiple_of(j * 512 + h * 256, 256), 256)]

    norm_two_back(0)
    rs_finish(3, keep_in(gd_out))
    rs_event(2, 0)
    dk_acc[...] = jnp.zeros((512, 512), F32)
    dv_acc[...] = jnp.zeros((512, 512), F32)
    attend_back((0, 1), 0, 4)
    rs_event(5, 0)
    norm_two_back(1)
    cross(4, pm.at[at(other, 256)], pmr).start()
    others_free(ready_two)
    flip(dattn)
    weight_grad(1, plain(ho), 1, 512)
    rs_event(2, 1)
    rs_finish(6, keep_in(gd_out, 1024))
    store(7, gd_out).start()
    attend_back((2, 3), 0, 2)
    rs_event(5, 1)
    flip(a1)
    weight_grad(0, heads_part(0), 3, 256)
    rs_event(2, 2)
    rs_event(1, 0)
    attend_back((2, 3), 2, 2)
    rows_drain(0, pcx, arrx)
    rows_drain(1, pcd, arrd)
    send_back = picks(arrive_ref).astype(LOW)
    cross(4, pm.at[at(other, 256)], pmr).wait_recv()

    def finish_y(i):
        part = at(i, 32)
        mine = at(t * 8 + i, 32)
        value = yb[part, :] + (pm[mine, :].astype(F32) + pmr[part, :].astype(F32)) + vrow[7:8, :]
        tok_v[part, :] = value.astype(LOW)

    loop(8, finish_y)
    pcx[...] = dot_nn(send_back, tok_v[...]).astype(LOW)
    rows_send(2, pcx, backy, 0, 5)
    rs_event(0, 0)
    rs_event(5, 2)

    def attn_in_back(rows):
        def step(i):
            po[rows, at(i, 256)] = dot_nt(
                dqkv[rows, 0:1536], wqkv[pl.ds(i * 4, 4)].reshape(256, 1536)
            ).astype(LOW)

        loop(4, step)

    for rb in range(2):
        rows = slice(rb * 256, rb * 256 + 256)
        cross(2 + rb, po.at[rows], por.at[rows]).wait_send()
    attn_in_back(at(other, 256))
    cross(7, po.at[at(other, 256)], por.at[pl.ds(0, 256)]).start()
    attn_in_back(own)
    rs_event(1, 1)
    rows_send(2, pcx, backy, 5, 10)
    weight_grad(4, heads_part(1), 3, 256)
    rs_finish(2, keep_in(gu_out))
    rs_event(0, 1)
    rows_send(2, pcx, backy, 10, 15)
    sums = jnp.zeros((1, 1536), F32)
    for i in range(4):
        sums = sums + jnp.sum(
            dqkv[i * 128 : i * 128 + 128, 0:1536].astype(F32), axis=0, keepdims=True
        )
    gvec[2:3, at(t, 512)] = sums[:, 0:512]
    gvec[3:4, at(t, 512)] = sums[:, 1024:1536]

    def norm_one_again(i):
        part = at(i, 32)
        normed, scale = stats(xg[at(t * 8 + i, 32), :].astype(F32))
        yb[part, :] = normed
        rstd[part, :] = jnp.broadcast_to(scale, (32, 128))

    loop(8, norm_one_again)
    rs_event(1, 2)
    rs_event(4, 0)
    rs_finish(5, keep_in(gu_out, 1024))
    store(6, gu_out).start()
    take_back = picks(rank_ref).T.astype(LOW)
    rs_event(0, 2)
    rs_event(4, 1)
    cross(7, po.at[at(other, 256)], por.at[pl.ds(0, 256)]).wait_recv()

    def norm_one_back(i):
        part = at(i, 32)
        mine = at(t * 8 + i, 32)
        grad = po[mine, :].astype(F32) + por[part, :].astype(F32)
        normed, scale = yb[part, :], rstd[part, 0:1]
        e = grad * vrow[0:1, :]
        inner = e - jnp.mean(e, axis=-1, keepdims=True)
        inner = inner - normed * jnp.mean(e * normed, axis=-1, keepdims=True)
        cot_v[part, :] = (res[mine, :] + inner * scale).astype(LOW)
        gvec[0:1, :] += jnp.sum(grad * normed, axis=0, keepdims=True)
        gvec[1:2, :] += jnp.sum(grad, axis=0, keepdims=True)

    loop(8, norm_one_back)

    for e in range(16):
        svec[e, 0:8, :] = gvec[:, 128 * (e // 2) : 128 * (e // 2) + 128]
        svec[e, 8:16, :] = jnp.zeros((8, 128), F32)
    for j in range(8):
        svec[8 * t + j, 8:9, :] = gbup[:, 256 * j : 256 * j + 128]
        svec[8 * t + j, 9:10, :] = gbup[:, 256 * j + 128 : 256 * j + 256]
    tiles_send(5, lambda spot: svec.at[spot], svr)
    a2[0:256, :] = dot_nn(send_back, cot_v[...]).astype(LOW)
    rows_send(3, a2, backd)
    svr[d] = svec[d]
    rs_event(4, 2)
    rows_wait(2, pcx, backy)
    tok_v[...] = dot_nn(take_back, backy[...]).astype(LOW)
    store(0, tok_v).start()
    rs_finish(1, keep_in(go_out))
    store(5, go_out).start()
    rs_finish(0, keep_heads(0))
    tiles_all(5, svr).wait_recv()
    small = jnp.zeros((16, 128), F32)
    for e in range(16):
        small = small + svr[e]
    sown[...] = small
    cross(8, sown, sown_r).start()
    rs_finish(4, keep_heads(256))
    for i, ref in enumerate((gq_out, gk_out, gv_out)):
        store(2 + i, ref).start()
    cross(8, sown, sown_r).wait_recv()
    small_out[...] = sown[...] + sown_r[...]
    store(8, small_out).start()
    ag_drain(0)
    ag_drain(1)
    rows_wait(3, a2, backd)
    cot_v[...] = dot_nn(take_back, backd[...]).astype(LOW)
    store(1, cot_v).start()

    for c in range(7):
        rs_drain(c)
    rows_drain(2, pcx, backy)
    rows_drain(3, a2, backd)
    tiles_all(4, vgat).wait_send()
    tiles_all(5, svr).wait_send()
    cross(0, xg.at[own], xg.at[own]).wait_send()
    cross(1, dyg.at[own], dyg.at[own]).wait_send()
    cross(4, pm.at[at(other, 256)], pmr).wait_send()
    for rb in range(2):
        rows = slice(rb * 256, rb * 256 + 256)
        cross(5 + rb, pd.at[rows], pdr.at[rows]).wait_send()
    cross(7, po.at[at(other, 256)], por.at[pl.ds(0, 256)]).wait_send()
    cross(8, sown, sown_r).wait_send()
    stored = (tok_v, cot_v, gq_out, gk_out, gv_out, go_out, gu_out, gd_out, small_out)
    for i, ref in enumerate(stored):
        store(i, ref).wait()


def settle_kernel(*refs):
    sources, homes = refs[:9], refs[9:26]
    held, short = refs[26:35], refs[35:44]
    in_sem, out_sem = refs[44], refs[45]
    ins = [pltpu.make_async_copy(sources[i], held[i], in_sem.at[i]) for i in range(9)]
    outs = [pltpu.make_async_copy(held[i], homes[i], out_sem.at[i]) for i in range(8)]
    outs += [pltpu.make_async_copy(short[i], homes[8 + i], out_sem.at[8 + i]) for i in range(9)]
    for i in (8, 6, 7, 0, 1, 2, 3, 4, 5):
        ins[i].start()
    core = lax.rem(lax.axis_index("dp"), 2)
    small = held[8]
    ins[8].wait()
    for i in range(8):
        row = small[i : i + 1, :]
        short[i][...] = jnp.where(core == 0, row[:, 0:64], row[:, 64:128]).reshape(64)
    short[8][0:128] = small[8:9, :].reshape(128)
    short[8][128:256] = small[9:10, :].reshape(128)
    for i in range(9):
        outs[8 + i].start()
    for i in (6, 7, 0, 1, 2, 3, 4, 5):
        ins[i].wait()
        outs[i].start()
    for copy in outs:
        copy.wait()


def fused_body(
    tokens,
    cotangent,
    norm1_gain,
    norm1_shift,
    w_query,
    b_query,
    w_key,
    w_value,
    b_value,
    w_out,
    b_out,
    norm2_gain,
    norm2_shift,
    w_up,
    b_up,
    w_down,
    b_down,
    lengths,
    deal_rank,
    arrival,
):
    def vm(*shape, dtype=LOW):
        return pltpu.VMEM(shape, dtype)

    def dma(*shape):
        return pltpu.SemaphoreType.DMA(shape)

    scratch = [pltpu.VMEM((64,), LOW)] * 8 + [
        pltpu.VMEM((256,), LOW),
        pltpu.VMEM((1, 1, 256), jnp.int32),
        pltpu.VMEM((1, 1, 256), jnp.int32),
        vm(64, 512, dtype=F32),
        vm(64, 512, dtype=F32),
        vm(64, 512, dtype=F32),
        vm(64, 512, dtype=F32),
        vm(64, 2048, dtype=F32),
        vm(64, 2048, dtype=F32),
        vm(16, 128, dtype=F32),
        vm(16, 64, 1536),
        vm(16, 64, 512),
        vm(16, 64, 2048),
        vm(16, 64, 2048),
        vm(16, 64, 768),
        vm(16, 64, 768),
        vm(16, 64, 512),
        vm(16, 64, 2048),
        vm(16, 64, 2048),
        vm(16, 64, 2048),
        vm(256, 1024),
        vm(256, 1024),
        vm(256, 1024),
        vm(256, 1024),
        vm(256, 1024),
        vm(256, 1024),
        vm(256, 1024),
        vm(256, 1024),
        vm(512, 1024),
        vm(512, 1024),
        vm(512, 1024),
        vm(512, 1536),
        vm(1536, 512),
        vm(512, 512),
        vm(8, 1, 512, dtype=F32),
        vm(512, 1024),
        vm(512, 1024),
        vm(512, 1024, dtype=F32),
        vm(256, 1024, dtype=F32),
        vm(512, 128, dtype=F32),
        vm(512, 1024),
        vm(512, 2048),
        vm(512, 2048),
        vm(512, 1024),
        vm(256, 1024),
        vm(512, 1024),
        vm(512, 1024),
        vm(512, 1024),
        vm(512, 512),
        vm(512, 512),
        vm(512, 512, dtype=F32),
        vm(512, 512, dtype=F32),
        vm(1024, 512),
        vm(16, 16, 128, dtype=F32),
        vm(8, 1024, dtype=F32),
        vm(1, 1536, dtype=F32),
        vm(1, 2048, dtype=F32),
        vm(8, 1024, dtype=F32),
        vm(1, 2048, dtype=F32),
        vm(16, 16, 128, dtype=F32),
        vm(16, 16, 128, dtype=F32),
        vm(16, 128, dtype=F32),
        vm(16, 128, dtype=F32),
        vm(1, 512, dtype=jnp.int32),
        dma(20),
        dma(9),
        dma(6),
        dma(6, 2, 4),
        dma(6),
        dma(6),
        dma(6),
        dma(6),
        dma(9),
        dma(9),
        dma(7),
        dma(7, 2),
        dma(7),
        dma(7, 2, 4),
        dma(6),
        dma(7),
        pltpu.SemaphoreType.REGULAR,
        pltpu.SemaphoreType.REGULAR,
    ]
    anywhere = pl.BlockSpec(memory_space=pl.ANY)
    outs = (
        jax.ShapeDtypeStruct((256, 1024), LOW),
        jax.ShapeDtypeStruct((256, 1024), LOW),
        jax.ShapeDtypeStruct((64, 512), F32),
        jax.ShapeDtypeStruct((64, 512), F32),
        jax.ShapeDtypeStruct((64, 512), F32),
        jax.ShapeDtypeStruct((64, 512), F32),
        jax.ShapeDtypeStruct((64, 2048), F32),
        jax.ShapeDtypeStruct((64, 2048), F32),
        jax.ShapeDtypeStruct((16, 128), F32),
    )
    parts = pl.pallas_call(
        fused_kernel,
        name="fused_layer",
        out_shape=outs,
        in_specs=[anywhere] * 19 + [pl.BlockSpec(memory_space=pltpu.SMEM)],
        out_specs=[anywhere] * 9,
        scratch_shapes=scratch,
        compiler_params=pltpu.CompilerParams(
            collective_id=0, has_side_effects=True, vmem_limit_bytes=67043328
        ),
    )(
        tokens,
        cotangent,
        w_query,
        w_key,
        w_value,
        w_out.T,
        w_up,
        w_down.T,
        norm1_gain,
        norm1_shift,
        b_query,
        b_value,
        b_out,
        norm2_gain,
        norm2_shift,
        b_down,
        b_up,
        deal_rank,
        arrival,
        lengths,
    )
    short = jax.ShapeDtypeStruct((64,), F32)
    finals = outs[:8] + (short,) * 8 + (jax.ShapeDtypeStruct((256,), F32),)
    done = pl.pallas_call(
        settle_kernel,
        name="settle",
        out_shape=finals,
        in_specs=[anywhere] * 9,
        out_specs=[anywhere] * 17,
        scratch_shapes=[vm(*out.shape, dtype=out.dtype) for out in outs + finals[8:]]
        + [dma(9), dma(17)],
    )(*parts)
    result, grad_tokens, grad_q, grad_k, grad_v, grad_out, grad_up, grad_down = done[:8]
    gain_one, shift_one, bias_q, bias_v, bias_out, gain_two, shift_two, bias_down, bias_up = done[8:]
    return (
        result,
        grad_tokens,
        gain_one,
        shift_one,
        grad_q,
        bias_q,
        grad_k,
        grad_v,
        bias_v,
        grad_out.T,
        bias_out,
        gain_two,
        shift_two,
        grad_up,
        bias_up,
        grad_down.T,
        bias_down,
    )


def solution(mesh):
    in_specs = (
        P(("dp", "tensor"), None),
        P(("dp", "tensor"), None),
        P("dp"),
        P("dp"),
        P("dp", "tensor"),
        P("dp"),
        P("dp", "tensor"),
        P("dp", "tensor"),
        P("dp"),
        P("tensor", "dp"),
        P("dp"),
        P("dp"),
        P("dp"),
        P("dp", "tensor"),
        P("dp"),
        P("tensor", "dp"),
        P("dp"),
        P("dp", None),
        P("dp", "tensor", None),
        P("dp", "tensor", None),
    )
    out_specs = (
        P(("dp", "tensor"), None),
        P(("dp", "tensor"), None),
        P("dp"),
        P("dp"),
        P("dp", "tensor"),
        P("dp"),
        P("dp", "tensor"),
        P("dp", "tensor"),
        P("dp"),
        P("tensor", "dp"),
        P("dp"),
        P("dp"),
        P("dp"),
        P("dp", "tensor"),
        P("dp"),
        P("tensor", "dp"),
        P("dp"),
    )
    small_slice = mesh.shape["dp"] == 16 and mesh.shape["tensor"] == 2
    program = fused_body if small_slice else body
    return jax.shard_map(program, mesh=mesh, in_specs=in_specs, out_specs=out_specs, check_vma=False)
```

```python
import jax
import jax.numpy as jnp
from jax import lax
from jax.experimental import pallas as pl
from jax.experimental.pallas import tpu as pltpu
from jax.sharding import PartitionSpec as P

D = 1024
HEADS = 16
HEAD_DIM = 64
FF = 4096


EPSILON = 1e-05
GELU_SCALE = 0.7978845608028654


def layer_norm(values, norm_gain, norm_shift):
    center = values - jnp.mean(values, axis=-1, keepdims=True)
    spread = jnp.mean(center * center, axis=-1, keepdims=True)
    return center * lax.rsqrt(spread + EPSILON) * norm_gain + norm_shift


def gelu_tanh(values):
    return jax.nn.gelu(values, approximate=True)


def contract_rows(first_op, second_op):
    return lax.dot_general(
        first_op, second_op, (((0,), (0,)), ((), ())), preferred_element_type=jnp.float32
    )


def contract_cols(first_op, second_op):
    return lax.dot_general(
        first_op, second_op, (((1,), (1,)), ((), ())), preferred_element_type=jnp.float32
    )


def take_block(vector, block_index, block_size):
    return lax.dynamic_slice_in_dim(vector, block_index * block_size, block_size, 0).astype(
        jnp.float32
    )


def place_block(total_size, block_vec, block_index):
    holder = jnp.zeros((total_size,), jnp.float32)
    return lax.dynamic_update_slice_in_dim(holder, block_vec, block_index * block_vec.shape[0], 0)


def sequence_marks(seq_lengths, group_rows):
    seq_ends = jnp.cumsum(seq_lengths)
    seq_starts = seq_ends - seq_lengths
    row_ids = lax.iota(jnp.int32, group_rows)
    inside = (row_ids[:, None] >= seq_starts[None, :]) & (row_ids[:, None] < seq_ends[None, :])
    seq_index = lax.iota(jnp.int32, seq_lengths.shape[0])
    seq_ids = jnp.sum(jnp.where(inside, seq_index[None, :], 0), axis=1)
    seq_start = jnp.sum(jnp.where(inside, seq_starts[None, :], 0), axis=1)
    return (seq_ids, row_ids - seq_start, row_ids)


def body(
    tokens,
    cotangent,
    norm1_gain,
    norm1_shift,
    w_query,
    b_query,
    w_key,
    w_value,
    b_value,
    w_out,
    b_out,
    norm2_gain,
    norm2_shift,
    w_up,
    b_up,
    w_down,
    b_down,
    lengths,
    deal_rank,
    arrival,
):
    dp_count = lax.axis_size("dp")
    tensor_count = lax.axis_size("tensor")
    tensor_rank = lax.axis_index("tensor")
    tok_rows = tokens.shape[0]
    features = tokens.shape[1]
    piece_rows = tok_rows // dp_count
    group_rows = tok_rows * tensor_count
    sending_rank = deal_rank.reshape(tok_rows)
    deal_order = jnp.argsort(sending_rank)
    arrive_order = arrival.reshape(tok_rows)
    return_order = jnp.argsort(arrive_order)

    def relocate(first_part, second_part):
        return (
            lax.all_to_all(first_part, "dp", split_axis=0, concat_axis=0, tiled=True),
            lax.all_to_all(second_part, "dp", split_axis=0, concat_axis=0, tiled=True),
        )

    def to_pieces(row_data, row_order):
        return row_data[row_order].reshape(dp_count, piece_rows, features)

    moved_x, moved_dy = relocate(to_pieces(tokens, deal_order), to_pieces(cotangent, deal_order))
    local_x = moved_x.reshape(tok_rows, features)[arrive_order]
    local_dy = moved_dy.reshape(tok_rows, features)[arrive_order]
    part_rows = w_query.shape[0]
    head_cols = w_query.shape[1]
    hidden_cols = w_up.shape[1]
    vectors = (
        norm1_gain,
        norm1_shift,
        b_query,
        b_value,
        b_out,
        norm2_gain,
        norm2_shift,
        b_down,
    )
    up_wide = b_up.shape[0] // part_rows
    vec_cols = jnp.concatenate(
        [jnp.stack(vectors, axis=1), b_up.reshape(part_rows, up_wide)], axis=1
    )
    vec_cols = jnp.pad(vec_cols, ((0, 0), (0, 128 - vec_cols.shape[1])))
    packed = jnp.concatenate(
        [w_query, w_key, w_value, w_out.T, w_up, w_down.T, vec_cols], axis=1
    )
    packed_all = lax.all_gather(packed, "dp", axis=0, tiled=True)
    edges = [0, head_cols, 2 * head_cols, 3 * head_cols, 4 * head_cols]
    edges += [4 * head_cols + hidden_cols, 4 * head_cols + 2 * hidden_cols]
    query_cols, key_cols, value_cols, out_cols, up_cols, down_cols = (
        packed_all[:, edges[i] : edges[i + 1]] for i in range(6)
    )
    out_rows = out_cols.T
    down_rows = down_cols.T
    vec_all = packed_all[:, edges[6] :]
    (
        gain_one,
        shift_one,
        bias_query,
        bias_value,
        bias_out,
        gain_two,
        shift_two,
        bias_down,
    ) = (vec_all[:, i] for i in range(8))
    bias_up = vec_all[:, 8 : 8 + up_wide].reshape(-1)
    gain_one = gain_one.astype(jnp.float32)
    shift_one = shift_one.astype(jnp.float32)
    gain_two = gain_two.astype(jnp.float32)
    shift_two = shift_two.astype(jnp.float32)
    local_heads = head_cols // HEAD_DIM
    score_scale = HEAD_DIM ** (-0.5)
    query_bias = take_block(bias_query, tensor_rank, head_cols)
    value_bias = take_block(bias_value, tensor_rank, head_cols)
    up_bias = take_block(bias_up, tensor_rank, hidden_cols)
    x_rows = local_x.astype(jnp.float32)
    first_in = layer_norm(x_rows, gain_one, shift_one).astype(jnp.bfloat16)
    group_one = lax.all_gather(first_in, "tensor", axis=0, tiled=True)
    queries = (
        jnp.dot(group_one, query_cols, preferred_element_type=jnp.float32) + query_bias
    ).astype(jnp.bfloat16)
    queries = queries.reshape(group_rows, local_heads, HEAD_DIM)
    keyset = jnp.dot(group_one, key_cols, preferred_element_type=jnp.float32).astype(jnp.bfloat16)
    keyset = keyset.reshape(group_rows, local_heads, HEAD_DIM)
    valset = (
        jnp.dot(group_one, value_cols, preferred_element_type=jnp.float32) + value_bias
    ).astype(jnp.bfloat16)
    valset = valset.reshape(group_rows, local_heads, HEAD_DIM)
    head_ids = tensor_rank * local_heads + lax.iota(jnp.int32, local_heads)
    slopes = jnp.exp2(-8.0 * (head_ids.astype(jnp.float32) + 1.0) / HEADS)
    seq_ids, positions, row_ids = sequence_marks(lengths[0], group_rows)
    qblock = min(512, group_rows)
    blocks = group_rows // qblock
    block_starts = lax.iota(jnp.int32, blocks) * qblock

    def block_scores(row_start):
        query_rows = lax.dynamic_slice_in_dim(queries, row_start, qblock, 0)
        raw_scores = (
            jnp.einsum("qhd,khd->hqk", query_rows, keyset, preferred_element_type=jnp.float32)
            * score_scale
        )
        seq_rows = lax.dynamic_slice_in_dim(seq_ids, row_start, qblock, 0)
        pos_rows = lax.dynamic_slice_in_dim(positions, row_start, qblock, 0)
        row_rows = lax.dynamic_slice_in_dim(row_ids, row_start, qblock, 0)
        distance = (pos_rows[:, None] - positions[None, :]).astype(jnp.float32)
        allowed = (seq_rows[:, None] == seq_ids[None, :]) & (row_rows[:, None] >= row_ids[None, :])
        scores = jnp.where(
            allowed[None], raw_scores - slopes[:, None, None] * distance[None], -1e30
        )
        return (query_rows, scores)

    def attend(row_start):
        query_rows, scores = block_scores(row_start)
        row_max = jnp.max(scores, axis=-1, keepdims=True)
        exponent = jnp.exp(scores - row_max)
        row_total = jnp.sum(exponent, axis=-1, keepdims=True)
        attn_probs = (exponent / row_total).astype(jnp.bfloat16)
        mixed = jnp.einsum("hqk,khd->qhd", attn_probs, valset, preferred_element_type=jnp.float32)
        return (mixed, row_max[..., 0] + jnp.log(row_total[..., 0]))

    mixed_all, log_totals = lax.map(attend, block_starts)
    heads_out = mixed_all.reshape(group_rows, head_cols).astype(jnp.bfloat16)
    attn_out = lax.psum_scatter(
        jnp.dot(heads_out, out_rows, preferred_element_type=jnp.float32).astype(jnp.bfloat16),
        "tensor",
        scatter_dimension=0,
        tiled=True,
    ).astype(jnp.float32) + bias_out.astype(jnp.float32)
    residual = x_rows + attn_out
    second_in = layer_norm(residual, gain_two, shift_two).astype(jnp.bfloat16)
    grad_in = local_dy.astype(jnp.float32)
    down_bias_term = jnp.sum(grad_in, axis=0)
    group_two = lax.all_gather(second_in, "tensor", axis=0, tiled=True)
    pre_act = jnp.dot(group_two, up_cols, preferred_element_type=jnp.float32) + up_bias
    activated = gelu_tanh(pre_act).astype(jnp.bfloat16)
    mlp_out = lax.psum_scatter(
        jnp.dot(activated, down_rows, preferred_element_type=jnp.float32).astype(jnp.bfloat16),
        "tensor",
        scatter_dimension=0,
        tiled=True,
    ).astype(jnp.float32)
    result = residual + mlp_out + bias_down.astype(jnp.float32)
    group_dy = lax.all_gather(local_dy, "tensor", axis=0, tiled=True)
    grad_down = contract_rows(activated, group_dy)
    grad_act = contract_cols(group_dy, down_rows)
    gelu_pull = jax.vjp(gelu_tanh, pre_act)[1]
    grad_pre = gelu_pull(grad_act)[0].astype(jnp.bfloat16)
    grad_up = contract_rows(group_two, grad_pre)
    up_bias_term = place_block(FF, jnp.sum(grad_pre, axis=0, dtype=jnp.float32), tensor_rank)
    grad_two = lax.psum_scatter(
        contract_cols(grad_pre, up_cols).astype(jnp.bfloat16),
        "tensor",
        scatter_dimension=0,
        tiled=True,
    ).astype(jnp.float32)
    result_low = result.astype(jnp.bfloat16)
    norm_two_pull = jax.vjp(layer_norm, residual, gain_two, shift_two)[1]
    grad_res_norm, gain_two_term, shift_two_term = norm_two_pull(grad_two)
    grad_resid = grad_in + grad_res_norm
    grad_attn = grad_resid.astype(jnp.bfloat16)
    out_bias_term = jnp.sum(grad_attn, axis=0, dtype=jnp.float32)
    group_grad = lax.all_gather(grad_attn, "tensor", axis=0, tiled=True)
    grad_out = contract_rows(heads_out, group_grad)
    grad_heads = (
        contract_cols(group_grad, out_rows)
        .astype(jnp.bfloat16)
        .reshape(group_rows, local_heads, HEAD_DIM)
    )

    def attend_back(running, block_item):
        key_accum, value_accum = running
        row_start, log_total = block_item
        query_rows, scores = block_scores(row_start)
        attn_probs = jnp.exp(scores - log_total[..., None])
        grad_rows = lax.dynamic_slice_in_dim(grad_heads, row_start, qblock, 0)
        grad_probs = jnp.einsum(
            "qhd,khd->hqk", grad_rows, valset, preferred_element_type=jnp.float32
        )
        row_dot = jnp.sum(attn_probs * grad_probs, axis=-1, keepdims=True)
        grad_scores = (attn_probs * (grad_probs - row_dot)).astype(jnp.bfloat16)
        grad_query_rows = jnp.einsum(
            "hqk,khd->qhd", grad_scores, keyset, preferred_element_type=jnp.float32
        )
        grad_query_rows = (grad_query_rows * score_scale).astype(jnp.bfloat16)
        key_accum = (
            key_accum
            + jnp.einsum(
                "hqk,qhd->khd", grad_scores, query_rows, preferred_element_type=jnp.float32
            )
            * score_scale
        )
        value_accum = value_accum + jnp.einsum(
            "hqk,qhd->khd",
            attn_probs.astype(jnp.bfloat16),
            grad_rows,
            preferred_element_type=jnp.float32,
        )
        return ((key_accum, value_accum), grad_query_rows)

    zero_heads = jnp.zeros((group_rows, local_heads, HEAD_DIM), jnp.float32)
    (key_accum, value_accum), grad_query_blocks = lax.scan(
        attend_back, (zero_heads, zero_heads), (block_starts, log_totals)
    )
    grad_query = grad_query_blocks.reshape(group_rows, head_cols)
    grad_key = key_accum.reshape(group_rows, head_cols).astype(jnp.bfloat16)
    grad_value = value_accum.reshape(group_rows, head_cols).astype(jnp.bfloat16)
    query_bias_term = place_block(D, jnp.sum(grad_query, axis=0, dtype=jnp.float32), tensor_rank)
    value_bias_term = place_block(D, jnp.sum(grad_value, axis=0, dtype=jnp.float32), tensor_rank)
    grad_wquery = contract_rows(group_one, grad_query)
    grad_wkey = contract_rows(group_one, grad_key)
    grad_wvalue = contract_rows(group_one, grad_value)
    grad_one = lax.psum_scatter(
        (
            contract_cols(grad_query, query_cols)
            + contract_cols(grad_key, key_cols)
            + contract_cols(grad_value, value_cols)
        ).astype(jnp.bfloat16),
        "tensor",
        scatter_dimension=0,
        tiled=True,
    ).astype(jnp.float32)
    norm_one_pull = jax.vjp(layer_norm, x_rows, gain_one, shift_one)[1]
    grad_x_norm, gain_one_term, shift_one_term = norm_one_pull(grad_one)
    grad_tokens = (grad_resid + grad_x_norm).astype(jnp.bfloat16)
    small_terms = jnp.stack(
        (
            gain_one_term,
            shift_one_term,
            query_bias_term,
            value_bias_term,
            out_bias_term,
            gain_two_term,
            shift_two_term,
            down_bias_term,
        ),
        axis=1,
    )
    small_terms = jnp.concatenate([small_terms, up_bias_term.reshape(-1, up_wide)], axis=1)
    small_terms = jnp.pad(small_terms, ((0, 0), (0, 128 - small_terms.shape[1])))
    terms = (grad_wquery, grad_wkey, grad_wvalue, grad_out.T, grad_up, grad_down.T, small_terms)
    packed_grads = jnp.concatenate([term.astype(jnp.bfloat16) for term in terms], axis=1)
    reduced = lax.psum_scatter(packed_grads, "dp", scatter_dimension=0, tiled=True).astype(
        jnp.float32
    )
    shards = [reduced[:, edges[i] : edges[i + 1]] for i in range(6)]
    shards[3] = shards[3].T
    shards[5] = shards[5].T
    sums = lax.psum(reduced[:, edges[6] : edges[6] + 8 + up_wide], "tensor")
    smalls = [sums[:, i] for i in range(7)] + [sums[:, 8:].reshape(-1), sums[:, 7]]
    back_y, back_dx = relocate(
        to_pieces(result_low, return_order), to_pieces(grad_tokens, return_order)
    )
    given_y = back_y.reshape(tok_rows, features)[sending_rank]
    given_dx = back_dx.reshape(tok_rows, features)[sending_rank]
    return (
        given_y,
        given_dx,
        smalls[0],
        smalls[1],
        shards[0],
        smalls[2],
        shards[1],
        shards[2],
        smalls[3],
        shards[3],
        smalls[4],
        smalls[5],
        smalls[6],
        shards[4],
        smalls[7],
        shards[5],
        smalls[8],
    )


MESH = pl.DeviceIdType.MESH
F32 = jnp.float32
LOW = jnp.bfloat16
RING = 8
PAIR = 128


def dot_nn(first_op, second_op):
    return lax.dot_general(
        first_op, second_op, (((1,), (0,)), ((), ())), preferred_element_type=F32
    )


def dot_nt(first_op, second_op):
    return lax.dot_general(
        first_op, second_op, (((1,), (1,)), ((), ())), preferred_element_type=F32
    )


def loop(count, step):
    def run(i, carry):
        step(i)
        return carry

    lax.fori_loop(0, count, run, 0)


def at(index, size):
    return pl.ds(pl.multiple_of(index * size, size), size)


def fused_kernel(
    tok_ref,
    cot_ref,
    wq_ref,
    wk_ref,
    wv_ref,
    wot_ref,
    wup_ref,
    wdt_ref,
    *refs,
):
    vectors, refs = refs[:9], refs[9:]
    rank_ref, arrive_ref, len_ref = refs[:3]
    homes, refs = refs[3:12], refs[12:]
    little, refs = refs[:11], refs[11:]
    fused_layer(
        (tok_ref, cot_ref, wq_ref, wk_ref, wv_ref, wot_ref, wup_ref, wdt_ref),
        vectors + (rank_ref, arrive_ref),
        little,
        len_ref,
        homes,
        *refs,
    )


def fused_layer(
    given,
    far_little,
    little,
    len_ref,
    homes,
    gq_out,
    gk_out,
    gv_out,
    go_out,
    gu_out,
    gd_out,
    small_out,
    wqkv,
    wo,
    wu,
    wd,
    ga,
    gb,
    go,
    gu,
    gd,
    land,
    tok_v,
    cot_v,
    pcx,
    pcd,
    arrx,
    arrd,
    backy,
    backd,
    xg,
    dyg,
    a1,
    qkv,
    qkvt,
    ho,
    lse,
    po,
    por,
    res,
    yb,
    rstd,
    a2,
    act,
    dpre,
    pm,
    pmr,
    pd,
    pdr,
    dattn,
    dh,
    dht,
    dk_acc,
    dv_acc,
    tbuf,
    vgat,
    vrow,
    bqkv,
    bup,
    gvec,
    gbup,
    svec,
    svr,
    sown,
    sown_r,
    start_row,
    ld,
    st,
    ag_s,
    ag_r,
    mt_s,
    mt_r,
    aa_s,
    aa_r,
    y_s,
    y_r,
    rm_s,
    rm_r,
    rr_s,
    rr_r,
    ax_r,
    rx_r,
    ready_one,
    ready_two,
):
    tok_ref, cot_ref, wq_ref, wk_ref, wv_ref, wot_ref, wup_ref, wdt_ref = given
    vectors, rank_ref, arrive_ref = little[:9], little[9], little[10]
    d = lax.axis_index("dp")
    t = lax.axis_index("tensor")
    other = 1 - t
    core = lax.rem(d, 2)
    chip = lax.div(d, 2)
    xc = lax.rem(chip, 2)
    zc = lax.div(chip, 2)
    p = zc + xc * (7 - 2 * zc)

    def chip_at(pos):
        pos = lax.rem(pos + 2 * RING, RING)
        xx = lax.div(pos, 4)
        zz = pos + xx * (7 - 2 * pos)
        return zz * 2 + xx

    def dev(pos):
        return chip_at(pos) * 2 + core

    def mdev(pos):
        return chip_at(pos) * 2 + 1 - core

    def outer(pos):
        spot = lax.rem(pos + 2 * RING, 4)
        return (spot == 0) | (spot == 3)

    inner = ~outer(p)
    even = lax.rem(p, 2) == 0
    over = dev(7 - p)
    mate = d + 1 - 2 * core
    sides = (dev(p + 1), dev(p - 1))
    weights = (wqkv, wo, wu, wu, wd, wd)
    firsts = (0, 0, 0, 1024, 0, 1024)
    spans = (1536, 512, 1024, 1024, 1024, 1024)
    grads = (ga, go, gu, gd, gb, gu, gd)
    starts_at = (0, 0, 0, 0, 0, 1024, 1024)
    widths = (768, 512, 1024, 1024, 768, 1024, 1024)
    landing = (wd, wd, wu, land, wd, wu, land)
    offsets = (0, 1536, 0, 0, 768, 1024, 1024)
    dqkv = act

    def remote(src, dst, send, recv, device):
        return pltpu.make_async_remote_copy(
            src_ref=src,
            dst_ref=dst,
            send_sem=send,
            recv_sem=recv,
            device_id=device,
            device_id_type=MESH,
        )

    def signal(sem, device):
        pl.semaphore_signal(sem, inc=1, device_id=device, device_id_type=MESH)

    loads = [
        pltpu.make_async_copy(tok_ref, tok_v, ld.at[0]),
        pltpu.make_async_copy(cot_ref, cot_v, ld.at[1]),
        pltpu.make_async_copy(wq_ref, wqkv.at[d, :, pl.ds(0, 512)], ld.at[2]),
        pltpu.make_async_copy(wk_ref, wqkv.at[d, :, pl.ds(512, 512)], ld.at[3]),
        pltpu.make_async_copy(wv_ref, wqkv.at[d, :, pl.ds(1024, 512)], ld.at[4]),
        pltpu.make_async_copy(wot_ref, wo.at[d], ld.at[5]),
        pltpu.make_async_copy(wup_ref, wu.at[d], ld.at[6]),
        pltpu.make_async_copy(wdt_ref, wd.at[d], ld.at[7]),
    ]
    for i in range(2):
        loads[i].start()
    fetches = [
        pltpu.make_async_copy(far_little[i], little[i], ld.at[9 + i]) for i in range(11)
    ]
    for fetch in fetches:
        fetch.start()
    for i in range(2, 8):
        loads[i].start()
    barrier = pltpu.get_barrier_semaphore()

    def store(i, src):
        return pltpu.make_async_copy(src, homes[i], st.at[i])

    def greet(k):
        signal(barrier, {"dp": lax.rem(d + k + 1, 16)})

    loop(15, greet)
    signal(barrier, {"tensor": other})

    def rows_send(kind, src, dst, low=0, high=15):
        def step(k):
            spot = lax.rem(d + low + k + 1, 16)
            remote(
                src.at[at(spot, 16)],
                dst.at[at(d, 16)],
                aa_s.at[kind],
                aa_r.at[kind],
                {"dp": spot},
            ).start()

        loop(high - low, step)
        if low == 0:
            dst[at(d, 16), :] = src[at(d, 16), :]

    def rows_all(kind, src, dst):
        bulk = pl.ds(0, 240)
        return remote(src.at[bulk], dst.at[bulk], aa_s.at[kind], aa_r.at[kind], {"dp": mate})

    def rows_wait(kind, src, dst):
        rows_all(kind, src, dst).wait_recv()

    def rows_drain(kind, src, dst):
        rows_all(kind, src, dst).wait_send()

    def tiles_send(kind, src_of, dst):
        def step(k):
            spot = lax.rem(d + k + 1, 16)
            remote(src_of(spot), dst.at[d], aa_s.at[kind], aa_r.at[kind], {"dp": spot}).start()

        loop(15, step)

    def tiles_all(kind, dst):
        bulk = dst.at[pl.ds(0, 15)]
        return remote(bulk, bulk, aa_s.at[kind], aa_r.at[kind], {"dp": mate})

    def cross(i, src, dst):
        return remote(src, dst, y_s.at[i], y_r.at[i], {"tensor": other})

    def shard(c, slot, rows=pl.ds(0, 64)):
        return weights[c].at[slot, rows, pl.ds(firsts[c], spans[c])]

    def ring_part(c, slot, way, step):
        if step == 3:
            return shard(c, slot, pl.ds(32 * way, 32))
        return shard(c, slot)

    def turn(way, steps):
        return p - steps if way == 0 else p + steps

    def ag_copy(c, way, step):
        part = ring_part(c, dev(turn(way, step)), way, step)
        return remote(
            part, part, ag_s.at[c], ag_r.at[c, way, step], {"dp": sides[way]}
        )

    def ag_arrival(c, way, step):
        part = ring_part(c, dev(turn(way, step + 1)), way, step)
        return remote(
            part, part, ag_s.at[c], ag_r.at[c, way, step], {"dp": sides[way]}
        )

    def mate_copy(c, k, place):
        if k == 0:
            part = shard(c, place(p))
        else:
            way, step = (k - 1) // 4, (k - 1) % 4
            part = ring_part(c, place(turn(way, step + 1)), way, step)
        return remote(part, part, mt_s.at[c], mt_r.at[c], {"dp": mate})

    def ag_start(c):
        for way in range(2):
            ag_copy(c, way, 0).start()
        mate_copy(c, 0, dev).start()

    def ag_over(c):
        part = shard(c, dev(jnp.where(even, p - 1, p + 1)))
        return remote(part, part, ag_s.at[c], ax_r.at[c], {"dp": over})

    def ag_event(c, step):
        if step == 3:

            @pl.when(inner)
            def _():
                part = shard(c, dev(p + 4))
                remote(part, part, ag_s.at[c], ax_r.at[c], {"dp": over}).wait_recv()

        for way in range(2):
            if step == 3:

                @pl.when(outer(p))
                def _():
                    ag_arrival(c, way, step).wait_recv()

            else:
                ag_arrival(c, way, step).wait_recv()
            if step == 2:

                @pl.when(outer(turn(1 - way, 1)))
                def _():
                    ag_copy(c, way, 3).start()

            elif step < 2:
                ag_copy(c, way, step + 1).start()
            mate_copy(c, 1 + 4 * way + step, dev).start()
        if step == 0:

            @pl.when(inner)
            def _():
                ag_over(c).start()

    def mate_all(c):
        bulk = weights[c].at[pl.ds(0, 8), pl.ds(0, 64), pl.ds(firsts[c], spans[c])]
        return remote(bulk, bulk, mt_s.at[c], mt_r.at[c], {"dp": mate})

    def ag_finish(c):
        mate_all(c).wait_recv()

    def ag_drain(c):
        def sent(halves):
            bulk = weights[c].at[pl.ds(0, halves), pl.ds(0, 32), pl.ds(firsts[c], spans[c])]
            remote(bulk, bulk, ag_s.at[c], ag_r.at[c, 0, 0], {"dp": over}).wait_send()

        pl.when(inner)(lambda: sent(15))
        pl.when(outer(p))(lambda: sent(13))
        mate_all(c).wait_send()

    def inbox(c, slot, rows=pl.ds(0, 64)):
        return landing[c].at[slot, rows, pl.ds(offsets[c], widths[c])]

    def arrived(c, slot, rows):
        return landing[c][slot, rows, offsets[c] : offsets[c] + widths[c]].astype(F32)

    halves = (1 - lax.div(zc, 2), lax.div(zc, 2))

    def rm_send(c, half):
        for i in range(4):
            spot = half * 4 + i
            remote(
                owed(c, spot * 2 + 1 - core),
                inbox(c, spot),
                rm_s.at[c],
                rm_r.at[c, half],
                {"dp": mate},
            ).start()

    def rm_wait(c, half):
        bulk = landing[c].at[pl.ds(half * 4, 4), pl.ds(0, 64), pl.ds(offsets[c], widths[c])]
        remote(bulk, bulk, rm_s.at[c], rm_r.at[c, half], {"dp": mate}).wait_recv()

    def owed(c, slot, rows=pl.ds(0, 64)):
        return grads[c].at[slot, rows, pl.ds(starts_at[c], widths[c])]

    def rs_copy(c, way, step):
        dest = dev(p + 4 - step if way == 0 else p - 4 + step)
        slot = 8 + way * 4 + step
        if step == 0:
            half = pl.ds(32 * way, 32)
            src, dst = owed(c, dest, half), inbox(c, slot, half)
        else:
            src, dst = owed(c, dest), inbox(c, slot)
        return remote(src, dst, rr_s.at[c], rr_r.at[c, way, step], {"dp": sides[way]})

    def rs_add(c, slot, rows, boxes):
        total = grads[c][slot, rows, starts_at[c] : starts_at[c] + widths[c]].astype(F32)
        for box in boxes:
            total += arrived(c, box, rows)
        return total

    def rs_over(c, slot):
        return remote(
            owed(c, dev(p + 4)), inbox(c, slot), rr_s.at[c], rx_r.at[c], {"dp": over}
        )

    def rs_fold(c, slot, first, count, boxes):
        def add(i):
            rows = at(i + first, 16)
            total = rs_add(c, slot, rows, boxes).astype(LOW)
            grads[c][slot, rows, starts_at[c] : starts_at[c] + widths[c]] = total

        loop(count, add)

    def rs_start(c):
        far = chip_at(p + 4)
        rm_wait(c, halves[0])
        rs_fold(c, far * 2 + core, 0, 4, (far,))

        @pl.when(outer(p))
        def _():
            for way in range(2):
                rs_copy(c, way, 0).start()

        @pl.when(inner)
        def _():
            rs_over(c, jnp.where(even, 12, 8)).start()

    def rs_event(c, step):
        if step == 2:

            @pl.when(inner)
            def _():
                box = jnp.where(even, 8, 12)
                rs_over(c, box).wait_recv()
                rs_fold(c, dev(jnp.where(even, p - 1, p + 1)), 0, 4, (box,))

        for way in range(2):
            pos = p + 3 - step if way == 0 else p - 3 + step
            spot = chip_at(pos)
            slot = spot * 2 + core
            box = 8 + way * 4 + step
            if step == 0 and way == 0:
                rm_wait(c, halves[1])
            if step == 0:

                @pl.when(outer(pos))
                def _():
                    rs_copy(c, way, 0).wait_recv()
                    rs_fold(c, slot, 2 * way, 2, (spot, box))
                    rs_fold(c, slot, 2 - 2 * way, 2, (spot,))

                @pl.when(~outer(pos))
                def _():
                    rs_fold(c, slot, 0, 4, (spot,))

            else:
                rs_copy(c, way, step).wait_recv()
                rs_fold(c, slot, 0, 4, (spot, box))
            rs_copy(c, way, step + 1).start()

    def rs_finish(c, keep):
        for way in range(2):
            rs_copy(c, way, 3).wait_recv()

        def add(i):
            rows = at(i, 16)
            keep(rows, rs_add(c, d, rows, (chip, 11, 15)))

        loop(4, add)

    def keep_in(ref, first=0):
        def keep(rows, total):
            ref[rows, first : first + total.shape[1]] = total

        return keep

    def keep_heads(first):
        def keep(rows, total):
            for j, ref in enumerate((gq_out, gk_out, gv_out)):
                ref[rows, first : first + 256] = total[:, 256 * j : 256 * j + 256]

        return keep

    def rs_drain(c):
        columns = pl.ds(starts_at[c], widths[c])
        sent = grads[c].at[pl.ds(0, 7), pl.ds(0, 64), columns]
        remote(sent, sent, rr_s.at[c], rr_r.at[c, 0, 1], {"dp": over}).wait_send()
        sent = grads[c].at[pl.ds(0, 8), pl.ds(0, 64), columns]
        remote(sent, sent, rm_s.at[c], rm_r.at[c, 0], {"dp": mate}).wait_send()

    def free_for_reduction(sem):
        signal(sem, {"dp": mate})
        for side in sides:
            signal(sem, {"dp": side})

        @pl.when(inner)
        def _():
            signal(sem, {"dp": over})

    def others_free(sem):
        pl.when(inner)(lambda: pl.semaphore_wait(sem, 4))
        pl.when(outer(p))(lambda: pl.semaphore_wait(sem, 3))

    def picks(ref):
        slots = lax.broadcasted_iota(jnp.int32, (256, 256), 0)
        return jnp.where(slots == ref[0, :, :], 1.0, 0.0)

    for fetch in fetches:
        fetch.wait()
    zeros = jnp.zeros((1, 64), F32)
    for i in range(8):
        row = vectors[i][...].astype(F32).reshape(1, 64)
        early = jnp.concatenate([row, zeros], axis=1)
        late = jnp.concatenate([zeros, row], axis=1)
        vgat[d, i : i + 1, :] = jnp.where(core == 0, early, late)
    row = vectors[8][...].astype(F32).reshape(1, 256)
    vgat[d, 8:9, :] = row[:, 0:128]
    vgat[d, 9:10, :] = row[:, 128:256]
    vgat[d, 10:16, :] = jnp.zeros((6, 128), F32)
    loads[0].wait()
    spread = picks(rank_ref).astype(LOW)
    pcx[...] = dot_nn(spread, tok_v[...]).astype(LOW)
    pl.semaphore_wait(barrier, 16)
    rows_send(0, pcx, arrx)
    tiles_send(4, lambda spot: vgat.at[d], vgat)
    for i in range(2, 6):
        loads[i].wait()
    ag_start(0)
    ag_start(1)
    loads[1].wait()
    pcd[...] = dot_nn(spread, cot_v[...]).astype(LOW)
    for i in range(6, 8):
        loads[i].wait()

    own = at(t, 256)
    gather_rows = picks(arrive_ref).T.astype(LOW)
    rows_wait(0, pcx, arrx)
    xg[own, :] = dot_nn(gather_rows, arrx[...]).astype(LOW)
    cross(0, xg.at[own], xg.at[own]).start()
    ag_event(0, 0)
    ag_event(1, 0)

    tiles_all(4, vgat).wait_recv()
    for m in range(8):
        both = vgat[2 * m, :, :] + vgat[2 * m + 1, :, :]
        vrow[:, 128 * m : 128 * (m + 1)] = both[0:8, :]
    for j in range(8):
        block = vgat[8 * t + j, :, :]
        bup[:, 256 * j : 256 * j + 128] = block[8:9, :]
        bup[:, 256 * j + 128 : 256 * j + 256] = block[9:10, :]
    bqkv[:, 0:512] = vrow[2:3, at(t, 512)]
    bqkv[:, 512:1024] = jnp.zeros((1, 512), F32)
    bqkv[:, 1024:1536] = vrow[3:4, at(t, 512)]
    ends = jnp.int32(0)
    row_ids = lax.broadcasted_iota(jnp.int32, (1, 512), 1)
    starts = jnp.zeros((1, 512), jnp.int32)
    for i in range(3):
        ends = ends + len_ref[0, i]
        starts = jnp.where(row_ids >= ends, ends, starts)
    start_row[...] = starts
    gvec[...] = jnp.zeros((8, 1024), F32)

    def stats(values):
        center = values - jnp.mean(values, axis=-1, keepdims=True)
        spread_of = jnp.mean(center * center, axis=-1, keepdims=True)
        scale = lax.rsqrt(spread_of + EPSILON)
        return center * scale, scale

    def norm_one(half):
        def step(i):
            rows = at(half * 8 + i, 32)
            normed, _ = stats(xg[rows, :].astype(F32))
            a1[rows, :] = (normed * vrow[0:1, :] + vrow[1:2, :]).astype(LOW)

        loop(8, step)

    norm_one(t)
    ag_event(0, 1)
    ag_event(1, 1)
    cross(0, xg.at[own], xg.at[at(other, 256)]).wait_recv()
    norm_one(other)
    ag_event(0, 2)
    ag_event(1, 2)
    ag_start(2)
    ag_start(3)
    rows_send(1, pcd, arrd, 0, 5)
    ag_event(0, 3)
    ag_event(1, 3)
    ag_finish(0)

    def project(i):
        cols = at(i, 256)
        value = dot_nn(a1[...], wqkv[:, :, cols].reshape(1024, 256)) + bqkv[:, cols]
        low = value.astype(LOW).astype(F32)
        qkv[:, cols] = low.astype(LOW)
        qkvt[cols, :] = low.T.astype(LOW)

    loop(6, project)
    rows_send(1, pcd, arrd, 5, 10)

    def slope_of(pair, half):
        head = (t * 8 + pair * 2 + half + 1).astype(F32)
        return jnp.exp2(jnp.full((1, PAIR), -0.5, F32) * head)

    def padded(block, half):
        zero = jnp.zeros_like(block)
        return jnp.concatenate([block, zero] if half == 0 else [zero, block], axis=0)

    def band(qb):
        first = max(0, qb - 2) * 128
        width = (qb + 1) * 128 - first
        keys = lax.broadcasted_iota(jnp.int32, (width, PAIR), 0) + first
        rows = lax.broadcasted_iota(jnp.int32, (width, PAIR), 1) + qb * 128
        allowed = (keys <= rows) & (keys >= start_row[:, qb * 128 : qb * 128 + 128])
        return first, width, allowed, (rows - keys).astype(F32)

    def score(pair, half, qb, first, width, allowed, distance):
        key_rows = qkv[first : first + width, at(pair + 4, PAIR)]
        query = qkvt[at(pair * 2 + half, 64), qb * 128 : qb * 128 + 128] * 0.125
        raw = dot_nn(key_rows, padded(query, half))
        return jnp.where(allowed, raw - slope_of(pair, half) * distance, -1e30)

    def attend(qbs, first_pair, count):
        def step(index):
            pair = index + first_pair
            for qb in qbs:
                first, width, allowed, distance = band(qb)
                parts = []
                for half in range(2):
                    s = score(pair, half, qb, first, width, allowed, distance)
                    top = jnp.max(s, axis=0, keepdims=True)
                    e = jnp.exp(s - top)
                    total = jnp.sum(e, axis=0, keepdims=True)
                    probs = (e * (1.0 / total)).astype(LOW)
                    lse[pair * 2 + half, :, qb * 128 : qb * 128 + 128] = top + jnp.log(total)
                    value_t = qkvt[at(16 + pair * 2 + half, 64), first : first + width]
                    parts.append(dot_nn(value_t, probs))
                ho[qb * 128 : qb * 128 + 128, at(pair, PAIR)] = (
                    jnp.concatenate(parts, axis=0).T.astype(LOW)
                )

        loop(count, step)

    def out_project(rb):
        rows = slice(rb * 256, rb * 256 + 256)

        def step(i):
            po[rows, at(i, 256)] = dot_nt(ho[rows, :], wo[pl.ds(i * 4, 4)].reshape(256, 512)).astype(LOW)

        loop(4, step)
        cross(2 + rb, po.at[rows], por.at[rows]).start()

    attend((0, 1), 0, 4)
    ag_finish(1)
    out_project(0)
    ag_event(2, 0)
    attend((2, 3), 0, 2)
    ag_event(3, 0)
    attend((2, 3), 2, 2)
    out_project(1)
    rows_send(1, pcd, arrd, 10, 15)
    ag_event(2, 1)
    ag_event(3, 1)
    ag_start(4)
    ag_event(2, 2)
    ag_start(5)
    rows_wait(1, pcd, arrd)
    own_dy = dot_nn(gather_rows, arrd[...])
    dyg[own, :] = own_dy.astype(LOW)
    gvec[7:8, :] = jnp.sum(own_dy, axis=0, keepdims=True)
    cross(1, dyg.at[own], dyg.at[own]).start()
    ag_event(3, 2)
    ag_event(4, 0)
    ag_event(2, 3)

    def mlp_enter(rb):
        rows = slice(rb * 256, rb * 256 + 256)
        cross(2 + rb, po.at[rows], por.at[rows]).wait_recv()

        def enter(i):
            part = at(rb * 8 + i, 32)
            value = xg[part, :].astype(F32) + (po[part, :].astype(F32) + por[part, :].astype(F32))
            value = value + vrow[4:5, :]

            @pl.when(t == rb)
            def _():
                yb[at(i, 32), :] = value

            normed, scale = stats(value)
            res[part, :] = normed
            rstd[part, :] = jnp.broadcast_to(scale, (32, 128))
            a2[part, :] = (normed * vrow[5:6, :] + vrow[6:7, :]).astype(LOW)

        loop(8, enter)

    def up(i):
        cols = at(i, 256)
        v = dot_nn(a2[...], wu[:, :, cols].reshape(1024, 256)) + bup[:, cols]
        square = v * v
        bend = jnp.tanh(GELU_SCALE * (v + 0.044715 * (square * v)))
        half_v = 0.5 * v
        both = 1.0 + bend
        act[:, cols] = (half_v * both).astype(LOW)
        slope = 0.5 * both + (half_v * (1.0 - bend * bend)) * (
            GELU_SCALE + (GELU_SCALE * 3.0 * 0.044715) * square
        )
        dpre[:, cols] = slope.astype(LOW)

    def act_back(i):
        cols = at(i, 256)
        grad = dot_nn(dyg[...], wd[:, :, cols].reshape(1024, 256))
        back = (grad * dpre[:, cols].astype(F32)).astype(LOW)
        dpre[:, cols] = back
        gbup[:, cols] = jnp.sum(back.astype(F32), axis=0, keepdims=True)

    def mlp_back(rb):
        rows = slice(rb * 256, rb * 256 + 256)

        def down(i):
            pd[rows, at(i, 256)] = dot_nt(dpre[rows, :], wu[pl.ds(i * 4, 4)].reshape(256, 2048)).astype(LOW)

        loop(4, down)
        cross(5 + rb, pd.at[rows], pdr.at[rows]).start()

    def mlp_out(i):
        pm[:, at(i, 256)] = dot_nt(act[...], wd[pl.ds(i * 4, 4)].reshape(256, 2048)).astype(LOW)

    def flip(ref):
        def step(i):
            tbuf[at(i, 256), :] = ref[:, at(i, 256)].T

        loop(4, step)

    def plain(ref, first=0):
        return lambda j: ref[:, at(j + first, 512)]

    def weight_grad(c, part):
        half = halves[part]
        second, count, wide = {
            0: (heads_part(0), 3, 256),
            1: (plain(ho), 1, 512),
            2: (plain(dpre), 2, 512),
            3: (plain(act), 2, 512),
            4: (heads_part(1), 3, 256),
            5: (plain(dpre, 2), 2, 512),
            6: (plain(act, 2), 2, 512),
        }[c]
        rows = at(half, 512)

        def inner(j):
            grads[c][pl.ds(half * 8, 8), :, at(j + starts_at[c] // wide, wide)] = (
                dot_nn(tbuf[rows, :], second(j)).astype(LOW).reshape(8, 64, wide)
            )

        loop(count, inner)
        rm_send(c, half)

    def heads_part(h):
        return lambda j: dqkv[:, pl.ds(pl.multiple_of(j * 512 + h * 256, 256), 256)]

    mlp_enter(0)
    ag_event(5, 0)
    mlp_enter(1)
    ag_event(4, 1)
    ag_finish(2)
    loop(4, up)
    ag_event(5, 1)
    ag_event(3, 3)
    ag_finish(3)
    loop(4, lambda i: up(i + 4))
    ag_event(4, 2)
    cross(1, dyg.at[own], dyg.at[at(other, 256)]).wait_recv()
    flip(dyg)
    weight_grad(3, 0)
    ag_event(5, 2)
    weight_grad(3, 1)
    ag_event(4, 3)
    weight_grad(6, 0)
    rs_start(3)
    weight_grad(6, 1)
    ag_event(5, 3)
    ag_finish(4)
    ag_finish(5)
    loop(4, act_back)
    rs_start(6)
    rs_event(3, 0)
    loop(4, lambda i: act_back(i + 4))
    rs_event(6, 0)
    mlp_back(0)
    rs_event(3, 1)
    mlp_back(1)
    rs_event(6, 1)
    for c in range(2, 4):
        ag_drain(c)
    free_for_reduction(ready_one)
    loop(4, mlp_out)
    rs_event(3, 2)
    for c in range(4, 6):
        ag_drain(c)
    free_for_reduction(ready_two)
    others_free(ready_one)
    flip(a2)
    weight_grad(2, 0)
    weight_grad(2, 1)
    rs_event(6, 2)
    weight_grad(5, 0)
    rs_start(2)
    weight_grad(5, 1)
    rs_finish(3, keep_in(gd_out))

    def norm_two_back(rb):
        rows = slice(rb * 256, rb * 256 + 256)
        cross(5 + rb, pd.at[rows], pdr.at[rows]).wait_recv()

        def step(i):
            part = at(rb * 8 + i, 32)
            grad = pd[part, :].astype(F32) + pdr[part, :].astype(F32)
            normed, scale = res[part, :], rstd[part, 0:1]
            e = grad * vrow[5:6, :]
            inner = e - jnp.mean(e, axis=-1, keepdims=True)
            inner = inner - normed * jnp.mean(e * normed, axis=-1, keepdims=True)
            dy = dyg[part, :].astype(F32)
            full = dy + inner * scale
            res[part, :] = full
            low = full.astype(LOW)
            dattn[part, :] = low
            gvec[4:5, :] += 0.5 * jnp.sum(low.astype(F32), axis=0, keepdims=True)
            gvec[5:6, :] += 0.5 * jnp.sum(grad * normed, axis=0, keepdims=True)
            gvec[6:7, :] += 0.5 * jnp.sum(grad, axis=0, keepdims=True)

        loop(8, step)

        def heads(i):
            cols = at(i, 256)
            value = dot_nn(dattn[rows, :], wo[:, :, cols].reshape(1024, 256)).astype(LOW)
            dh[rows, cols] = value
            dht[cols, rows] = value.astype(F32).T.astype(LOW)

        loop(2, heads)

    lanes = lax.broadcasted_iota(jnp.int32, (1, PAIR), 1) < 64

    def attend_back(qbs, first_pair, count):
        def step(index):
            pair = index + first_pair
            for qb in qbs:
                first, width, allowed, distance = band(qb)
                queries = slice(qb * 128, qb * 128 + 128)
                span = slice(first, first + width)
                values = qkv[span, at(pair + 8, PAIR)]
                query_rows = qkv[queries, at(pair, PAIR)]
                grad_rows = dh[queries, at(pair, PAIR)]
                parts, keys_part, values_part = [], [], []
                for half in range(2):
                    s = score(pair, half, qb, first, width, allowed, distance)
                    probs = jnp.exp(s - lse[pair * 2 + half, :, queries])
                    grad_t = dht[at(pair * 2 + half, 64), queries]
                    grad_p = dot_nn(values, padded(grad_t, half))
                    row_dot = jnp.sum(probs * grad_p, axis=0, keepdims=True)
                    grad_s = (probs * (grad_p - row_dot)).astype(LOW)
                    key_t = qkvt[at(8 + pair * 2 + half, 64), span]
                    parts.append(dot_nn(key_t, grad_s))
                    keys_part.append(dot_nn(grad_s, query_rows))
                    values_part.append(dot_nn(probs.astype(LOW), grad_rows))
                dqkv[queries, at(pair, PAIR)] = (
                    (jnp.concatenate(parts, axis=0) * 0.125).T.astype(LOW)
                )
                dk_acc[span, at(pair, PAIR)] += jnp.where(lanes, keys_part[0], keys_part[1])
                dv_acc[span, at(pair, PAIR)] += jnp.where(lanes, values_part[0], values_part[1])
            if 3 in qbs:
                dqkv[:, at(pair + 4, PAIR)] = (dk_acc[:, at(pair, PAIR)] * 0.125).astype(LOW)
                dqkv[:, at(pair + 8, PAIR)] = dv_acc[:, at(pair, PAIR)].astype(LOW)

        loop(count, step)

    norm_two_back(0)
    rs_start(5)
    rs_event(2, 0)
    dk_acc[...] = jnp.zeros((512, 512), F32)
    dv_acc[...] = jnp.zeros((512, 512), F32)
    attend_back((0, 1), 0, 2)
    rs_event(5, 0)
    attend_back((0, 1), 2, 2)
    rs_event(2, 1)
    norm_two_back(1)
    cross(4, pm.at[at(other, 256)], pmr).start()
    rs_event(5, 1)
    others_free(ready_two)
    flip(dattn)
    weight_grad(1, 0)
    weight_grad(1, 1)
    rs_event(2, 2)
    rs_finish(6, keep_in(gd_out, 1024))
    store(7, gd_out).start()
    attend_back((2, 3), 0, 1)
    rs_start(1)
    attend_back((2, 3), 1, 1)
    rs_event(5, 2)
    flip(a1)
    weight_grad(0, 0)
    weight_grad(0, 1)
    rs_event(1, 0)
    attend_back((2, 3), 2, 1)
    rs_start(0)
    attend_back((2, 3), 3, 1)
    rows_drain(0, pcx, arrx)
    rows_drain(1, pcd, arrd)
    send_back = picks(arrive_ref).astype(LOW)
    cross(4, pm.at[at(other, 256)], pmr).wait_recv()

    def finish_y(i):
        part = at(i, 32)
        mine = at(t * 8 + i, 32)
        value = yb[part, :] + (pm[mine, :].astype(F32) + pmr[part, :].astype(F32)) + vrow[7:8, :]
        tok_v[part, :] = value.astype(LOW)

    loop(8, finish_y)
    pcx[...] = dot_nn(send_back, tok_v[...]).astype(LOW)
    rows_send(2, pcx, backy, 0, 5)
    rs_event(0, 0)

    def attn_in_back(rows):
        def step(i):
            po[rows, at(i, 256)] = dot_nt(
                dqkv[rows, 0:1536], wqkv[pl.ds(i * 4, 4)].reshape(256, 1536)
            ).astype(LOW)

        loop(4, step)

    for rb in range(2):
        rows = slice(rb * 256, rb * 256 + 256)
        cross(2 + rb, po.at[rows], por.at[rows]).wait_send()
    attn_in_back(at(other, 256))
    cross(7, po.at[at(other, 256)], por.at[pl.ds(0, 256)]).start()
    attn_in_back(own)
    rs_event(1, 1)
    rows_send(2, pcx, backy, 5, 10)
    weight_grad(4, 0)
    weight_grad(4, 1)
    rs_finish(2, keep_in(gu_out))
    rs_event(0, 1)
    rs_start(4)
    rows_send(2, pcx, backy, 10, 15)
    sums = jnp.zeros((1, 1536), F32)
    for i in range(4):
        sums = sums + jnp.sum(
            dqkv[i * 128 : i * 128 + 128, 0:1536].astype(F32), axis=0, keepdims=True
        )
    gvec[2:3, at(t, 512)] = sums[:, 0:512]
    gvec[3:4, at(t, 512)] = sums[:, 1024:1536]

    def norm_one_again(i):
        part = at(i, 32)
        normed, scale = stats(xg[at(t * 8 + i, 32), :].astype(F32))
        yb[part, :] = normed
        rstd[part, :] = jnp.broadcast_to(scale, (32, 128))

    loop(8, norm_one_again)
    rs_event(1, 2)
    rs_event(4, 0)
    rs_finish(5, keep_in(gu_out, 1024))
    store(6, gu_out).start()
    take_back = picks(rank_ref).T.astype(LOW)
    rs_event(0, 2)
    rs_event(4, 1)
    cross(7, po.at[at(other, 256)], por.at[pl.ds(0, 256)]).wait_recv()

    def norm_one_back(i):
        part = at(i, 32)
        mine = at(t * 8 + i, 32)
        grad = po[mine, :].astype(F32) + por[part, :].astype(F32)
        normed, scale = yb[part, :], rstd[part, 0:1]
        e = grad * vrow[0:1, :]
        inner = e - jnp.mean(e, axis=-1, keepdims=True)
        inner = inner - normed * jnp.mean(e * normed, axis=-1, keepdims=True)
        cot_v[part, :] = (res[mine, :] + inner * scale).astype(LOW)
        gvec[0:1, :] += jnp.sum(grad * normed, axis=0, keepdims=True)
        gvec[1:2, :] += jnp.sum(grad, axis=0, keepdims=True)

    loop(8, norm_one_back)

    for e in range(16):
        svec[e, 0:8, :] = gvec[:, 128 * (e // 2) : 128 * (e // 2) + 128]
        svec[e, 8:16, :] = jnp.zeros((8, 128), F32)
    for j in range(8):
        svec[8 * t + j, 8:9, :] = gbup[:, 256 * j : 256 * j + 128]
        svec[8 * t + j, 9:10, :] = gbup[:, 256 * j + 128 : 256 * j + 256]
    tiles_send(5, lambda spot: svec.at[spot], svr)
    a2[0:256, :] = dot_nn(send_back, cot_v[...]).astype(LOW)
    rows_send(3, a2, backd)
    svr[d] = svec[d]
    rs_event(4, 2)
    rows_wait(2, pcx, backy)
    tok_v[...] = dot_nn(take_back, backy[...]).astype(LOW)
    store(0, tok_v).start()
    rs_finish(1, keep_in(go_out))
    store(5, go_out).start()
    rs_finish(0, keep_heads(0))
    tiles_all(5, svr).wait_recv()
    small = jnp.zeros((16, 128), F32)
    for e in range(16):
        small = small + svr[e]
    sown[...] = small
    cross(8, sown, sown_r).start()
    rs_finish(4, keep_heads(256))
    for i, ref in enumerate((gq_out, gk_out, gv_out)):
        store(2 + i, ref).start()
    cross(8, sown, sown_r).wait_recv()
    small_out[...] = sown[...] + sown_r[...]
    store(8, small_out).start()
    ag_drain(0)
    ag_drain(1)
    rows_wait(3, a2, backd)
    cot_v[...] = dot_nn(take_back, backd[...]).astype(LOW)
    store(1, cot_v).start()

    for c in range(7):
        rs_drain(c)
    rows_drain(2, pcx, backy)
    rows_drain(3, a2, backd)
    tiles_all(4, vgat).wait_send()
    tiles_all(5, svr).wait_send()
    cross(0, xg.at[own], xg.at[own]).wait_send()
    cross(1, dyg.at[own], dyg.at[own]).wait_send()
    cross(4, pm.at[at(other, 256)], pmr).wait_send()
    for rb in range(2):
        rows = slice(rb * 256, rb * 256 + 256)
        cross(5 + rb, pd.at[rows], pdr.at[rows]).wait_send()
    cross(7, po.at[at(other, 256)], por.at[pl.ds(0, 256)]).wait_send()
    cross(8, sown, sown_r).wait_send()
    stored = (tok_v, cot_v, gq_out, gk_out, gv_out, go_out, gu_out, gd_out, small_out)
    for i, ref in enumerate(stored):
        store(i, ref).wait()


def settle_kernel(*refs):
    sources, homes = refs[:9], refs[9:26]
    held, short = refs[26:35], refs[35:44]
    in_sem, out_sem = refs[44], refs[45]
    ins = [pltpu.make_async_copy(sources[i], held[i], in_sem.at[i]) for i in range(9)]
    outs = [pltpu.make_async_copy(held[i], homes[i], out_sem.at[i]) for i in range(8)]
    outs += [pltpu.make_async_copy(short[i], homes[8 + i], out_sem.at[8 + i]) for i in range(9)]
    for i in (8, 6, 7, 0, 1, 2, 3, 4, 5):
        ins[i].start()
    core = lax.rem(lax.axis_index("dp"), 2)
    small = held[8]
    ins[8].wait()
    for i in range(8):
        row = small[i : i + 1, :]
        short[i][...] = jnp.where(core == 0, row[:, 0:64], row[:, 64:128]).reshape(64)
    short[8][0:128] = small[8:9, :].reshape(128)
    short[8][128:256] = small[9:10, :].reshape(128)
    for i in range(9):
        outs[8 + i].start()
    for i in (6, 7, 0, 1, 2, 3, 4, 5):
        ins[i].wait()
        outs[i].start()
    for copy in outs:
        copy.wait()


def fused_body(
    tokens,
    cotangent,
    norm1_gain,
    norm1_shift,
    w_query,
    b_query,
    w_key,
    w_value,
    b_value,
    w_out,
    b_out,
    norm2_gain,
    norm2_shift,
    w_up,
    b_up,
    w_down,
    b_down,
    lengths,
    deal_rank,
    arrival,
):
    def vm(*shape, dtype=LOW):
        return pltpu.VMEM(shape, dtype)

    def dma(*shape):
        return pltpu.SemaphoreType.DMA(shape)

    scratch = [pltpu.VMEM((64,), LOW)] * 8 + [
        pltpu.VMEM((256,), LOW),
        pltpu.VMEM((1, 1, 256), jnp.int32),
        pltpu.VMEM((1, 1, 256), jnp.int32),
        vm(64, 512, dtype=F32),
        vm(64, 512, dtype=F32),
        vm(64, 512, dtype=F32),
        vm(64, 512, dtype=F32),
        vm(64, 2048, dtype=F32),
        vm(64, 2048, dtype=F32),
        vm(16, 128, dtype=F32),
        vm(16, 64, 1536),
        vm(16, 64, 512),
        vm(16, 64, 2048),
        vm(16, 64, 2048),
        vm(16, 64, 768),
        vm(16, 64, 768),
        vm(16, 64, 512),
        vm(16, 64, 2048),
        vm(16, 64, 2048),
        vm(16, 64, 2048),
        vm(256, 1024),
        vm(256, 1024),
        vm(256, 1024),
        vm(256, 1024),
        vm(256, 1024),
        vm(256, 1024),
        vm(256, 1024),
        vm(256, 1024),
        vm(512, 1024),
        vm(512, 1024),
        vm(512, 1024),
        vm(512, 1536),
        vm(1536, 512),
        vm(512, 512),
        vm(8, 1, 512, dtype=F32),
        vm(512, 1024),
        vm(512, 1024),
        vm(512, 1024, dtype=F32),
        vm(256, 1024, dtype=F32),
        vm(512, 128, dtype=F32),
        vm(512, 1024),
        vm(512, 2048),
        vm(512, 2048),
        vm(512, 1024),
        vm(256, 1024),
        vm(512, 1024),
        vm(512, 1024),
        vm(512, 1024),
        vm(512, 512),
        vm(512, 512),
        vm(512, 512, dtype=F32),
        vm(512, 512, dtype=F32),
        vm(1024, 512),
        vm(16, 16, 128, dtype=F32),
        vm(8, 1024, dtype=F32),
        vm(1, 1536, dtype=F32),
        vm(1, 2048, dtype=F32),
        vm(8, 1024, dtype=F32),
        vm(1, 2048, dtype=F32),
        vm(16, 16, 128, dtype=F32),
        vm(16, 16, 128, dtype=F32),
        vm(16, 128, dtype=F32),
        vm(16, 128, dtype=F32),
        vm(1, 512, dtype=jnp.int32),
        dma(20),
        dma(9),
        dma(6),
        dma(6, 2, 4),
        dma(6),
        dma(6),
        dma(6),
        dma(6),
        dma(9),
        dma(9),
        dma(7),
        dma(7, 2),
        dma(7),
        dma(7, 2, 4),
        dma(6),
        dma(7),
        pltpu.SemaphoreType.REGULAR,
        pltpu.SemaphoreType.REGULAR,
    ]
    anywhere = pl.BlockSpec(memory_space=pl.ANY)
    outs = (
        jax.ShapeDtypeStruct((256, 1024), LOW),
        jax.ShapeDtypeStruct((256, 1024), LOW),
        jax.ShapeDtypeStruct((64, 512), F32),
        jax.ShapeDtypeStruct((64, 512), F32),
        jax.ShapeDtypeStruct((64, 512), F32),
        jax.ShapeDtypeStruct((64, 512), F32),
        jax.ShapeDtypeStruct((64, 2048), F32),
        jax.ShapeDtypeStruct((64, 2048), F32),
        jax.ShapeDtypeStruct((16, 128), F32),
    )
    parts = pl.pallas_call(
        fused_kernel,
        name="fused_layer",
        out_shape=outs,
        in_specs=[anywhere] * 19 + [pl.BlockSpec(memory_space=pltpu.SMEM)],
        out_specs=[anywhere] * 9,
        scratch_shapes=scratch,
        compiler_params=pltpu.CompilerParams(
            collective_id=0, has_side_effects=True, vmem_limit_bytes=67043328
        ),
    )(
        tokens,
        cotangent,
        w_query,
        w_key,
        w_value,
        w_out.T,
        w_up,
        w_down.T,
        norm1_gain,
        norm1_shift,
        b_query,
        b_value,
        b_out,
        norm2_gain,
        norm2_shift,
        b_down,
        b_up,
        deal_rank,
        arrival,
        lengths,
    )
    short = jax.ShapeDtypeStruct((64,), F32)
    finals = outs[:8] + (short,) * 8 + (jax.ShapeDtypeStruct((256,), F32),)
    done = pl.pallas_call(
        settle_kernel,
        name="settle",
        out_shape=finals,
        in_specs=[anywhere] * 9,
        out_specs=[anywhere] * 17,
        scratch_shapes=[vm(*out.shape, dtype=out.dtype) for out in outs + finals[8:]]
        + [dma(9), dma(17)],
    )(*parts)
    result, grad_tokens, grad_q, grad_k, grad_v, grad_out, grad_up, grad_down = done[:8]
    gain_one, shift_one, bias_q, bias_v, bias_out, gain_two, shift_two, bias_down, bias_up = done[8:]
    return (
        result,
        grad_tokens,
        gain_one,
        shift_one,
        grad_q,
        bias_q,
        grad_k,
        grad_v,
        bias_v,
        grad_out.T,
        bias_out,
        gain_two,
        shift_two,
        grad_up,
        bias_up,
        grad_down.T,
        bias_down,
    )


def solution(mesh):
    in_specs = (
        P(("dp", "tensor"), None),
        P(("dp", "tensor"), None),
        P("dp"),
        P("dp"),
        P("dp", "tensor"),
        P("dp"),
        P("dp", "tensor"),
        P("dp", "tensor"),
        P("dp"),
        P("tensor", "dp"),
        P("dp"),
        P("dp"),
        P("dp"),
        P("dp", "tensor"),
        P("dp"),
        P("tensor", "dp"),
        P("dp"),
        P("dp", None),
        P("dp", "tensor", None),
        P("dp", "tensor", None),
    )
    out_specs = (
        P(("dp", "tensor"), None),
        P(("dp", "tensor"), None),
        P("dp"),
        P("dp"),
        P("dp", "tensor"),
        P("dp"),
        P("dp", "tensor"),
        P("dp", "tensor"),
        P("dp"),
        P("tensor", "dp"),
        P("dp"),
        P("dp"),
        P("dp"),
        P("dp", "tensor"),
        P("dp"),
        P("tensor", "dp"),
        P("dp"),
    )
    small_slice = mesh.shape["dp"] == 16 and mesh.shape["tensor"] == 2
    program = fused_body if small_slice else body
    return jax.shard_map(program, mesh=mesh, in_specs=in_specs, out_specs=out_specs, check_vma=False)
```
